32 devices in a mesh: dp: 16 (over z, y, x), ctx: 2 (over core).
Axes of the slice: x: 2, y: 2, z: 4, core: 2. Of those that a mesh axis runs over, the one named last changes fastest.
Arguments:
- tokens: bfloat16 [16, 2, 2, 256, 768], P('dp', None, 'ctx'), may hold values from -6 to 6
- prev_logits: bfloat16 [16, 12, 2, 2, 256, 1024], P('dp', None, None, 'ctx'), may hold values from -6 to 6
- teacher: bfloat16 [16, 2, 2, 256, 768], P('dp', None, 'ctx'), may hold values from -8 to 8
- lengths: int32 [16], P('dp'), may hold values from 256 to 1024, as said below
- w_query: bfloat16 [768, 768], P('dp'), may hold values from -0.21875 to 0.21875
- w_key: bfloat16 [768, 768], P('dp'), may hold values from -0.21875 to 0.21875
- w_value: bfloat16 [768, 768], P('dp'), may hold values from -0.21875 to 0.21875
- w_output: bfloat16 [768, 768], P('dp'), may hold values from -2.5 to 2.5
- w_inner: bfloat16 [768, 3072], P('dp'), may hold values from -0.21875 to 0.21875
- w_outer: bfloat16 [3072, 768], P('dp'), may hold values from -0.109375 to 0.109375
- bias_query: bfloat16 [768], P('dp'), may hold values from -3 to 3
- bias_value: bfloat16 [768], P('dp'), may hold values from -0.19921875 to 0.19921875
- bias_output: bfloat16 [768], P('dp'), may hold values from -0.59765625 to 0.59765625
- attn_gain: bfloat16 [768], P('dp'), may hold values from 0.25 to 1.75
- attn_shift: bfloat16 [768], P('dp'), may hold values from -2 to 2
- inner_bias: bfloat16 [3072], P('dp'), may hold values from -3 to 3
- outer_bias: bfloat16 [768], P('dp'), may hold values from -2 to 2
- ffn_gain: bfloat16 [768], P('dp'), may hold values from 0.796875 to 1.1953125
- ffn_shift: bfloat16 [768], P('dp'), may hold values from -2 to 2
Outputs:
- output: bfloat16 [16, 2, 2, 256, 768], P('dp', None, 'ctx')
- logits: bfloat16 [16, 12, 2, 2, 256, 1024], P('dp', None, None, 'ctx')
- loss: float32 [], replicated
- grad_tokens: bfloat16 [16, 2, 2, 256, 768], P('dp', None, 'ctx')
- grad_prev_logits: bfloat16 [16, 12, 2, 2, 256, 1024], P('dp', None, None, 'ctx')
- grad_w_query: float32 [768, 768], P('dp')
- grad_w_key: float32 [768, 768], P('dp')
- grad_w_value: float32 [768, 768], P('dp')
- grad_w_output: float32 [768, 768], P('dp')
- grad_w_inner: float32 [768, 3072], P('dp')
- grad_w_outer: float32 [3072, 768], P('dp')
- grad_bias_query: float32 [768], P('dp')
- grad_bias_value: float32 [768], P('dp')
- grad_bias_output: float32 [768], P('dp')
- grad_attn_gain: float32 [768], P('dp')
- grad_attn_shift: float32 [768], P('dp')
- grad_inner_bias: float32 [3072], P('dp')
- grad_outer_bias: float32 [768], P('dp')
- grad_ffn_gain: float32 [768], P('dp')
- grad_ffn_shift: float32 [768], P('dp')
The draws below stay inside these ranges and needn't reach their ends.
Inputs may be any that keep to these rules, and one draw needn't show every extreme that they name: `lengths`: valid positions of each sequence; slots at or beyond a sequence's length are padding; some sequence is full.
All inputs are finite; a program needn't handle non-finite values.
Results may differ from the reference program's by a relative error of at most 0.017.
Values may be sent and summed in bfloat16 or wider, within the bound.
No kernel may reach another device: no remote copies, remote signals or barrier semaphores. Data moves between devices by JAX's collectives and lax.ppermute only.
A program may use at most 256 MiB of HBM per device.

```python
from functools import partial
import jax
import jax.numpy as jnp
from jax import lax

D = 768
H = 12
HD = 64
FF = 3072
SEQ = 1024
BLK = 256
SEQS = 16
LOSS_SCALE = 6291456
N_CTX = 2


def draw_lengths(key, part):
    seq_index = jnp.arange(SEQS, dtype=jnp.int32)
    lowest = SEQ // 4
    rising = lowest + (SEQ - lowest) * seq_index // max(SEQS - 1, 1)
    jitter = jax.random.randint(key, (SEQS,), 0, SEQ // 8 + 1, dtype=jnp.int32)
    return jnp.minimum(rising + jitter, SEQ).astype(jnp.int32)


def shared_fields(key):
    token_noise = jax.random.normal(jax.random.fold_in(key, 11), (SEQS, 2, N_CTX, BLK, D), jnp.float32)
    token_values = jnp.clip(token_noise, -6.0, 6.0)
    shift_noise = jax.random.normal(jax.random.fold_in(key, 12), (D,), jnp.float32)
    shift_values = jnp.clip(0.3 * shift_noise, -2.0, 2.0)
    return (token_values, shift_values)


def draw_tokens(key, part):
    token_values, shift_values = shared_fields(key)
    return token_values.astype(jnp.bfloat16)


def draw_ffn_shift(key, part):
    token_values, shift_values = shared_fields(key)
    return shift_values.astype(jnp.bfloat16)


def draw_teacher(key, part):
    token_values, shift_values = shared_fields(key)
    noise_key = jax.random.fold_in(key, 13)
    spread = jax.random.normal(noise_key, (SEQS, 2, N_CTX, BLK, D), jnp.float32)
    extra = 0.6 * jnp.clip(spread, -4.0, 4.0)
    target = shift_values + 0.8 * token_values + extra
    return jnp.clip(target, -8.0, 8.0).astype(jnp.bfloat16)


def level_of(key, shape, cuts, least, top_value):
    def one(axis_at, blocks):
        heights = jax.random.uniform(jax.random.fold_in(jax.random.fold_in(key, 6), axis_at), (blocks,), jnp.float32, least / len(cuts), top_value / len(cuts))
        return jnp.repeat(jnp.exp(heights), shape[axis_at] // blocks).reshape((-1,) + (1,) * (len(shape) - axis_at - 1))

    loudness = one(*cuts[0])
    for cut in cuts[1:]:
        loudness = loudness * one(*cut)
    return loudness


def centred(rng, extent, scale, reach, cuts=(), kind=jnp.bfloat16):
    factor_of = level_of(rng, extent, cuts, -0.22, 0.18) if cuts else 1.0
    entries = jax.random.normal(rng, extent, jnp.float32) * scale * factor_of
    return jnp.minimum(jnp.maximum(entries, -reach), reach).astype(kind)


def setup_inputs(seed: int = 0) -> dict:
    splits = jax.random.split(jax.random.key(seed), 20)
    return {
        "tokens": draw_tokens(jax.random.fold_in(splits[19], 71), 0),
        "prev_logits": centred(splits[1], (SEQS, H, 2, N_CTX, BLK, SEQ), 1.0, 6.0, ((0, 16), (3, 2))),
        "teacher": draw_teacher(jax.random.fold_in(splits[19], 71), 0),
        "lengths": draw_lengths(jax.random.fold_in(splits[19], 71), 0),
        "w_query": centred(splits[4], (D, D), D ** -0.5, 0.21875, ((0, 16),)),
        "w_key": centred(splits[5], (D, D), D ** -0.5, 0.21875, ((0, 16),)),
        "w_value": centred(splits[6], (D, D), D ** -0.5, 0.21875, ((0, 16),)),
        "w_output": centred(splits[7], (D, D), (max(D // 128, 1)) ** -0.5, 2.5, ((0, 16),)),
        "w_inner": centred(splits[8], (D, FF), D ** -0.5, 0.21875, ((0, 16),)),
        "w_outer": centred(splits[9], (FF, D), FF ** -0.5, 0.109375, ((0, 16),)),
        "bias_query": centred(splits[10], (D,), 0.5, 3.0, ((0, 16),)),
        "bias_value": centred(splits[11], (D,), 0.03, 0.19921875, ((0, 16),)),
        "bias_output": centred(splits[12], (D,), 0.1, 0.59765625, ((0, 16),)),
        "attn_gain": jnp.clip(1.0 + 0.15 * jax.random.normal(splits[13], (D,), jnp.float32), 0.25, 1.75).astype(jnp.bfloat16),
        "attn_shift": centred(splits[14], (D,), 0.3, 2.0, ((0, 16),)),
        "inner_bias": centred(splits[15], (FF,), 0.5, 3.0, ((0, 16),)),
        "outer_bias": centred(splits[16], (D,), 0.3, 2.0, ((0, 16),)),
        "ffn_gain": jnp.clip(1.0 + 0.04 * jax.random.normal(splits[17], (D,), jnp.float32), 0.796875, 1.1953125).astype(jnp.bfloat16),
        "ffn_shift": draw_ffn_shift(jax.random.fold_in(splits[19], 71), 0),
    }


EPSILON = 1e-05
NEG_BIG = -1e+30

@jax.custom_vjp
def low(v):
    return lax.optimization_barrier(v.astype(jnp.bfloat16)).astype(jnp.float32)

@jax.custom_vjp
def low_back(v):
    return v

def low_keep(v):
    return (low(v), None)

def low_pass(kept, grad):
    return (grad,)

def back_keep(v):
    return (v, None)

def back_low(kept, grad):
    return (low(grad),)
low.defvjp(low_keep, low_pass)
low_back.defvjp(back_keep, back_low)

def matmul(left, right):
    return jnp.dot(left, right, precision=lax.Precision.HIGHEST)

def layout_positions():
    halves = jnp.arange(2, dtype=jnp.int32)[:, None, None]
    slot_index = jnp.arange(N_CTX, dtype=jnp.int32)[None, :, None]
    within = jnp.arange(BLK, dtype=jnp.int32)[None, None, :]
    front_pos = slot_index * BLK + within
    back_pos = (2 * N_CTX - 1 - slot_index) * BLK + within
    return jnp.where(halves == 0, front_pos, back_pos).reshape(SEQ)

def layer_norm(activation, norm_gain, norm_shift):
    center = activation - lax.optimization_barrier(jnp.mean(activation, axis=-1, keepdims=True))
    spread = lax.optimization_barrier(jnp.mean(center * center, axis=-1, keepdims=True))
    return center * lax.rsqrt(spread + EPSILON) * norm_gain + norm_shift

def sequence_layer(weight_values, token_block, previous, target, length):
    w_query, w_key, w_value, w_output, w_inner, w_outer, bias_query, bias_value, bias_output, attn_gain, attn_shift, inner_bias, outer_bias, ffn_gain, ffn_shift = weight_values
    token_rows = token_block.reshape(SEQ, D)
    positions = layout_positions()
    valid_rows = (positions < length).astype(jnp.float32)
    allowed = (positions[None, :] <= positions[:, None]) & (positions[None, :] < length)
    queries = low(low_back(matmul(token_rows, w_query) + bias_query))
    key_rows = low(low_back(matmul(token_rows, w_key)))
    values = low(low_back(matmul(token_rows, w_value) + bias_value))
    query_heads = queries.reshape(SEQ, H, HD).transpose(1, 0, 2)
    key_heads = key_rows.reshape(SEQ, H, HD).transpose(1, 0, 2)
    value_heads = values.reshape(SEQ, H, HD).transpose(1, 0, 2)
    score_scale = HD ** (-0.5)
    raw_scores = jnp.einsum('hqd,hkd->hqk', query_heads, key_heads, precision=lax.Precision.HIGHEST) * score_scale
    raw_scores = low_back(raw_scores + previous.reshape(H, SEQ, SEQ))
    masked = jnp.where(allowed[None], raw_scores, NEG_BIG)
    row_max = lax.optimization_barrier(jnp.max(masked, axis=-1, keepdims=True))
    exponent = jnp.exp(masked - row_max)
    probability = low(exponent / lax.optimization_barrier(jnp.sum(exponent, axis=-1, keepdims=True)))
    mixed_rows = jnp.einsum('hqk,hkd->qhd', probability, value_heads, precision=lax.Precision.HIGHEST)
    mixed_rows = low(low_back(mixed_rows.reshape(SEQ, D)))
    attn_out = low_back(matmul(mixed_rows, w_output) + bias_output)
    first = layer_norm(token_rows + attn_out, attn_gain, attn_shift)
    inner_pre = low_back(matmul(low(first), w_inner) + inner_bias)
    active = low(jax.nn.gelu(inner_pre, approximate=False))
    outer_pre = low_back(matmul(active, w_outer) + outer_bias)
    result = layer_norm(first + outer_pre, ffn_gain, ffn_shift)
    errors = result - target.reshape(SEQ, D)
    square_sum = jnp.sum(valid_rows[:, None] * errors * errors)
    return (low(result).reshape(2, N_CTX, BLK, D), low(raw_scores).reshape(H, 2, N_CTX, BLK, SEQ), square_sum)

def reference(tokens, prev_logits, teacher, lengths, w_query, w_key, w_value, w_output, w_inner, w_outer, bias_query, bias_value, bias_output, attn_gain, attn_shift, inner_bias, outer_bias, ffn_gain, ffn_shift):
    weight_values = tuple((item.astype(jnp.float32) for item in (w_query, w_key, w_value, w_output, w_inner, w_outer, bias_query, bias_value, bias_output, attn_gain, attn_shift, inner_bias, outer_bias, ffn_gain, ffn_shift)))
    token_values = tokens.astype(jnp.float32)
    prev_values = prev_logits.astype(jnp.float32)
    target_values = teacher.astype(jnp.float32)

    def forward(token_input, prev_input, weight_input):

        def per_sequence(sequence_items):
            return jax.checkpoint(partial(sequence_layer, weight_input))(*sequence_items)
        seq_outputs, raw_logits, squares = lax.map(per_sequence, (token_input, prev_input, target_values, lengths))
        valid_total = jnp.sum(lengths).astype(jnp.float32)
        loss_value = jnp.sum(squares) / (valid_total * D)
        return (loss_value, (seq_outputs, raw_logits))
    loss_value, pullback, aux_values = jax.vjp(forward, token_values, prev_values, weight_values, has_aux=True)
    seq_outputs, raw_logits = aux_values
    grad_token_values, grad_prev_values, grad_weights = pullback(jnp.asarray(LOSS_SCALE, jnp.float32))
    return (seq_outputs.astype(jnp.bfloat16), raw_logits.astype(jnp.bfloat16), loss_value, grad_token_values.astype(jnp.bfloat16), grad_prev_values.astype(jnp.bfloat16), grad_weights[0], grad_weights[1], grad_weights[2], grad_weights[3], grad_weights[4], grad_weights[5], grad_weights[6], grad_weights[7], grad_weights[8], grad_weights[9], grad_weights[10], grad_weights[11], grad_weights[12], grad_weights[13], grad_weights[14])
```

```python
import functools

import jax
import jax.numpy as jnp
from jax import lax
from jax.experimental import pallas as pl
from jax.experimental.pallas import tpu as pltpu
from jax.sharding import PartitionSpec as P

EPSILON = 1e-05
NEG_BIG = -1e30
POS_BIG = 3.0e38
LANES = 128
f32 = jnp.float32
bf16 = jnp.bfloat16
ANY = pl.BlockSpec(memory_space=pl.ANY)


def mm(left, right):
    return jnp.dot(left, right, preferred_element_type=f32)


def mm_tn(left, right):
    return lax.dot_general(left, right, (((0,), (0,)), ((), ())), preferred_element_type=f32)


def mm_nt(left, right):
    return lax.dot_general(left, right, (((1,), (1,)), ((), ())), preferred_element_type=f32)


def struct(shape, dtype):
    return jax.ShapeDtypeStruct(shape, dtype)


def params():
    return pltpu.CompilerParams(vmem_limit_bytes=56 << 20)


def cost(flops, bytes_accessed, transcendentals=0):
    return pl.CostEstimate(
        flops=int(flops), bytes_accessed=int(bytes_accessed), transcendentals=int(transcendentals)
    )


def whole_block(array):
    rank = len(array.shape)
    return pl.BlockSpec(array.shape, lambda *_: (0,) * rank)


def flip(array, axis_name, bit):
    size = lax.axis_size(axis_name)
    return lax.ppermute(array, axis_name, [(i, i ^ bit) for i in range(size)])


def gather_planes(array, dp_rank):
    parts = [array] + [flip(array, "dp", 4 * step) for step in (1, 2, 3)]
    mine = dp_rank // 4
    column = jnp.stack([lax.select_n(mine ^ z, *parts) for z in range(4)])
    cut = split_row(array.shape[0])
    near = flip(column, "dp", 1)
    far = flip(column, "dp", 2)
    upper = flip(near[:, :cut], "dp", 2)
    lower = flip(far[:, cut:], "dp", 1)
    return column, near, far, upper, lower


def split_row(rows):
    return rows // 32 * 16


def scatter_planes(kept, arrived, dp_rank):
    _, rows, cols = kept.shape
    plane, mine = dp_rank % 4, dp_rank // 4
    cut = split_row(rows)
    kept, arrived = kept.reshape(4, 4, rows, cols), arrived.reshape(4, 4, rows, cols)

    def term(which, start=0, stop=rows):
        take = lambda a: lax.dynamic_index_in_dim(a, which, 1, keepdims=False)[:, start:stop]
        return take(kept).astype(f32) + take(arrived).astype(f32)

    upper = flip(term(plane ^ 3, 0, cut).astype(bf16), "dp", 2).astype(f32)
    lower = flip(term(plane ^ 3, cut).astype(bf16), "dp", 1).astype(f32)
    near = jnp.concatenate([term(plane ^ 1, 0, cut) + upper, term(plane ^ 1, cut)], axis=1)
    far = jnp.concatenate([term(plane ^ 2, 0, cut), term(plane ^ 2, cut) + lower], axis=1)
    near = flip(near.astype(bf16), "dp", 1).astype(f32)
    far = flip(far.astype(bf16), "dp", 2).astype(f32)
    column = term(plane) + near + far
    pick = lambda z: lax.dynamic_index_in_dim(column, z, 0, keepdims=False)
    total = pick(mine)
    for step in (1, 2, 3):
        total = total + flip(pick(mine ^ step).astype(bf16), "dp", 4 * step).astype(f32)
    return total


def scatter_small(terms, scalar, dp_rank):
    n = terms.shape[1]
    both = jnp.concatenate([terms.reshape(-1), scalar.reshape(1)])
    both = both + flip(both, "ctx", 1)
    grid, scalar = both[:-1].reshape(2, 2, 2, 2, n), both[-1:]
    bits = [(dp_rank >> shift) & 1 for shift in (3, 2, 1, 0)]
    for axis, shift in ((2, 1), (2, 0), (0, 3), (0, 2)):
        bit = bits[3 - shift]
        pick = lambda which: lax.dynamic_index_in_dim(grid, which, axis, keepdims=False)
        sent = pick(1 - bit)
        got = flip(jnp.concatenate([sent.reshape(-1), scalar]), "dp", 1 << shift)
        grid = pick(bit) + got[:-1].reshape(sent.shape)
        scalar = scalar + got[-1:]
    return grid.reshape(n), scalar[0]


def assemble_kernel(units, unit_rows, cut, extra, ranks, column, near, far, upper, lower, *refs):
    outs, sem = refs[:-1], refs[-1]
    plane = ranks[1]
    copies = []

    def copy(source, dest):
        copies.append(pltpu.make_async_copy(source, dest, sem.at[len(copies)]))

    for offset, ref in ((0, column), (1, near), (2, far), (3, None)):
        for unit in range(units + (1 if extra else 0)):
            start = unit * unit_rows
            rows = unit_rows if unit < units else extra
            dest = outs[0].at[unit, :, plane ^ offset] if unit < units else outs[1].at[:, plane ^ offset]
            if ref is not None:
                copy(ref.at[:, pl.ds(start, rows)], dest)
                continue
            stop = start + rows
            if start < cut:
                count = min(stop, cut) - start
                copy(upper.at[:, pl.ds(start, count)], dest.at[:, pl.ds(0, count)])
            if stop > cut:
                skip = max(start, cut)
                copy(lower.at[:, pl.ds(skip - cut, stop - skip)], dest.at[:, pl.ds(skip - start, stop - skip)])
    for item in copies:
        item.start()
    for item in copies:
        item.wait()


def assemble(pieces, info, units, unit_rows, extra=0):
    rows, cols = pieces[0].shape[1:]
    cut = split_row(rows)
    shapes = [struct((units, 4, 4, unit_rows, cols), bf16)]
    if extra:
        shapes.append(struct((4, 4, extra, cols), bf16))
    outs = pl.pallas_call(
        functools.partial(assemble_kernel, units, unit_rows, cut, extra),
        out_shape=shapes,
        grid_spec=pltpu.PrefetchScalarGridSpec(
            num_scalar_prefetch=1,
            grid=(1,),
            in_specs=[ANY] * 5,
            out_specs=[whole_block(s) for s in shapes],
            scratch_shapes=[pltpu.SemaphoreType.DMA((5 * (units + 1) + 1,))],
        ),
        compiler_params=params(),
        cost_estimate=cost(0, 64 * rows * cols),
        name="assemble",
    )(info, *pieces)
    matrix = outs[0].reshape(units, 16 * unit_rows, cols)
    return (matrix, outs[1].reshape(16, extra, cols)) if extra else matrix


def slot_start(slot, ctx_size, block_len):
    half, which = divmod(slot, ctx_size)
    return (which if half == 0 else 2 * ctx_size - 1 - which) * block_len


def head_lanes(which, head_dim):
    lane = lax.broadcasted_iota(jnp.int32, (1, LANES), 1)
    return (lane >= which * head_dim) & (lane < (which + 1) * head_dim)


def attend_kernel(
    block_len, ctx_size, head_dim, info, q_ref, k_ref, v_ref, prev_ref, logit_ref, prob_ref, mix_ref, limit_ref
):
    seq_len = 2 * ctx_size * block_len
    half = ctx_size * block_len
    heads = LANES // head_dim

    @pl.when(pl.program_id(0) == 0)
    def _():
        core, length = info[0], info[2]
        within = lax.broadcasted_iota(jnp.int32, (block_len, block_len), 1)
        row = lax.broadcasted_iota(jnp.int32, (block_len, block_len), 0)
        for part in range(2):
            start = core if part == 0 else 2 * ctx_size - 1 - core
            query_pos = row + start * block_len
            for slot in range(2 * ctx_size):
                key_pos = within + slot_start(slot, ctx_size, block_len)
                allowed = (key_pos <= query_pos) & (key_pos < length)
                limit_ref[
                    part * block_len : (part + 1) * block_len,
                    slot * block_len : (slot + 1) * block_len,
                ] = jnp.where(allowed, POS_BIG, NEG_BIG)

    scale = head_dim ** (-0.5)
    for part in range(2):
        rows = slice(part * block_len, (part + 1) * block_len)
        keys = half if part == 0 else seq_len
        mixed = jnp.zeros((block_len, LANES), f32)
        for which in range(heads):
            lanes = head_lanes(which, head_dim)
            query = jnp.where(lanes, q_ref[rows, :].astype(f32) * scale, 0.0).astype(bf16)
            raw = mm_nt(query, k_ref[...]) + prev_ref[which, rows, :].astype(f32)
            logit_ref[which, rows, :] = raw.astype(bf16)
            masked = jnp.minimum(raw[:, :keys], limit_ref[rows, :keys])
            top = jnp.max(masked, axis=-1, keepdims=True)
            exponent = jnp.exp(masked - top)
            total = jnp.sum(exponent, axis=-1, keepdims=True)
            probability = (exponent * (1.0 / total)).astype(bf16)
            prob_ref[which, rows, :keys] = probability
            mixed = jnp.where(lanes, mm(probability, v_ref[:keys, :]), mixed)
        mix_ref[rows, :] = mixed.astype(bf16)


def attend_back_kernel(
    block_len, ctx_size, head_dim, q_ref, k_ref, v_ref, prob_ref, gm_ref, gs_ref, gq_ref, gk_ref, gv_ref, gk_sum, gv_sum
):
    seq_len = 2 * ctx_size * block_len
    half = ctx_size * block_len
    heads = LANES // head_dim
    scale = head_dim ** (-0.5)
    gk_sum[...] = jnp.zeros_like(gk_sum)
    gv_sum[...] = jnp.zeros_like(gv_sum)
    for part in range(2):
        rows = slice(part * block_len, (part + 1) * block_len)
        keys = half if part == 0 else seq_len
        grad_query = jnp.zeros((block_len, LANES), f32)
        for which in range(heads):
            lanes = head_lanes(which, head_dim)
            grad_mix = jnp.where(lanes, gm_ref[rows, :], 0.0).astype(bf16)
            query = jnp.where(lanes, q_ref[rows, :], 0.0).astype(bf16)
            prob_low = prob_ref[which, rows, :keys]
            probability = prob_low.astype(f32)
            grad_prob = mm_nt(grad_mix, v_ref[:keys, :])
            term = probability * grad_prob
            row_dot = jnp.sum(term, axis=-1, keepdims=True)
            grad_score = (term - probability * row_dot).astype(bf16)
            gs_ref[which, rows, :keys] = grad_score
            if keys < seq_len:
                gs_ref[which, rows, keys:] = jnp.zeros((block_len, seq_len - keys), bf16)
            gv_sum[:keys, :] += mm_tn(prob_low, grad_mix)
            gk_sum[:keys, :] += mm_tn(grad_score, query)
            grad_query = jnp.where(lanes, mm(grad_score, k_ref[:keys, :]), grad_query)
        gq_ref[rows, :] = (grad_query * scale).astype(bf16)
    gk_ref[...] = (gk_sum[...] * scale).astype(bf16)
    gv_ref[...] = gv_sum[...].astype(bf16)


def attend(info, queries, keys, values, prev, block_len, ctx_size, head_dim):
    head_count, rows, seq_len = prev.shape
    pairs = LANES // head_dim
    wide = pl.BlockSpec((pairs, rows, seq_len), lambda h, i: (h, 0, 0))
    narrow = pl.BlockSpec((rows, LANES), lambda h, i: (0, h))
    whole = pl.BlockSpec((seq_len, LANES), lambda h, i: (0, h))
    return pl.pallas_call(
        functools.partial(attend_kernel, block_len, ctx_size, head_dim),
        out_shape=(struct(prev.shape, bf16), struct(prev.shape, bf16), struct(queries.shape, bf16)),
        grid_spec=pltpu.PrefetchScalarGridSpec(
            num_scalar_prefetch=1,
            grid=(head_count // pairs,),
            in_specs=[narrow, whole, whole, wide],
            out_specs=[wide, wide, narrow],
            scratch_shapes=[pltpu.VMEM((rows, seq_len), f32)],
        ),
        compiler_params=params(),
        cost_estimate=cost(8 * rows * seq_len * LANES * head_count, 6 * prev.size, prev.size),
        name="attend",
    )(info, queries, keys, values, prev)


def attend_back(queries, keys, values, probs, grad_mixed, block_len, ctx_size, head_dim):
    head_count, rows, seq_len = probs.shape
    pairs = LANES // head_dim
    wide = pl.BlockSpec((pairs, rows, seq_len), lambda h: (h, 0, 0))
    narrow = pl.BlockSpec((rows, LANES), lambda h: (0, h))
    whole = pl.BlockSpec((seq_len, LANES), lambda h: (0, h))
    return pl.pallas_call(
        functools.partial(attend_back_kernel, block_len, ctx_size, head_dim),
        out_shape=(
            struct(probs.shape, bf16),
            struct(queries.shape, bf16),
            struct(keys.shape, bf16),
            struct(values.shape, bf16),
        ),
        grid=(head_count // pairs,),
        in_specs=[narrow, whole, whole, wide, narrow],
        out_specs=[wide, narrow, whole, whole],
        scratch_shapes=[pltpu.VMEM((seq_len, LANES), f32), pltpu.VMEM((seq_len, LANES), f32)],
        compiler_params=params(),
        cost_estimate=cost(16 * rows * seq_len * LANES * head_count, 4 * probs.size),
        name="attend_back",
    )(queries, keys, values, probs, grad_mixed)


def side_lanes(info, side, width):
    half = info[0] if side == 0 else 1 - info[0]
    return pl.ds(pl.multiple_of(half * width, LANES), width)


def project_kernel(info, own_tok, oth_tok, w_own, w_oth, bq, bv, q_ref, k_ref, v_ref):
    core, unit = info[0], pl.program_id(0)
    block_len = k_ref.shape[2]
    width = w_own.shape[2]
    for side, w in ((0, w_own), (1, w_oth)):
        lanes = side_lanes(info, side, width)

        @pl.when(unit == 0)
        def _():
            q_ref[:, lanes] = (mm(own_tok[...], w[0]) + bq[:, lanes]).astype(bf16)

        def both(out, bias):
            for where, tok in ((core, own_tok), (1 - core, oth_tok)):
                value = (mm(tok[...], w[0]) + bias).astype(bf16)
                for part in range(2):
                    out[part, where, :, lanes] = value[part * block_len : (part + 1) * block_len]

        @pl.when(unit == 1)
        def _():
            both(k_ref, 0.0)

        @pl.when(unit == 2)
        def _():
            both(v_ref, bv[:, lanes])


def project(info, own_tok, oth_tok, w_own, w_oth, bq, bv, block_len):
    rows, width = own_tok.shape
    half = w_own.shape[2]
    w_spec = pl.BlockSpec((1, width, half), lambda i, _: (i, 0, 0))
    q_shape = struct((rows, width), bf16)
    k_shape = struct((2, 2, block_len, width), bf16)
    q, k, v = pl.pallas_call(
        project_kernel,
        out_shape=(q_shape, k_shape, k_shape),
        grid_spec=pltpu.PrefetchScalarGridSpec(
            num_scalar_prefetch=1,
            grid=(3,),
            in_specs=[whole_block(own_tok)] * 2 + [w_spec] * 2 + [whole_block(bq)] * 2,
            out_specs=[whole_block(q_shape), whole_block(k_shape), whole_block(k_shape)],
        ),
        compiler_params=params(),
        cost_estimate=cost(10 * rows * width * width, 10 * rows * width + 6 * width * width),
        name="project",
    )(info, own_tok, oth_tok, w_own, w_oth, bq, bv)
    return q, k.reshape(2 * rows, width), v.reshape(2 * rows, width)


def first_kernel(info, mix, tok, w_own, w_oth, bias, gain, shift, first_ref, low_ref, norm_ref, inv_ref, acc):
    width = w_own.shape[2]
    for side, w in ((0, w_own), (1, w_oth)):
        lanes = side_lanes(info, side, width)
        acc[:, lanes] = mm(mix[...], w[0]) + bias[:, lanes]
    tile = 128
    for start in range(0, acc.shape[0], tile):
        rows = slice(start, start + tile)
        total = tok[rows, :].astype(f32) + acc[rows, :]
        center = total - jnp.mean(total, axis=-1, keepdims=True)
        inverse = lax.rsqrt(jnp.mean(center * center, axis=-1, keepdims=True) + EPSILON)
        normed = center * inverse
        first = normed * gain[...] + shift[...]
        norm_ref[rows, :] = normed
        inv_ref[rows, :] = jnp.broadcast_to(inverse, (tile, LANES))
        first_ref[rows, :] = first
        low_ref[rows, :] = first.astype(bf16)


def first_norm(info, mix, tok, w_own, w_oth, bias, gain, shift):
    rows, width = tok.shape
    half = w_own.shape[2]
    w_spec = pl.BlockSpec((1, width, half), lambda i, _: (3, 0, 0))
    shapes = [
        struct((rows, width), f32),
        struct((rows, width), bf16),
        struct((rows, width), f32),
        struct((rows, LANES), f32),
    ]
    return pl.pallas_call(
        first_kernel,
        out_shape=shapes,
        grid_spec=pltpu.PrefetchScalarGridSpec(
            num_scalar_prefetch=1,
            grid=(1,),
            in_specs=[whole_block(mix), whole_block(tok), w_spec, w_spec] + [whole_block(bias)] * 3,
            out_specs=[whole_block(s) for s in shapes],
            scratch_shapes=[pltpu.VMEM((rows, width), f32)],
        ),
        compiler_params=params(),
        cost_estimate=cost(2 * rows * width * width, 16 * rows * width + 2 * width * width),
        name="first_norm",
    )(info, mix, tok, w_own, w_oth, bias, gain, shift)


def normal_parts(value):
    size = jnp.abs(value)
    near = 1.0 / (1.0 + (0.3275911 * 0.7071067811865476) * size)
    series = 1.061405429
    for factor in (-1.453152027, 1.421413741, -0.284496736, 0.254829592):
        series = series * near + factor
    bell = jnp.exp(-0.5 * value * value)
    tail = 0.5 * series * near * bell
    return jnp.where(value >= 0.0, 1.0 - tail, tail), bell * 0.3989422804014327


def inner_kernel(info, low, w_own, w_oth, bias, act_ref, slope_ref):
    def work(w):
        value = mm(low[...], w[0]) + bias[...]
        below, density = normal_parts(value)
        act_ref[...] = (value * below).astype(bf16)
        slope_ref[...] = (below + value * density).astype(bf16)

    @pl.when(pl.program_id(0) == 0)
    def _():
        work(w_own)

    @pl.when(pl.program_id(0) == 1)
    def _():
        work(w_oth)


def unit_specs(units, width, half):
    own = pl.BlockSpec((1, width, half), lambda s, u, _: (jnp.where(s == 0, u, units - 1), 0, 0))
    oth = pl.BlockSpec((1, width, half), lambda s, u, _: (jnp.where(s == 0, 0, u), 0, 0))
    return own, oth


def unit_column(units):
    return lambda s, u, info: (0, jnp.where(s == 0, info[0], 1 - info[0]) * units + u)


def inner(info, low, w_own, w_oth, bias):
    rows, width = low.shape
    units, _, half = w_own.shape
    own, oth = unit_specs(units, width, half)
    column = unit_column(units)
    shape = struct((rows, bias.shape[1]), bf16)
    return pl.pallas_call(
        inner_kernel,
        out_shape=(shape, shape),
        grid_spec=pltpu.PrefetchScalarGridSpec(
            num_scalar_prefetch=1,
            grid=(2, units),
            in_specs=[whole_block(low), own, oth, pl.BlockSpec((1, half), column)],
            out_specs=[pl.BlockSpec((rows, half), column)] * 2,
        ),
        compiler_params=params(),
        cost_estimate=cost(2 * low.size * bias.shape[1], 4 * shape.size, 2 * shape.size),
        name="inner",
    )(info, low, w_own, w_oth, bias)


def outer_kernel(
    ctx_size, info, factor, act, w_own, w_oth, first, teacher, bias, gain, shift, out_ref, go_ref, gs_ref, sum_ref, acc
):
    step = pl.program_id(0)

    @pl.when(step == 0)
    def _():
        acc[...] = jnp.zeros_like(acc)

    half = w_own.shape[1]
    for side, w in ((0, w_own), (1, w_oth)):
        lanes = side_lanes(info, side, half)
        acc[:, lanes] += mm(act[...], w[...])

    @pl.when(step == pl.num_programs(0) - 1)
    def _():
        rows_all, width = acc.shape
        block_len = rows_all // 2
        tile = 128
        sums = [jnp.zeros((1, width), f32) for _ in range(4)]
        for start in range(0, rows_all, tile):
            rows = slice(start, start + tile)
            part, inside = divmod(start, block_len)
            base = (info[0] if part == 0 else 2 * ctx_size - 1 - info[0]) * block_len + inside
            position = lax.broadcasted_iota(jnp.int32, (tile, 1), 0) + base
            valid = (position < info[2]).astype(f32)
            total = first[rows, :] + (acc[rows, :] + bias[...])
            center = total - jnp.mean(total, axis=-1, keepdims=True)
            inverse = lax.rsqrt(jnp.mean(center * center, axis=-1, keepdims=True) + EPSILON)
            normed = center * inverse
            result = normed * gain[...] + shift[...]
            out_ref[rows, :] = result.astype(bf16)
            error = (result - teacher[rows, :].astype(f32)) * valid
            grad_result = error * factor[0]
            grad_normed = grad_result * gain[...]
            mean_grad = jnp.mean(grad_normed, axis=-1, keepdims=True)
            mean_cross = jnp.mean(grad_normed * normed, axis=-1, keepdims=True)
            grad_sum = inverse * (grad_normed - mean_grad - normed * mean_cross)
            grad_low = grad_sum.astype(bf16)
            gs_ref[rows, :] = grad_sum
            go_ref[rows, :] = grad_low
            for index, value in enumerate(
                (grad_result * normed, grad_result, grad_low.astype(f32), error * error)
            ):
                sums[index] = sums[index] + jnp.sum(value, axis=0, keepdims=True)
        for index in range(4):
            sum_ref[index : index + 1, :] = sums[index]


def outer(info, factor, act, w_own, w_oth, first, teacher, bias, gain, shift, ctx_size):
    rows, width = first.shape
    full, half = w_own.shape
    chunk = full // 8
    w_spec = pl.BlockSpec((chunk, half), lambda j, _: (j, 0))
    shapes = [
        struct((rows, width), bf16),
        struct((rows, width), bf16),
        struct((rows, width), f32),
        struct((8, width), f32),
    ]
    return pl.pallas_call(
        functools.partial(outer_kernel, ctx_size),
        out_shape=shapes,
        grid_spec=pltpu.PrefetchScalarGridSpec(
            num_scalar_prefetch=1,
            grid=(8,),
            in_specs=[
                pl.BlockSpec(memory_space=pltpu.SMEM),
                pl.BlockSpec((rows, chunk), lambda j, _: (0, j)),
                w_spec,
                w_spec,
                whole_block(first),
                whole_block(teacher),
            ]
            + [whole_block(bias)] * 3,
            out_specs=[whole_block(s) for s in shapes],
            scratch_shapes=[pltpu.VMEM((rows, width), f32)],
        ),
        compiler_params=params(),
        cost_estimate=cost(2 * rows * width * full, 2 * rows * full + 2 * width * full + 12 * rows * width),
        name="outer",
    )(info, factor, act, w_own, w_oth, first, teacher, bias, gain, shift)


def outer_back_kernel(info, go, act, slope, w_own, w_oth, gi_ref, sum_ref, keep_ref, send_ref):
    half = w_own.shape[1]
    own, oth = go[:, side_lanes(info, 0, half)], go[:, side_lanes(info, 1, half)]
    keep_ref[...] = mm_tn(act[...], own).astype(bf16)
    send_ref[...] = mm_tn(act[...], oth).astype(bf16)
    grad_active = mm_nt(own, w_own[...]) + mm_nt(oth, w_oth[...])
    grad_inner = (grad_active * slope[...].astype(f32)).astype(bf16)
    gi_ref[...] = grad_inner
    sum_ref[...] = jnp.sum(grad_inner.astype(f32), axis=0, keepdims=True)


def outer_back(info, go, act, slope, w_own, w_oth):
    rows, full = act.shape
    half = w_own.shape[1]
    chunk = full // 8
    w_spec = pl.BlockSpec((chunk, half), lambda j, _: (j, 0))
    column = pl.BlockSpec((rows, chunk), lambda j, _: (0, j))
    return pl.pallas_call(
        outer_back_kernel,
        out_shape=(
            struct((rows, full), bf16),
            struct((1, full), f32),
            struct((full, half), bf16),
            struct((full, half), bf16),
        ),
        grid_spec=pltpu.PrefetchScalarGridSpec(
            num_scalar_prefetch=1,
            grid=(8,),
            in_specs=[whole_block(go), column, column, w_spec, w_spec],
            out_specs=[column, pl.BlockSpec((1, chunk), lambda j, _: (0, j)), w_spec, w_spec],
        ),
        compiler_params=params(),
        cost_estimate=cost(8 * rows * full * half, 6 * rows * full + 8 * full * half),
        name="outer_back",
    )(info, go, act, slope, w_own, w_oth)


def inner_back_kernel(
    info, gi, low, w_own, w_oth, gs_two, norm, inv, gain, mix, wo_own, wo_oth,
    keep_ref, send_ref, gs_ref, ga_ref, gm_ref, sum_ref, acc,
):
    side, unit = pl.program_id(0), pl.program_id(1)
    units = pl.num_programs(1)

    @pl.when((side == 0) & (unit == 0))
    def _():
        acc[...] = jnp.zeros_like(acc)

    ranks, rows_all, half = keep_ref.shape
    shard = low.shape[1] // ranks

    def work(w, out):
        acc[...] += mm_nt(gi[...], w[0])
        term = mm_tn(low[...], gi[...]).astype(bf16)
        start = pl.multiple_of(unit * shard, 16)
        out[:, pl.ds(start, shard), :] = term.reshape(ranks, shard, half)

    @pl.when(side == 0)
    def _():
        work(w_own, keep_ref)

    @pl.when(side == 1)
    def _():
        work(w_oth, send_ref)

    @pl.when((side == 1) & (unit == units - 1))
    def _():
        width = acc.shape[1]
        tile = 128
        sums = [jnp.zeros((1, width), f32) for _ in range(3)]
        for start in range(0, acc.shape[0], tile):
            rows = slice(start, start + tile)
            normed = norm[rows, :]
            grad_first = gs_two[rows, :] + acc[rows, :]
            grad_normed = grad_first * gain[...]
            mean_grad = jnp.mean(grad_normed, axis=-1, keepdims=True)
            mean_cross = jnp.mean(grad_normed * normed, axis=-1, keepdims=True)
            grad_sum = inv[rows, 0:1] * (grad_normed - mean_grad - normed * mean_cross)
            grad_low = grad_sum.astype(bf16)
            gs_ref[rows, :] = grad_sum
            ga_ref[rows, :] = grad_low
            for index, value in enumerate((grad_first * normed, grad_first, grad_low.astype(f32))):
                sums[index] = sums[index] + jnp.sum(value, axis=0, keepdims=True)
        for index in range(3):
            sum_ref[index : index + 1, :] = sums[index]
        total = jnp.zeros((acc.shape[0], width), f32)
        for which, w, out in ((0, wo_own, keep_ref), (1, wo_oth, send_ref)):
            grad_low = ga_ref[:, side_lanes(info, which, half)]
            total = total + mm_nt(grad_low, w[0])
            term = mm_tn(mix[...], grad_low).astype(bf16)
            out[:, rows_all - shard :, :] = term.reshape(ranks, shard, half)
        gm_ref[...] = total.astype(bf16)


def inner_back(info, gi, low, w_own, w_oth, gs_two, norm, inv, gain, mix, wo_own, wo_oth):
    rows, width = low.shape
    units, _, half = w_own.shape
    own, oth = unit_specs(units, width, half)
    wo = pl.BlockSpec((1, width, half), lambda s, u, _: (3, 0, 0))
    shapes = [
        struct((16, width // 16 * (units + 1), half), bf16),
        struct((16, width // 16 * (units + 1), half), bf16),
        struct((rows, width), f32),
        struct((rows, width), bf16),
        struct((rows, width), bf16),
        struct((8, width), f32),
    ]
    return pl.pallas_call(
        inner_back_kernel,
        out_shape=shapes,
        grid_spec=pltpu.PrefetchScalarGridSpec(
            num_scalar_prefetch=1,
            grid=(2, units),
            in_specs=[
                pl.BlockSpec((rows, half), unit_column(units)),
                whole_block(low),
                own,
                oth,
                whole_block(gs_two),
                whole_block(norm),
                whole_block(inv),
                whole_block(gain),
                whole_block(mix),
                wo,
                wo,
            ],
            out_specs=[whole_block(s) for s in shapes],
            scratch_shapes=[pltpu.VMEM((rows, width), f32)],
        ),
        compiler_params=params(),
        cost_estimate=cost(4 * gi.size * width + 4 * rows * width * width, 4 * gi.size + 20 * rows * width),
        name="inner_back",
    )(info, gi, low, w_own, w_oth, gs_two, norm, inv, gain, mix, wo_own, wo_oth)


def token_weights_kernel(info, own_tok, oth_tok, gq, gk, gv, keep_ref, send_ref, sum_ref):
    core = info[0]
    ranks, rows_all, half = keep_ref.shape
    shard = rows_all // 3
    block_len = gk.shape[2]
    for side, out in ((0, keep_ref), (1, send_ref)):
        lanes = side_lanes(info, side, half)
        term = mm_tn(own_tok[...], gq[:, lanes])
        out[:, 0:shard, :] = term.astype(bf16).reshape(ranks, shard, half)
        for index, grad in ((1, gk), (2, gv)):
            term = None
            for where, tok in ((core, own_tok), (1 - core, oth_tok)):
                for part in range(2):
                    piece = mm_tn(
                        tok[part * block_len : (part + 1) * block_len, :], grad[part, where, :, lanes]
                    )
                    term = piece if term is None else term + piece
            out[:, index * shard : (index + 1) * shard, :] = term.astype(bf16).reshape(
                ranks, shard, half
            )
    sum_ref[0:1, :] = jnp.sum(gq[...].astype(f32), axis=0, keepdims=True)
    total = jnp.zeros((1, gq.shape[1]), f32)
    for part in range(2):
        for where in range(2):
            total = total + jnp.sum(gv[part, where].astype(f32), axis=0, keepdims=True)
    sum_ref[1:2, :] = total


def token_weights(info, own_tok, oth_tok, gq, gk, gv):
    rows, width = own_tok.shape
    out = struct((16, 3 * width // 16, width // 2), bf16)
    shapes = [out, out, struct((8, width), f32)]
    args = (own_tok, oth_tok, gq, gk, gv)
    return pl.pallas_call(
        token_weights_kernel,
        out_shape=shapes,
        grid_spec=pltpu.PrefetchScalarGridSpec(
            num_scalar_prefetch=1,
            grid=(1,),
            in_specs=[whole_block(a) for a in args],
            out_specs=[whole_block(s) for s in shapes],
        ),
        compiler_params=params(),
        cost_estimate=cost(10 * rows * width * width, 14 * rows * width + 6 * width * width),
        name="token_weights",
    )(info, *args)


def token_terms_kernel(info, gq, gk, gv, w_own, w_oth, gs_one, own_ref, send_ref):
    core = info[0]
    half = w_own.shape[2]
    block_len = gk.shape[2]
    for part in range(2):
        rows = slice(part * block_len, (part + 1) * block_len)
        own = gs_one[rows, :]
        oth = jnp.zeros_like(own)
        for side, w in ((0, w_own), (1, w_oth)):
            lanes = side_lanes(info, side, half)
            own = own + mm_nt(gq[rows, lanes], w[0])
            own = own + mm_nt(gk[part, core, :, lanes], w[1]) + mm_nt(gv[part, core, :, lanes], w[2])
            oth = oth + mm_nt(gk[part, 1 - core, :, lanes], w[1])
            oth = oth + mm_nt(gv[part, 1 - core, :, lanes], w[2])
        own_ref[rows, :] = own
        send_ref[rows, :] = oth.astype(bf16)


def token_terms(info, gq, gk, gv, w_own, w_oth, gs_one):
    rows, width = gq.shape
    w_spec = pl.BlockSpec((3,) + w_own.shape[1:], lambda i, _: (0, 0, 0))
    shapes = [struct((rows, width), f32), struct((rows, width), bf16)]
    return pl.pallas_call(
        token_terms_kernel,
        out_shape=shapes,
        grid_spec=pltpu.PrefetchScalarGridSpec(
            num_scalar_prefetch=1,
            grid=(1,),
            in_specs=[whole_block(gq), whole_block(gk), whole_block(gv), w_spec, w_spec, whole_block(gs_one)],
            out_specs=[whole_block(s) for s in shapes],
        ),
        compiler_params=params(),
        cost_estimate=cost(10 * rows * width * width, 20 * rows * width + 6 * width * width),
        name="token_terms",
    )(info, gq, gk, gv, w_own, w_oth, gs_one)


def layout_positions(block_len, ctx_size, slot_index):
    within = jnp.arange(block_len, dtype=jnp.int32)
    front_pos = slot_index * block_len + within
    back_pos = (2 * ctx_size - 1 - slot_index) * block_len + within
    return (front_pos, back_pos)


def norm_forward(activation):
    center = activation - jnp.mean(activation, axis=-1, keepdims=True)
    inverse = lax.rsqrt(jnp.mean(center * center, axis=-1, keepdims=True) + EPSILON)
    return (center * inverse, inverse)


def norm_backward(grad_normed, normed, inverse):
    mean_grad = jnp.mean(grad_normed, axis=-1, keepdims=True)
    mean_cross = jnp.mean(grad_normed * normed, axis=-1, keepdims=True)
    return inverse * (grad_normed - mean_grad - normed * mean_cross)


def weight_grad(left, right):
    return lax.dot_general(
        left, right, (((0,), (0,)), ((), ())), preferred_element_type=jnp.float32
    )


def back_product(left, right):
    return lax.dot_general(
        left, right, (((1,), (1,)), ((), ())), preferred_element_type=jnp.float32
    )


def gelu_exact(inputs):
    return jax.nn.gelu(inputs, approximate=False)


def column_sum(matrix):
    return jnp.sum(matrix.astype(jnp.float32), axis=0)


def local_plain(
    tokens,
    prev_logits,
    teacher,
    lengths,
    w_query,
    w_key,
    w_value,
    w_output,
    w_inner,
    w_outer,
    bias_query,
    bias_value,
    bias_output,
    attn_gain,
    attn_shift,
    inner_bias,
    outer_bias,
    ffn_gain,
    ffn_shift,
):
    f32 = jnp.float32
    bf16 = jnp.bfloat16
    ctx_size = lax.axis_size("ctx")
    ctx_rank = lax.axis_index("ctx")
    dp_size = lax.axis_size("dp")
    groups = tokens.shape[0]
    block_len = tokens.shape[3]
    model_width = tokens.shape[4]
    head_count = prev_logits.shape[1]
    seq_len = prev_logits.shape[-1]
    head_dim = model_width // head_count
    local_rows = 2 * block_len
    total_rows = groups * local_rows
    score_scale = head_dim ** (-0.5)
    (
        query_matrix,
        key_matrix,
        value_matrix,
        output_matrix,
        query_add,
        value_add,
        output_add,
        first_gain,
        first_shift,
    ) = (
        lax.all_gather(w_query, "dp", axis=0, tiled=True),
        lax.all_gather(w_key, "dp", axis=0, tiled=True),
        lax.all_gather(w_value, "dp", axis=0, tiled=True),
        lax.all_gather(w_output, "dp", axis=0, tiled=True),
        lax.all_gather(bias_query, "dp", axis=0, tiled=True),
        lax.all_gather(bias_value, "dp", axis=0, tiled=True),
        lax.all_gather(bias_output, "dp", axis=0, tiled=True),
        lax.all_gather(attn_gain, "dp", axis=0, tiled=True),
        lax.all_gather(attn_shift, "dp", axis=0, tiled=True),
    )
    token_rows = tokens.reshape(total_rows, model_width)
    queries = (
        jnp.dot(token_rows, query_matrix, preferred_element_type=f32) + query_add.astype(f32)
    ).astype(bf16)
    key_rows = jnp.dot(token_rows, key_matrix, preferred_element_type=f32).astype(bf16)
    values = (
        jnp.dot(token_rows, value_matrix, preferred_element_type=f32) + value_add.astype(f32)
    ).astype(bf16)
    key_blocks, value_blocks = (
        lax.all_gather(
            key_rows.reshape(groups, 2, 1, block_len, model_width), "ctx", axis=2, tiled=True
        ),
        lax.all_gather(
            values.reshape(groups, 2, 1, block_len, model_width), "ctx", axis=2, tiled=True
        ),
    )
    inner_matrix, outer_matrix, inner_add, outer_add, second_gain, second_shift = (
        lax.all_gather(w_inner, "dp", axis=0, tiled=True),
        lax.all_gather(w_outer, "dp", axis=0, tiled=True),
        lax.all_gather(inner_bias, "dp", axis=0, tiled=True),
        lax.all_gather(outer_bias, "dp", axis=0, tiled=True),
        lax.all_gather(ffn_gain, "dp", axis=0, tiled=True),
        lax.all_gather(ffn_shift, "dp", axis=0, tiled=True),
    )
    front_pos, back_pos = layout_positions(block_len, ctx_size, ctx_rank)
    query_pos = jnp.stack([front_pos, back_pos]).reshape(local_rows)
    key_front, key_back = layout_positions(
        block_len, ctx_size, jnp.arange(ctx_size, dtype=jnp.int32)[:, None]
    )
    key_pos = jnp.stack([key_front, key_back]).reshape(seq_len)
    allowed = (key_pos[None, None, :] <= query_pos[None, :, None]) & (
        key_pos[None, None, :] < lengths[:, None, None]
    )
    valid_rows = (query_pos[None, :] < lengths[:, None]).astype(f32).reshape(total_rows)
    query_heads = queries.reshape(groups, local_rows, head_count, head_dim).transpose(2, 0, 1, 3)
    key_heads = key_blocks.reshape(groups, seq_len, head_count, head_dim).transpose(2, 0, 1, 3)
    value_heads = value_blocks.reshape(groups, seq_len, head_count, head_dim).transpose(2, 0, 1, 3)
    prev_rows = prev_logits.reshape(groups, head_count, local_rows, seq_len)

    def scores_of(head_id):
        raw_scores = (
            jnp.einsum(
                "grd,gkd->grk", query_heads[head_id], key_heads[head_id], preferred_element_type=f32
            )
            * score_scale
        )
        raw_scores = raw_scores + lax.dynamic_index_in_dim(
            prev_rows, head_id, 1, keepdims=False
        ).astype(f32)
        return (raw_scores, jnp.where(allowed, raw_scores, NEG_BIG))

    def attend(head_id):
        raw_scores, masked = scores_of(head_id)
        row_max = jnp.max(masked, axis=-1, keepdims=True)
        exponent = jnp.exp(masked - row_max)
        row_total = jnp.sum(exponent, axis=-1, keepdims=True)
        probability = (exponent / row_total).astype(bf16)
        mixed_part = jnp.einsum(
            "grk,gkd->grd", probability, value_heads[head_id], preferred_element_type=f32
        )
        return (mixed_part, row_max[..., 0] + jnp.log(row_total[..., 0]), raw_scores.astype(bf16))

    mixed_heads, log_totals, raw_heads = lax.map(attend, jnp.arange(head_count))
    raw_logits = jnp.moveaxis(raw_heads, 0, 1).reshape(prev_logits.shape)
    mixed_rows = mixed_heads.transpose(1, 2, 0, 3).reshape(total_rows, model_width).astype(bf16)
    attn_out = jnp.dot(mixed_rows, output_matrix, preferred_element_type=f32) + output_add.astype(
        f32
    )
    first_normed, first_inverse = norm_forward(token_rows.astype(f32) + attn_out)
    first = first_normed * first_gain.astype(f32) + first_shift.astype(f32)
    first_low = first.astype(bf16)
    inner_pre = jnp.dot(first_low, inner_matrix, preferred_element_type=f32) + inner_add.astype(f32)
    active, gelu_back = jax.vjp(gelu_exact, inner_pre)
    active_low = active.astype(bf16)
    outer_pre = jnp.dot(active_low, outer_matrix, preferred_element_type=f32) + outer_add.astype(
        f32
    )
    second_normed, second_inverse = norm_forward(first + outer_pre)
    result = second_normed * second_gain.astype(f32) + second_shift.astype(f32)
    errors = (result - teacher.reshape(total_rows, model_width).astype(f32)) * valid_rows[:, None]
    square_sum, valid_total = lax.psum(
        (jnp.sum(errors * errors), jnp.sum(valid_rows)), ("dp", "ctx")
    )
    loss_value = square_sum / (valid_total * model_width)
    loss_scale = dp_size * groups * seq_len * model_width / 2.0
    grad_result = errors * (loss_scale * 2.0 / (valid_total * model_width))
    grad_second_gain = jnp.sum(grad_result * second_normed, axis=0)
    grad_second_shift = jnp.sum(grad_result, axis=0)
    grad_sum_two = norm_backward(
        grad_result * second_gain.astype(f32), second_normed, second_inverse
    )
    grad_outer = grad_sum_two.astype(bf16)
    grad_outer_matrix = weight_grad(active_low, grad_outer)
    grad_outer_add = column_sum(grad_outer)
    grad_active = back_product(grad_outer, outer_matrix)
    grad_inner = gelu_back(grad_active)[0].astype(bf16)
    grad_inner_matrix = weight_grad(first_low, grad_inner)
    grad_inner_add = column_sum(grad_inner)
    grad_first = grad_sum_two + back_product(grad_inner, inner_matrix)
    grad_first_gain = jnp.sum(grad_first * first_normed, axis=0)
    grad_first_shift = jnp.sum(grad_first, axis=0)
    grad_sum_one = norm_backward(grad_first * first_gain.astype(f32), first_normed, first_inverse)
    grad_attn = grad_sum_one.astype(bf16)
    grad_output_matrix = weight_grad(mixed_rows, grad_attn)
    grad_output_add = column_sum(grad_attn)
    grad_mixed = back_product(grad_attn, output_matrix).astype(bf16)
    grad_mixed_heads = grad_mixed.reshape(groups, local_rows, head_count, head_dim).transpose(
        2, 0, 1, 3
    )

    def attend_back(head_id):
        _, masked = scores_of(head_id)
        probability = jnp.exp(masked - log_totals[head_id][..., None])
        grad_part = grad_mixed_heads[head_id]
        grad_value_part = jnp.einsum(
            "grk,grd->gkd", probability.astype(bf16), grad_part, preferred_element_type=f32
        )
        grad_probs = jnp.einsum(
            "grd,gkd->grk", grad_part, value_heads[head_id], preferred_element_type=f32
        )
        row_dot = jnp.sum(probability * grad_probs, axis=-1, keepdims=True)
        grad_scores = (probability * (grad_probs - row_dot)).astype(bf16)
        grad_query_part = (
            jnp.einsum("grk,gkd->grd", grad_scores, key_heads[head_id], preferred_element_type=f32)
            * score_scale
        )
        grad_key_part = (
            jnp.einsum(
                "grk,grd->gkd", grad_scores, query_heads[head_id], preferred_element_type=f32
            )
            * score_scale
        )
        return (grad_scores, grad_query_part, grad_key_part, grad_value_part)

    grad_score_heads, grad_query_heads, grad_key_heads, grad_value_heads = lax.map(
        attend_back, jnp.arange(head_count)
    )
    grad_logits = jnp.moveaxis(grad_score_heads, 0, 1).reshape(prev_logits.shape)
    grad_queries = (
        grad_query_heads.transpose(1, 2, 0, 3).reshape(total_rows, model_width).astype(bf16)
    )
    key_terms = grad_key_heads.transpose(1, 2, 0, 3).reshape(
        groups, 2, ctx_size, block_len, model_width
    )
    value_terms = grad_value_heads.transpose(1, 2, 0, 3).reshape(
        groups, 2, ctx_size, block_len, model_width
    )
    key_sums, value_sums = (
        lax.psum_scatter(
            key_terms.astype(jnp.bfloat16), "ctx", scatter_dimension=2, tiled=True
        ).astype(jnp.float32),
        lax.psum_scatter(
            value_terms.astype(jnp.bfloat16), "ctx", scatter_dimension=2, tiled=True
        ).astype(jnp.float32),
    )
    grad_keys = key_sums.reshape(total_rows, model_width).astype(bf16)
    grad_values = value_sums.reshape(total_rows, model_width).astype(bf16)
    grad_query_matrix = weight_grad(token_rows, grad_queries)
    grad_key_matrix = weight_grad(token_rows, grad_keys)
    grad_value_matrix = weight_grad(token_rows, grad_values)
    grad_query_add = column_sum(grad_queries)
    grad_value_add = column_sum(grad_values)
    grad_token_rows = (
        grad_sum_one
        + back_product(grad_queries, query_matrix)
        + back_product(grad_keys, key_matrix)
        + back_product(grad_values, value_matrix)
    )
    matrix_grads = (
        grad_query_matrix,
        grad_key_matrix,
        grad_value_matrix,
        grad_output_matrix,
        grad_inner_matrix,
        grad_outer_matrix,
    )
    vector_grads = (
        grad_query_add,
        grad_value_add,
        grad_output_add,
        grad_first_gain,
        grad_first_shift,
        grad_inner_add,
        grad_outer_add,
        grad_second_gain,
        grad_second_shift,
    )
    summed = (
        lax.psum_scatter(
            matrix_grads[0].astype(jnp.bfloat16), "dp", scatter_dimension=0, tiled=True
        ).astype(jnp.float32),
        lax.psum_scatter(
            matrix_grads[1].astype(jnp.bfloat16), "dp", scatter_dimension=0, tiled=True
        ).astype(jnp.float32),
        lax.psum_scatter(
            matrix_grads[2].astype(jnp.bfloat16), "dp", scatter_dimension=0, tiled=True
        ).astype(jnp.float32),
        lax.psum_scatter(
            matrix_grads[3].astype(jnp.bfloat16), "dp", scatter_dimension=0, tiled=True
        ).astype(jnp.float32),
        lax.psum_scatter(
            matrix_grads[4].astype(jnp.bfloat16), "dp", scatter_dimension=0, tiled=True
        ).astype(jnp.float32),
        lax.psum_scatter(
            matrix_grads[5].astype(jnp.bfloat16), "dp", scatter_dimension=0, tiled=True
        ).astype(jnp.float32),
        lax.psum_scatter(
            vector_grads[0].astype(jnp.bfloat16), "dp", scatter_dimension=0, tiled=True
        ).astype(jnp.float32),
        lax.psum_scatter(
            vector_grads[1].astype(jnp.bfloat16), "dp", scatter_dimension=0, tiled=True
        ).astype(jnp.float32),
        lax.psum_scatter(
            vector_grads[2].astype(jnp.bfloat16), "dp", scatter_dimension=0, tiled=True
        ).astype(jnp.float32),
        lax.psum_scatter(
            vector_grads[3].astype(jnp.bfloat16), "dp", scatter_dimension=0, tiled=True
        ).astype(jnp.float32),
        lax.psum_scatter(
            vector_grads[4].astype(jnp.bfloat16), "dp", scatter_dimension=0, tiled=True
        ).astype(jnp.float32),
        lax.psum_scatter(
            vector_grads[5].astype(jnp.bfloat16), "dp", scatter_dimension=0, tiled=True
        ).astype(jnp.float32),
        lax.psum_scatter(
            vector_grads[6].astype(jnp.bfloat16), "dp", scatter_dimension=0, tiled=True
        ).astype(jnp.float32),
        lax.psum_scatter(
            vector_grads[7].astype(jnp.bfloat16), "dp", scatter_dimension=0, tiled=True
        ).astype(jnp.float32),
        lax.psum_scatter(
            vector_grads[8].astype(jnp.bfloat16), "dp", scatter_dimension=0, tiled=True
        ).astype(jnp.float32),
    )
    reduced = (
        lax.psum(summed[0].astype(jnp.bfloat16), "ctx").astype(jnp.float32),
        lax.psum(summed[1].astype(jnp.bfloat16), "ctx").astype(jnp.float32),
        lax.psum(summed[2].astype(jnp.bfloat16), "ctx").astype(jnp.float32),
        lax.psum(summed[3].astype(jnp.bfloat16), "ctx").astype(jnp.float32),
        lax.psum(summed[4].astype(jnp.bfloat16), "ctx").astype(jnp.float32),
        lax.psum(summed[5].astype(jnp.bfloat16), "ctx").astype(jnp.float32),
        lax.psum(summed[6].astype(jnp.bfloat16), "ctx").astype(jnp.float32),
        lax.psum(summed[7].astype(jnp.bfloat16), "ctx").astype(jnp.float32),
        lax.psum(summed[8].astype(jnp.bfloat16), "ctx").astype(jnp.float32),
        lax.psum(summed[9].astype(jnp.bfloat16), "ctx").astype(jnp.float32),
        lax.psum(summed[10].astype(jnp.bfloat16), "ctx").astype(jnp.float32),
        lax.psum(summed[11].astype(jnp.bfloat16), "ctx").astype(jnp.float32),
        lax.psum(summed[12].astype(jnp.bfloat16), "ctx").astype(jnp.float32),
        lax.psum(summed[13].astype(jnp.bfloat16), "ctx").astype(jnp.float32),
        lax.psum(summed[14].astype(jnp.bfloat16), "ctx").astype(jnp.float32),
    )
    return (
        result.astype(bf16).reshape(tokens.shape),
        raw_logits,
        loss_value,
        grad_token_rows.astype(bf16).reshape(tokens.shape),
        grad_logits,
        reduced[0],
        reduced[1],
        reduced[2],
        reduced[3],
        reduced[4],
        reduced[5],
        reduced[6],
        reduced[7],
        reduced[8],
        reduced[9],
        reduced[10],
        reduced[11],
        reduced[12],
        reduced[13],
        reduced[14],
    )


def local_fast(tokens, prev_logits, teacher, lengths, *parameters):
    w_query, w_key, w_value, w_output, w_inner, w_outer, *vectors = parameters
    ctx_size = lax.axis_size("ctx")
    core = lax.axis_index("ctx")
    dp_size = lax.axis_size("dp")
    dp_rank = lax.axis_index("dp")
    block_len, width = tokens.shape[3], tokens.shape[4]
    head_count, seq_len = prev_logits.shape[1], prev_logits.shape[-1]
    head_dim = width // head_count
    rows = 2 * block_len
    shard = w_query.shape[0]
    half = width // 2
    units = w_inner.shape[1] // width
    vector_sizes = [v.shape[0] for v in vectors]
    info = jnp.stack([core, dp_rank % 4, lengths[0]]).astype(jnp.int32)
    token_rows = tokens.reshape(rows, width)
    other_rows = flip(token_rows, "ctx", 1)

    def own_columns(w, cols, index=0):
        return lax.dynamic_slice_in_dim(w, core * (w.shape[1] // 2) + index * cols, cols, 1)

    packed = jnp.concatenate(
        list(vectors) + [(lengths // 32).astype(bf16), (lengths % 32).astype(bf16)]
    )
    packed = jnp.pad(packed, (0, width - packed.shape[0]))[None]
    first_chunk = jnp.concatenate(
        [own_columns(w, half) for w in (w_query, w_key, w_value, w_output)]
        + [jnp.pad(own_columns(packed, half), ((0, 15), (0, 0)))]
    )
    attn_own, table_own = assemble(gather_planes(first_chunk, dp_rank), info, 4, shard, 16)
    attn_oth, table_oth = flip(attn_own, "ctx", 1), flip(table_own, "ctx", 1)
    table_own, table_oth = table_own[:, 0], table_oth[:, 0]
    table = jnp.where(
        core == 0,
        jnp.concatenate([table_own, table_oth], axis=1),
        jnp.concatenate([table_oth, table_own], axis=1),
    ).astype(f32)
    inner_chunk = jnp.concatenate([own_columns(w_inner, half, i) for i in range(units)])
    inner_own = assemble(gather_planes(inner_chunk, dp_rank), info, units, shard)
    inner_oth = flip(inner_own, "ctx", 1)
    outer_chunk = own_columns(w_outer, half)
    outer_own = assemble(gather_planes(outer_chunk, dp_rank), info, 1, outer_chunk.shape[0])[0]
    outer_oth = flip(outer_own, "ctx", 1)

    spread, at = [], 0
    for size in vector_sizes:
        spread.append(table[:, at : at + size].reshape(1, 16 * size))
        at += size
    valid_total = jnp.sum(table[:, at] * 32.0 + table[:, at + 1])
    bq, bv, bo, gain_one, shift_one, b_inner, b_outer, gain_two, shift_two = spread

    queries, keys, values = project(
        info, token_rows, other_rows, attn_own, attn_oth, bq, bv, block_len
    )
    prev_rows = prev_logits.reshape(head_count, rows, seq_len)
    logits, probs, mixed = attend(
        info, queries, keys, values, prev_rows, block_len, ctx_size, head_dim
    )
    first, first_low, normed, inverse = first_norm(
        info, mixed, token_rows, attn_own, attn_oth, bo, gain_one, shift_one
    )
    active, slope = inner(info, first_low, inner_own, inner_oth, b_inner)
    loss_scale = dp_size * seq_len * width / 2.0
    factor = (loss_scale * 2.0 / (valid_total * width)).reshape(1)
    result, grad_outer, grad_sum_two, outer_sums = outer(
        info, factor, active, outer_own, outer_oth, first, teacher.reshape(rows, width),
        b_outer, gain_two, shift_two, ctx_size,
    )
    grad_inner, inner_sums, outer_keep, outer_send = outer_back(
        info, grad_outer, active, slope, outer_own, outer_oth
    )
    inner_keep, inner_send, grad_sum_one, _, grad_mixed, first_sums = inner_back(
        info, grad_inner, first_low, inner_own, inner_oth, grad_sum_two, normed, inverse,
        gain_one, mixed, attn_own, attn_oth,
    )
    grad_logits, grad_queries, grad_keys, grad_values = attend_back(
        queries, keys, values, probs, grad_mixed, block_len, ctx_size, head_dim
    )
    slots = (2, 2, block_len, width)
    grad_keys, grad_values = grad_keys.reshape(slots), grad_values.reshape(slots)
    attn_keep, attn_send, token_sums = token_weights(
        info, token_rows, other_rows, grad_queries, grad_keys, grad_values
    )
    own_terms, sent_terms = token_terms(
        info, grad_queries, grad_keys, grad_values, attn_own, attn_oth, grad_sum_one
    )
    grad_tokens = own_terms + flip(sent_terms, "ctx", 1).astype(f32)

    def reduce_chunk(keep, send):
        keep, send = keep.reshape(16, -1, half), send.reshape(16, -1, half)
        total = scatter_planes(keep, flip(send, "ctx", 1), dp_rank).astype(bf16)
        across = flip(total, "ctx", 1)
        return (
            jnp.where(core == 0, total, across).astype(f32),
            jnp.where(core == 0, across, total).astype(f32),
        )

    def join(pair, start, count):
        return jnp.concatenate([part[start : start + count] for part in pair], axis=1)

    outer_pair = reduce_chunk(outer_keep, outer_send)
    inner_pair = reduce_chunk(inner_keep, inner_send)
    attn_pair = reduce_chunk(attn_keep, attn_send)
    grad_w_outer = jnp.concatenate(outer_pair, axis=1)
    grad_w_inner = jnp.concatenate(
        [part[i * shard : (i + 1) * shard] for part in inner_pair for i in range(units)], axis=1
    )
    grad_w_output = join(inner_pair, units * shard, shard)
    grad_w_query, grad_w_key, grad_w_value = [join(attn_pair, i * shard, shard) for i in range(3)]

    vector_grads = (
        token_sums[0],
        token_sums[1],
        first_sums[2],
        first_sums[0],
        first_sums[1],
        inner_sums[0],
        outer_sums[2],
        outer_sums[0],
        outer_sums[1],
    )
    vector_terms = jnp.concatenate([g.reshape(16, -1) for g in vector_grads], axis=1)
    vector_total, square_sum = scatter_small(vector_terms, jnp.sum(outer_sums[3]), dp_rank)
    vector_totals, at = [], 0
    for size in vector_sizes:
        vector_totals.append(vector_total[at : at + size])
        at += size
    loss = square_sum / (valid_total * width)
    return (
        result.reshape(tokens.shape),
        logits.reshape(prev_logits.shape),
        loss,
        grad_tokens.astype(bf16).reshape(tokens.shape),
        grad_logits.reshape(prev_logits.shape),
        grad_w_query,
        grad_w_key,
        grad_w_value,
        grad_w_output,
        grad_w_inner,
        grad_w_outer,
        *vector_totals,
    )


def local(tokens, prev_logits, teacher, lengths, *parameters):
    width, shard = tokens.shape[-1], parameters[0].shape[0]
    fits = (
        lax.axis_size("dp") == 16
        and lax.axis_size("ctx") == 2
        and tokens.shape[0] == 1
        and shard % 16 == 0
        and width % 256 == 0
    )
    chosen = local_fast if fits else local_plain
    return chosen(tokens, prev_logits, teacher, lengths, *parameters)


def solution(mesh):
    rows = P("dp", None, "ctx", None, None)
    scores = P("dp", None, None, "ctx", None, None)
    matrix, vector = P("dp", None), P("dp")
    return jax.shard_map(
        local,
        mesh=mesh,
        in_specs=(rows, scores, rows, vector) + (matrix,) * 6 + (vector,) * 9,
        out_specs=(rows, scores, P(), rows, scores) + (matrix,) * 6 + (vector,) * 9,
        check_vma=False,
    )
```

```python
import functools

import jax
import jax.numpy as jnp
from jax import lax
from jax.experimental import pallas as pl
from jax.experimental.pallas import tpu as pltpu
from jax.sharding import PartitionSpec as P

EPSILON = 1e-05
NEG_BIG = -1e30
POS_BIG = 3.0e38
LANES = 128
f32 = jnp.float32
bf16 = jnp.bfloat16
ANY = pl.BlockSpec(memory_space=pl.ANY)


def mm(left, right):
    return jnp.dot(left, right, preferred_element_type=f32)


def mm_tn(left, right):
    return lax.dot_general(left, right, (((0,), (0,)), ((), ())), preferred_element_type=f32)


def mm_nt(left, right):
    return lax.dot_general(left, right, (((1,), (1,)), ((), ())), preferred_element_type=f32)


def struct(shape, dtype):
    return jax.ShapeDtypeStruct(shape, dtype)


def params():
    return pltpu.CompilerParams(vmem_limit_bytes=56 << 20)


def cost(flops, bytes_accessed, transcendentals=0):
    return pl.CostEstimate(
        flops=int(flops), bytes_accessed=int(bytes_accessed), transcendentals=int(transcendentals)
    )


def together(*values):
    return lax.optimization_barrier(values)


def after(value, *others):
    return lax.optimization_barrier((value, others))[0]


def whole_block(array):
    rank = len(array.shape)
    return pl.BlockSpec(array.shape, lambda *_: (0,) * rank)


def side_lanes(info, side, width):
    half = info[0] if side == 0 else 1 - info[0]
    return pl.ds(pl.multiple_of(half * width, LANES), width)


def flip(array, axis_name, bit):
    size = lax.axis_size(axis_name)
    return lax.ppermute(array, axis_name, [(i, i ^ bit) for i in range(size)])


def z_bits():
    dp_rank = lax.axis_index("dp")
    return dp_rank // 4 % 2, dp_rank // 8


def z_pair(array, arrived):
    low = z_bits()[0] == 0
    return jnp.stack([jnp.where(low, array, arrived), jnp.where(low, arrived, array)])


def z_column(pair, arrived):
    low = z_bits()[1] == 0
    return jnp.concatenate([jnp.where(low, pair, arrived), jnp.where(low, arrived, pair)])


def side_columns(column):
    return flip(column, "dp", 1), flip(column, "dp", 2)


def corner_column(sides):
    cut = split_row(sides[0].shape[1])
    return flip(sides[0][:, :cut], "dp", 2), flip(sides[1][:, cut:], "dp", 1)


def split_row(rows):
    return rows // 32 * 16


def scatter_corner(kept, arrived):
    cut = split_row(kept.shape[1])
    term = (kept.astype(f32) + arrived.astype(f32)).astype(bf16)
    return flip(term[:, :cut], "dp", 2), flip(term[:, cut:], "dp", 1)


def scatter_sides(near, far, corner):
    upper, lower = [part.astype(f32) for part in corner]
    near = near[0].astype(f32) + near[1].astype(f32)
    far = far[0].astype(f32) + far[1].astype(f32)
    cut = upper.shape[1]
    near = jnp.concatenate([near[:, :cut] + upper, near[:, cut:]], axis=1)
    far = jnp.concatenate([far[:, :cut], far[:, cut:] + lower], axis=1)
    return flip(near.astype(bf16), "dp", 1), flip(far.astype(bf16), "dp", 2)


def scatter_half(own, sides):
    column = sum(part.astype(f32) for part in (*own, *sides))
    column = column.reshape(2, 2, *column.shape[1:])
    high = z_bits()[1]
    pick = lambda half: lax.dynamic_index_in_dim(column, half, 0, keepdims=False)
    return pick(high), flip(pick(1 - high).astype(bf16), "dp", 8)


def scatter_rank(kept, arrived):
    column = kept + arrived.astype(f32)
    low = z_bits()[0]
    pick = lambda half: lax.dynamic_index_in_dim(column, half, 0, keepdims=False)
    return pick(low), flip(pick(1 - low).astype(bf16), "dp", 4)


def scatter_total(kept, arrived):
    total = (kept + arrived.astype(f32)).astype(bf16)
    return total, flip(total, "ctx", 1)


def by_halves(total, across):
    core = lax.axis_index("ctx")
    return (
        jnp.where(core == 0, total, across).astype(f32),
        jnp.where(core == 0, across, total).astype(f32),
    )


def pack_kernel(shapes_at, info, *refs):
    count = len(refs) - 7
    weights, vectors, (attn_ref, feed_ref) = refs[:5], refs[5 : 5 + count], refs[5 + count :]
    half = attn_ref.shape[1]
    shard = weights[0].shape[0]
    for index, ref in enumerate(weights[:3]):
        attn_ref[index * shard : (index + 1) * shard, :] = ref[:, side_lanes(info, 0, half)]
    units = weights[4].shape[1] // (2 * half)
    for unit in range(units):
        column = pl.multiple_of((info[0] * units + unit) * half, LANES)
        feed_ref[unit * shard : (unit + 1) * shard, :] = weights[4][:, pl.ds(column, half)]
    feed_ref[units * shard :, :] = weights[3][:, side_lanes(info, 0, half)]
    row = lax.broadcasted_iota(jnp.int32, (16, half), 0)
    table = jnp.zeros((16, half), f32)
    for index, ref in enumerate(vectors):
        value = jnp.pad(ref[...].astype(f32), ((0, 0), (0, half - ref.shape[1])))
        table = jnp.where(row == index, value, table)
    table = jnp.where(row == count, (info[2] // 32).astype(f32), table)
    table = jnp.where(row == count + 1, (info[2] % 32).astype(f32), table)
    attn_ref[3 * shard :, :] = table.astype(bf16)


def pack(info, weights, vectors):
    shard, width = weights[0].shape
    half, units = width // 2, weights[4].shape[1] // width
    shapes = [struct((3 * shard + 16, half), bf16), struct(((units + 1) * shard, half), bf16)]
    args = [*weights, *[v[None] for v in vectors]]
    return pl.pallas_call(
        functools.partial(pack_kernel, None),
        out_shape=shapes,
        grid_spec=pltpu.PrefetchScalarGridSpec(
            num_scalar_prefetch=1,
            grid=(1,),
            in_specs=[whole_block(a) for a in args],
            out_specs=[whole_block(s) for s in shapes],
        ),
        compiler_params=params(),
        cost_estimate=cost(0, 8 * sum(w.size for w in weights)),
        name="pack",
    )(info, *args)


def piece_parts(pieces, plane, start, rows):
    column, near, far, upper, lower = pieces
    cut = upper.shape[1]
    parts = [(ref.at[:, pl.ds(start, rows)], plane ^ offset, 0, rows) for offset, ref in ((0, column), (1, near), (2, far))]
    if start < cut:
        count = min(start + rows, cut) - start
        parts.append((upper.at[:, pl.ds(start, count)], plane ^ 3, 0, count))
    if start + rows > cut:
        skip = max(start, cut)
        count = start + rows - skip
        parts.append((lower.at[:, pl.ds(skip - cut, count)], plane ^ 3, skip - start, count))
    return parts


def slot_start(slot, ctx_size, block_len):
    half, which = divmod(slot, ctx_size)
    return (which if half == 0 else 2 * ctx_size - 1 - which) * block_len


def head_lanes(which, head_dim):
    lane = lax.broadcasted_iota(jnp.int32, (1, LANES), 1)
    return (lane >= which * head_dim) & (lane < (which + 1) * head_dim)


def attend_kernel(
    block_len, ctx_size, head_dim, info, q_ref, k_ref, v_ref, prev_ref, logit_ref, prob_ref, mix_ref, limit_ref
):
    seq_len = 2 * ctx_size * block_len
    half = ctx_size * block_len
    heads = LANES // head_dim

    @pl.when(pl.program_id(0) == 0)
    def _():
        core, length = info[0], info[2]
        within = lax.broadcasted_iota(jnp.int32, (block_len, block_len), 1)
        row = lax.broadcasted_iota(jnp.int32, (block_len, block_len), 0)
        for part in range(2):
            start = core if part == 0 else 2 * ctx_size - 1 - core
            query_pos = row + start * block_len
            for slot in range(2 * ctx_size):
                key_pos = within + slot_start(slot, ctx_size, block_len)
                allowed = (key_pos <= query_pos) & (key_pos < length)
                limit_ref[
                    part * block_len : (part + 1) * block_len,
                    slot * block_len : (slot + 1) * block_len,
                ] = jnp.where(allowed, POS_BIG, NEG_BIG)

    scale = head_dim ** (-0.5)
    for part in range(2):
        rows = slice(part * block_len, (part + 1) * block_len)
        keys = half if part == 0 else seq_len
        mixed = jnp.zeros((block_len, LANES), f32)
        for which in range(heads):
            lanes = head_lanes(which, head_dim)
            query = jnp.where(lanes, q_ref[rows, :].astype(f32) * scale, 0.0).astype(bf16)
            raw = mm_nt(query, k_ref[...]) + prev_ref[which, rows, :].astype(f32)
            logit_ref[which, rows, :] = raw.astype(bf16)
            masked = jnp.minimum(raw[:, :keys], limit_ref[rows, :keys])
            top = jnp.max(masked, axis=-1, keepdims=True)
            exponent = jnp.exp(masked - top)
            total = jnp.sum(exponent, axis=-1, keepdims=True)
            probability = (exponent * (1.0 / total)).astype(bf16)
            prob_ref[which, rows, :keys] = probability
            mixed = jnp.where(lanes, mm(probability, v_ref[:keys, :]), mixed)
        mix_ref[rows, :] = mixed.astype(bf16)


def attend_back_kernel(
    block_len, ctx_size, head_dim, q_ref, k_ref, v_ref, prob_ref, gm_ref, gs_ref, gq_ref, gk_ref, gv_ref, gk_sum, gv_sum
):
    seq_len = 2 * ctx_size * block_len
    half = ctx_size * block_len
    heads = LANES // head_dim
    scale = head_dim ** (-0.5)
    gk_sum[...] = jnp.zeros_like(gk_sum)
    gv_sum[...] = jnp.zeros_like(gv_sum)
    for part in range(2):
        rows = slice(part * block_len, (part + 1) * block_len)
        keys = half if part == 0 else seq_len
        grad_query = jnp.zeros((block_len, LANES), f32)
        for which in range(heads):
            lanes = head_lanes(which, head_dim)
            grad_mix = jnp.where(lanes, gm_ref[rows, :], 0.0).astype(bf16)
            query = jnp.where(lanes, q_ref[rows, :], 0.0).astype(bf16)
            prob_low = prob_ref[which, rows, :keys]
            probability = prob_low.astype(f32)
            grad_prob = mm_nt(grad_mix, v_ref[:keys, :])
            term = probability * grad_prob
            row_dot = jnp.sum(term, axis=-1, keepdims=True)
            grad_score = (term - probability * row_dot).astype(bf16)
            gs_ref[which, rows, :keys] = grad_score
            if keys < seq_len:
                gs_ref[which, rows, keys:] = jnp.zeros((block_len, seq_len - keys), bf16)
            gv_sum[:keys, :] += mm_tn(prob_low, grad_mix)
            gk_sum[:keys, :] += mm_tn(grad_score, query)
            grad_query = jnp.where(lanes, mm(grad_score, k_ref[:keys, :]), grad_query)
        gq_ref[rows, :] = (grad_query * scale).astype(bf16)
    gk_ref[...] = (gk_sum[...] * scale).astype(bf16)
    gv_ref[...] = gv_sum[...].astype(bf16)


def pair_specs(rows, seq_len, heads, places):
    def at(h, which):
        index = places[-1][which]
        for i in range(len(places) - 1):
            index = jnp.where(h == i, places[i][which], index)
        return index

    wide = pl.BlockSpec((heads, rows, seq_len), lambda h, *_: (at(h, 0), 0, 0))
    mixed = pl.BlockSpec((rows, LANES), lambda h, *_: (0, at(h, 0)))
    narrow = pl.BlockSpec((rows, LANES), lambda h, *_: (0, at(h, 1)))
    whole = pl.BlockSpec((seq_len, LANES), lambda h, *_: (0, at(h, 1)))
    return wide, mixed, narrow, whole


def attend(info, qkv, prev, places, carry, block_len, ctx_size, head_dim):
    head_count, rows, seq_len = prev.shape
    heads, count = LANES // head_dim, len(places)
    wide, mixed, narrow, whole = pair_specs(rows, seq_len, heads, places)
    kernel = functools.partial(attend_kernel, block_len, ctx_size, head_dim)
    given = () if carry is None else carry
    mixed_shape = struct((rows, head_count * head_dim), bf16)
    return pl.pallas_call(
        drop_refs(kernel, 5, len(given)),
        out_shape=(struct(prev.shape, bf16), struct(prev.shape, bf16), mixed_shape),
        grid_spec=pltpu.PrefetchScalarGridSpec(
            num_scalar_prefetch=1,
            grid=(count,),
            in_specs=[narrow, whole, whole, wide] + [ANY] * len(given),
            out_specs=[wide, wide, mixed],
            scratch_shapes=[pltpu.VMEM((rows, seq_len), f32)],
        ),
        input_output_aliases={5 + i: i for i in range(len(given))},
        compiler_params=params(),
        cost_estimate=cost(
            8 * rows * seq_len * LANES * heads * count,
            6 * rows * seq_len * heads * count,
            rows * seq_len * heads * count,
        ),
        name="attend",
    )(info, *qkv, prev, *given)


def drop_refs(kernel, start, count):
    def run(*refs):
        kernel(*refs[:start], *refs[start + count :])

    return run if count else kernel


def attend_back(qkv, probs, grad_mixed, places, carry, block_len, ctx_size, head_dim):
    head_count, rows, seq_len = probs.shape
    heads, count = LANES // head_dim, len(places)
    wide, mixed, narrow, whole = pair_specs(rows, seq_len, heads, places)
    kernel = functools.partial(attend_back_kernel, block_len, ctx_size, head_dim)
    given = tuple(carry)
    return pl.pallas_call(
        drop_refs(kernel, 5, len(given)),
        out_shape=[struct(probs.shape, bf16)] + [struct(a.shape, bf16) for a in qkv],
        grid=(count,),
        in_specs=[narrow, whole, whole, wide, mixed] + [ANY] * len(given),
        out_specs=[wide, narrow, whole, whole],
        scratch_shapes=[pltpu.VMEM((seq_len, LANES), f32), pltpu.VMEM((seq_len, LANES), f32)],
        input_output_aliases={5 + i: i for i in range(len(given))},
        compiler_params=params(),
        cost_estimate=cost(
            16 * rows * seq_len * LANES * heads * count, 4 * rows * seq_len * heads * count
        ),
        name="attend_back",
    )(*qkv, probs, grad_mixed, *given)


def by_sides(ref, info, width):
    return jnp.concatenate(
        [ref[:, side_lanes(info, 0, width)], ref[:, side_lanes(info, 1, width)]], axis=1
    )


def project_kernel(info, own_tok, oth_tok, *refs):
    own, oth = refs[:5], refs[5:10]
    q_ref, k_ref, v_ref, w, table_ref, long_ref, table, sem = refs[10:]
    core, plane = info[0], info[1]
    block_len = k_ref.shape[2]
    rows, width = own_tok.shape
    half, shard = width // 2, width // 16
    cuts = [slice(0, half), slice(half, width)]
    copies = []

    def copy(source, dest):
        copies.append(pltpu.make_async_copy(source, dest, sem.at[len(copies)]))
        copies[-1].start()

    for source, where, _, _ in piece_parts(own, plane, 3 * shard, 16):
        copy(source, table.at[:, where])
    for unit in range(3):
        for side, pieces in enumerate((own, oth)):
            for source, where, first, count in piece_parts(pieces, plane, unit * shard, shard):
                copy(source, w.at[unit, :, where, pl.ds(first, count), cuts[side]])
    for item in copies:
        item.wait()
    long_span = long_ref.shape[1] // 16
    for rank in range(16):
        piece = table[rank // 4, rank % 4].astype(f32)
        table_ref[:, rank * shard : (rank + 1) * shard] = piece[:, :shard]
        long_ref[:, rank * long_span : (rank + 1) * long_span] = piece[:, :long_span]
    weights = [w[unit].reshape(width, width) for unit in range(3)]
    tokens = jnp.concatenate([own_tok[...], oth_tok[...]], axis=0)
    lanes = [side_lanes(info, side, half) for side in range(2)]
    query = mm(own_tok[...], weights[0])
    for side in range(2):
        q_ref[:, lanes[side]] = (query[:, cuts[side]] + table_ref[0:1, lanes[side]]).astype(bf16)
    for out, weight, row in ((k_ref, weights[1], None), (v_ref, weights[2], 1)):
        value = mm(tokens, weight)
        for side in range(2):
            piece = value[:, cuts[side]]
            if row is not None:
                piece = piece + table_ref[row : row + 1, lanes[side]]
            piece = piece.astype(bf16)
            for index in range(4):
                where = core if index < 2 else 1 - core
                out[index % 2, where, :, lanes[side]] = piece[index * block_len : (index + 1) * block_len]


def project(info, own_tok, oth_tok, own, oth, block_len, long_size):
    rows, width = own_tok.shape
    shard = width // 16
    q_shape = struct((rows, width), bf16)
    k_shape = struct((2, 2, block_len, width), bf16)
    shapes = [
        q_shape,
        k_shape,
        k_shape,
        struct((3, 4, 4, shard, width), bf16),
        struct((16, width), f32),
        struct((16, 16 * long_size), f32),
    ]
    q, k, v, w, table, long = pl.pallas_call(
        project_kernel,
        out_shape=shapes,
        grid_spec=pltpu.PrefetchScalarGridSpec(
            num_scalar_prefetch=1,
            grid=(1,),
            in_specs=[whole_block(own_tok)] * 2 + [ANY] * 10,
            out_specs=[whole_block(s) for s in shapes],
            scratch_shapes=[
                pltpu.VMEM((4, 4, 16, width // 2), bf16),
                pltpu.SemaphoreType.DMA((40,)),
            ],
        ),
        compiler_params=params(),
        cost_estimate=cost(10 * rows * width * width, 20 * rows * width + 12 * width * width),
        name="project",
    )(info, own_tok, oth_tok, *own, *oth)
    w = w.reshape(3, width, width)
    return q, k.reshape(2 * rows, width), v.reshape(2 * rows, width), w, table, long


def normalize(total):
    center = total - jnp.mean(total, axis=-1, keepdims=True)
    inverse = lax.rsqrt(jnp.mean(center * center, axis=-1, keepdims=True) + EPSILON)
    return center * inverse, inverse


def normalize_back(grad, normed, inverse):
    mean_grad = jnp.mean(grad, axis=-1, keepdims=True)
    mean_cross = jnp.mean(grad * normed, axis=-1, keepdims=True)
    return inverse * (grad - mean_grad - normed * mean_cross)


def gelu_parts(value):
    size = jnp.abs(value)
    near = 1.0 / (1.0 + (0.3275911 * 0.7071067811865476) * size)
    series = 0.5 * 1.061405429
    for factor in (-1.453152027, 1.421413741, -0.284496736, 0.254829592):
        series = series * near + 0.5 * factor
    bell = jnp.exp2((-0.5 * 1.4426950408889634) * (value * value))
    tail = series * near * bell
    active = jnp.maximum(value, 0.0) - size * tail
    below = jnp.where(value >= 0.0, 1.0 - tail, tail)
    return active, below + value * (bell * 0.3989422804014327)


def put_table(stage, start, sums, count, long_row=None):
    shard = sums.shape[1] // 16
    cols = stage.shape[4]
    low = sums[0:8, :]
    row = lax.broadcasted_iota(jnp.int32, (16, cols), 0)
    for rank in range(16):
        part = low[:, rank * shard : (rank + 1) * shard]
        part = jnp.pad(part, ((0, 8), (0, cols - shard)))
        table = jnp.where(row < count, part, 0.0)
        if long_row is not None:
            at = long_row + rank // 4
            span = sums.shape[1] // 4
            long = sums[at : at + 1, rank % 4 * span : (rank % 4 + 1) * span]
            table = jnp.where(row == count, jnp.pad(long, ((0, 0), (0, cols - span))), table)
        table = table.astype(bf16)
        for side in range(2):
            stage[side, rank // 4, rank % 4, start : start + 16, :] = table


def feed_kernel(
    ctx_size, rows_at, info, mix, tok, teacher, table, long_table, *refs
):
    own, oth, own_d, oth_d = refs[:5], refs[5:10], refs[10:15], refs[15:20]
    (
    out_ref, gs_ref, gm_ref, sum_ref, *terms, wc, wd, act, slope, value_ref, first, norm, inv, low, acc, go, stage_d, stage_c, sem,
    ) = refs[20:]
    terms_d, terms_c = terms[:8], terms[8:]
    core, plane = info[0], info[1]
    b_inner = long_table.at[pl.ds(rows_at["long"], 1)]
    units, rows_all, width = act.shape
    half = width // 2
    shard = width // 16
    block_len = rows_all // 2
    tile = 128
    tiles = [slice(start, start + tile) for start in range(0, rows_all, tile)]
    lanes = [side_lanes(info, side, half) for side in range(2)]
    cuts = [slice(0, half), slice(half, width)]
    count = [0]

    def start(source, dest):
        copy = pltpu.make_async_copy(source, dest, sem.at[count[0]])
        count[0] += 1
        copy.start()
        return copy

    def wait(copies):
        for copy in copies:
            copy.wait()

    def vector(index):
        row = rows_at[index]
        return table[row : row + 1, :]

    def unit_rows(side, unit):
        where = core if side == 0 else 1 - core
        return pl.ds(pl.multiple_of((where * units + unit) * half, LANES), half)

    load_c = {}
    for unit in [units] + list(range(units)):
        load_c[unit] = [
            start(source, wc.at[unit, :, where, pl.ds(first_row, rows), cuts[side]])
            for side, pieces in enumerate((own, oth))
            for source, where, first_row, rows in piece_parts(pieces, plane, unit * shard, shard)
        ]
    load_d = [
        start(source, wd.at[:, where, pl.ds(first_row, rows), cuts[side]])
        for side, pieces in enumerate((own_d, oth_d))
        for source, where, first_row, rows in piece_parts(pieces, plane, 0, wd.shape[2])
    ]

    def outer_unit(unit):
        ranks = half // wd.shape[2]
        blocks = []
        for side in range(2):
            where = core if side == 0 else 1 - core
            for index in range(ranks):
                rank = (where * units + unit) * ranks + index
                blocks.append(wd[rank // 4, rank % 4])
        return jnp.concatenate(blocks, axis=0)

    wait(load_c[units])
    value = mm(mix[...], wc[units].reshape(width, width))
    for side in range(2):
        acc[:, lanes[side]] = value[:, cuts[side]]
    for rows in tiles:
        normed, inverse = normalize(tok[rows, :].astype(f32) + (acc[rows, :] + vector("bo")))
        total = normed * vector("gain_one") + vector("shift_one")
        norm[rows, :] = normed
        inv[rows, :] = jnp.broadcast_to(inverse, (tile, LANES))
        first[rows, :] = total
        low[rows, :] = total.astype(bf16)

    for unit in range(units + 1):
        if unit < units:
            wait(load_c[unit])
            value = mm(low[...], wc[unit].reshape(width, width))
            for side in range(2):
                where = core if side == 0 else 1 - core
                column = pl.ds(pl.multiple_of((where * units + unit) * half, LANES), half)
                value_ref[unit % 2, :, cuts[side]] = value[:, cuts[side]] + b_inner[:, column]
        if unit > 0:
            for rows in tiles:
                active, steep = gelu_parts(value_ref[(unit - 1) % 2, rows, :])
                act[unit - 1, rows, :] = active.astype(bf16)
                slope[unit - 1, rows, :] = steep.astype(bf16)
    value = None
    wait(load_d)
    for unit in range(units):
        term = mm(act[unit], outer_unit(unit))
        value = term if value is None else value + term
    for side in range(2):
        acc[:, lanes[side]] = value[:, cuts[side]]

    valid_total = jnp.sum(
        vector("count") * 32.0 + table[rows_at["count"] + 1 : rows_at["count"] + 2, :], axis=-1, keepdims=True
    )
    factor = rows_at["scale"] * shard / (valid_total * width)
    sums = [jnp.zeros((8, width), f32) for _ in range(4)]
    for rows in tiles:
        part, inside = divmod(rows.start, block_len)
        base = (core if part == 0 else 2 * ctx_size - 1 - core) * block_len + inside
        position = lax.broadcasted_iota(jnp.int32, (tile, 1), 0) + base
        valid = (position < info[2]).astype(f32)
        normed, inverse = normalize(first[rows, :] + (acc[rows, :] + vector("b_outer")))
        result = normed * vector("gain_two") + vector("shift_two")
        out_ref[rows, :] = result.astype(bf16)
        error = (result - teacher[rows, :].astype(f32)) * valid
        grad_result = error * factor
        grad_sum = normalize_back(grad_result * vector("gain_two"), normed, inverse)
        grad_low = grad_sum.astype(bf16)
        acc[rows, :] = grad_sum
        go[rows, :] = grad_low
        terms = (grad_result * normed, grad_result, grad_low.astype(f32), error * error)
        for index, term in enumerate(terms):
            sums[index] = sums[index] + jnp.sum(term.reshape(tile // 8, 8, width), axis=0)
    for index in range(4):
        sum_ref[index : index + 1, :] = jnp.sum(sums[index], axis=0, keepdims=True)

    grad = by_sides(go, info, half)

    def put_c(term, unit):
        term = term.astype(bf16)
        rows = slice(unit * shard, (unit + 1) * shard)
        for side in range(2):
            stage_c[side, :, :, rows, :] = term[:, cuts[side]].reshape(4, 4, shard, half)

    def send(stage, outs):
        return [
            start(stage.at[side, :, plane ^ offset], outs[4 * side + offset])
            for offset in (3, 1, 2, 0)
            for side in (1, 0)
        ]

    for unit in range(units):
        term = mm_tn(act[unit], grad).astype(bf16)
        deep = stage_d.shape[3]
        for side in range(2):
            where = core if side == 0 else 1 - core
            for index in range(half // deep):
                rank = (where * units + unit) * (half // deep) + index
                rows = slice(side * half + index * deep, side * half + (index + 1) * deep)
                for col in range(2):
                    stage_d[col, rank // 4, rank % 4] = term[rows, cuts[col]]
    sent = send(stage_d, terms_d)
    for unit in range(units):
        grad_active = mm_nt(grad, outer_unit(unit))
        grad_inner = (grad_active * slope[unit].astype(f32)).astype(bf16)
        slope[unit] = grad_inner
        total = jnp.sum(grad_inner.astype(f32), axis=0, keepdims=True)
        for side in range(2):
            column = (core if side == 0 else 1 - core) * units + unit
            at = pl.ds(pl.multiple_of((column % 2) * half, LANES), half)
            sum_ref[pl.ds(8 + column // 2, 1), at] = total[:, cuts[side]]
        put_c(mm_tn(low[...], slope[unit]), unit)
        acc[...] += mm_nt(slope[unit], wc[unit].reshape(width, width))

    sums = [jnp.zeros((8, width), f32) for _ in range(3)]
    for rows in tiles:
        normed, grad_first = norm[rows, :], acc[rows, :]
        grad_sum = normalize_back(grad_first * vector("gain_one"), normed, inv[rows, 0:1])
        grad_low = grad_sum.astype(bf16)
        gs_ref[rows, :] = grad_sum
        go[rows, :] = grad_low
        terms = (grad_first * normed, grad_first, grad_low.astype(f32))
        for index, term in enumerate(terms):
            sums[index] = sums[index] + jnp.sum(term.reshape(tile // 8, 8, width), axis=0)
    for index in range(3):
        sum_ref[4 + index : 5 + index, :] = jnp.sum(sums[index], axis=0, keepdims=True)
    grad = by_sides(go, info, half)
    put_c(mm_tn(mix[...], grad), units)
    put_table(stage_c, (units + 1) * shard, sum_ref, 7, 8)
    sent += send(stage_c, terms_c)
    gm_ref[...] = mm_nt(grad, wc[units].reshape(width, width)).astype(bf16)
    wait(sent)


def feed(info, mix, tok, teacher, table, long_table, own, oth, own_d, oth_d, rows_at, ctx_size):
    rows, width = tok.shape
    half, units = width // 2, long_table.shape[1] // width
    shapes = [
        struct((rows, width), bf16),
        struct((rows, width), f32),
        struct((rows, width), bf16),
        struct((16, width), f32),
    ]
    deep = units * width // 16
    terms = [struct((4, deep, half), bf16)] * 8 + [struct((4, width // 16 * (units + 1) + 16, half), bf16)] * 8
    blocks = (mix, tok, teacher, table, long_table)
    flops = 2 * rows * width * (6 * units + 3) * width
    return pl.pallas_call(
        functools.partial(feed_kernel, ctx_size, rows_at),
        out_shape=shapes + terms,
        grid_spec=pltpu.PrefetchScalarGridSpec(
            num_scalar_prefetch=1,
            grid=(1,),
            in_specs=[whole_block(a) for a in blocks] + [ANY] * 20,
            out_specs=[whole_block(s) for s in shapes] + [ANY] * 16,
            scratch_shapes=[
                pltpu.VMEM((units + 1, 4, 4, width // 16, width), bf16),
                pltpu.VMEM((4, 4, deep, width), bf16),
                pltpu.VMEM((units, rows, width), bf16),
                pltpu.VMEM((units, rows, width), bf16),
                pltpu.VMEM((2, rows, width), f32),
                pltpu.VMEM((rows, width), f32),
                pltpu.VMEM((rows, width), f32),
                pltpu.VMEM((rows, LANES), f32),
                pltpu.VMEM((rows, width), bf16),
                pltpu.VMEM((rows, width), f32),
                pltpu.VMEM((rows, width), bf16),
                pltpu.VMEM((2, 4, 4, deep, half), bf16),
                pltpu.VMEM((2, 4, 4, width // 16 * (units + 1) + 16, half), bf16),
                pltpu.SemaphoreType.DMA((12 * units + 40,)),
            ],
        ),
        compiler_params=params(),
        cost_estimate=cost(flops, 30 * width * width, 2 * rows * width * units),
        name="feed",
    )(info, *blocks, *own, *oth, *own_d, *oth_d)


def slot_rows(ref, core, lanes):
    return jnp.concatenate(
        [ref[part, where, :, lanes] for where in (core, 1 - core) for part in range(2)], axis=0
    )


def token_weights_kernel(info, own_tok, oth_tok, gq, gk, gv, *refs):
    outs, stage, sum_ref, sem = refs[:8], refs[8], refs[9], refs[10]
    core, plane = info[0], info[1]
    width = own_tok.shape[1]
    half, shard = width // 2, width // 16
    tokens = jnp.concatenate([own_tok[...], oth_tok[...]], axis=0)

    def put(term, index):
        term = term.astype(bf16)
        rows = slice(index * shard, (index + 1) * shard)
        for side in range(2):
            cut = slice(side * half, (side + 1) * half)
            stage[side, :, :, rows, :] = term[:, cut].reshape(4, 4, shard, half)

    for index, grad in ((1, gk), (2, gv)):
        left = [slot_rows(grad, core, side_lanes(info, side, half)) for side in range(2)]
        put(mm_tn(tokens, jnp.concatenate(left, axis=1)), index)
    put(mm_tn(own_tok[...], by_sides(gq, info, half)), 0)
    sum_ref[0:1, :] = jnp.sum(gq[...].astype(f32), axis=0, keepdims=True)
    total = jnp.zeros((1, width), f32)
    for part in range(2):
        for where in range(2):
            total = total + jnp.sum(gv[part, where].astype(f32), axis=0, keepdims=True)
    sum_ref[1:2, :] = total
    put_table(stage, 3 * shard, sum_ref, 2)
    copies = []
    for offset in (3, 1, 2, 0):
        for side in (1, 0):
            copy = pltpu.make_async_copy(
                stage.at[side, :, plane ^ offset], outs[4 * side + offset], sem.at[len(copies)]
            )
            copy.start()
            copies.append(copy)
    for copy in copies:
        copy.wait()


def token_weights(info, own_tok, oth_tok, gq, gk, gv):
    rows, width = own_tok.shape
    deep, half = 3 * width // 16 + 16, width // 2
    args = (own_tok, oth_tok, gq, gk, gv)
    return pl.pallas_call(
        token_weights_kernel,
        out_shape=[struct((4, deep, half), bf16)] * 8,
        grid_spec=pltpu.PrefetchScalarGridSpec(
            num_scalar_prefetch=1,
            grid=(1,),
            in_specs=[whole_block(a) for a in args],
            out_specs=[ANY] * 8,
            scratch_shapes=[
                pltpu.VMEM((2, 4, 4, deep, half), bf16),
                pltpu.VMEM((8, width), f32),
                pltpu.SemaphoreType.DMA((8,)),
            ],
        ),
        compiler_params=params(),
        cost_estimate=cost(10 * rows * width * width, 14 * rows * width),
        name="token_weights",
    )(info, *args)


def token_terms_kernel(info, gs_one, gq, gk, gv, w, own_ref, send_ref):
    core = info[0]
    rows, half = gs_one.shape[0], w.shape[2] // 2
    lanes = [side_lanes(info, side, half) for side in range(2)]
    both = None
    for grad, weight in ((gk, w[1]), (gv, w[2])):
        left = jnp.concatenate([slot_rows(grad, core, lanes[side]) for side in range(2)], axis=1)
        term = mm_nt(left, weight)
        both = term if both is None else both + term
    query = mm_nt(by_sides(gq, info, half), w[0])
    own_ref[...] = gs_one[...] + query + both[:rows]
    send_ref[...] = both[rows:].astype(bf16)


def token_terms(info, gs_one, gq, gk, gv, w):
    rows, width = gs_one.shape
    shapes = [struct((rows, width), f32), struct((rows, width), bf16)]
    args = (gs_one, gq, gk, gv, w)
    return pl.pallas_call(
        token_terms_kernel,
        out_shape=shapes,
        grid_spec=pltpu.PrefetchScalarGridSpec(
            num_scalar_prefetch=1,
            grid=(1,),
            in_specs=[whole_block(a) for a in args],
            out_specs=[whole_block(s) for s in shapes],
        ),
        compiler_params=params(),
        cost_estimate=cost(10 * rows * width * width, 20 * rows * width + 6 * width * width),
        name="token_terms",
    )(info, *args)


def layout_positions(block_len, ctx_size, slot_index):
    within = jnp.arange(block_len, dtype=jnp.int32)
    front_pos = slot_index * block_len + within
    back_pos = (2 * ctx_size - 1 - slot_index) * block_len + within
    return (front_pos, back_pos)


def norm_forward(activation):
    center = activation - jnp.mean(activation, axis=-1, keepdims=True)
    inverse = lax.rsqrt(jnp.mean(center * center, axis=-1, keepdims=True) + EPSILON)
    return (center * inverse, inverse)


def norm_backward(grad_normed, normed, inverse):
    mean_grad = jnp.mean(grad_normed, axis=-1, keepdims=True)
    mean_cross = jnp.mean(grad_normed * normed, axis=-1, keepdims=True)
    return inverse * (grad_normed - mean_grad - normed * mean_cross)


def weight_grad(left, right):
    return lax.dot_general(
        left, right, (((0,), (0,)), ((), ())), preferred_element_type=jnp.float32
    )


def back_product(left, right):
    return lax.dot_general(
        left, right, (((1,), (1,)), ((), ())), preferred_element_type=jnp.float32
    )


def gelu_exact(inputs):
    return jax.nn.gelu(inputs, approximate=False)


def column_sum(matrix):
    return jnp.sum(matrix.astype(jnp.float32), axis=0)


def local_plain(
    tokens,
    prev_logits,
    teacher,
    lengths,
    w_query,
    w_key,
    w_value,
    w_output,
    w_inner,
    w_outer,
    bias_query,
    bias_value,
    bias_output,
    attn_gain,
    attn_shift,
    inner_bias,
    outer_bias,
    ffn_gain,
    ffn_shift,
):
    f32 = jnp.float32
    bf16 = jnp.bfloat16
    ctx_size = lax.axis_size("ctx")
    ctx_rank = lax.axis_index("ctx")
    dp_size = lax.axis_size("dp")
    groups = tokens.shape[0]
    block_len = tokens.shape[3]
    model_width = tokens.shape[4]
    head_count = prev_logits.shape[1]
    seq_len = prev_logits.shape[-1]
    head_dim = model_width // head_count
    local_rows = 2 * block_len
    total_rows = groups * local_rows
    score_scale = head_dim ** (-0.5)
    (
        query_matrix,
        key_matrix,
        value_matrix,
        output_matrix,
        query_add,
        value_add,
        output_add,
        first_gain,
        first_shift,
    ) = (
        lax.all_gather(w_query, "dp", axis=0, tiled=True),
        lax.all_gather(w_key, "dp", axis=0, tiled=True),
        lax.all_gather(w_value, "dp", axis=0, tiled=True),
        lax.all_gather(w_output, "dp", axis=0, tiled=True),
        lax.all_gather(bias_query, "dp", axis=0, tiled=True),
        lax.all_gather(bias_value, "dp", axis=0, tiled=True),
        lax.all_gather(bias_output, "dp", axis=0, tiled=True),
        lax.all_gather(attn_gain, "dp", axis=0, tiled=True),
        lax.all_gather(attn_shift, "dp", axis=0, tiled=True),
    )
    token_rows = tokens.reshape(total_rows, model_width)
    queries = (
        jnp.dot(token_rows, query_matrix, preferred_element_type=f32) + query_add.astype(f32)
    ).astype(bf16)
    key_rows = jnp.dot(token_rows, key_matrix, preferred_element_type=f32).astype(bf16)
    values = (
        jnp.dot(token_rows, value_matrix, preferred_element_type=f32) + value_add.astype(f32)
    ).astype(bf16)
    key_blocks, value_blocks = (
        lax.all_gather(
            key_rows.reshape(groups, 2, 1, block_len, model_width), "ctx", axis=2, tiled=True
        ),
        lax.all_gather(
            values.reshape(groups, 2, 1, block_len, model_width), "ctx", axis=2, tiled=True
        ),
    )
    inner_matrix, outer_matrix, inner_add, outer_add, second_gain, second_shift = (
        lax.all_gather(w_inner, "dp", axis=0, tiled=True),
        lax.all_gather(w_outer, "dp", axis=0, tiled=True),
        lax.all_gather(inner_bias, "dp", axis=0, tiled=True),
        lax.all_gather(outer_bias, "dp", axis=0, tiled=True),
        lax.all_gather(ffn_gain, "dp", axis=0, tiled=True),
        lax.all_gather(ffn_shift, "dp", axis=0, tiled=True),
    )
    front_pos, back_pos = layout_positions(block_len, ctx_size, ctx_rank)
    query_pos = jnp.stack([front_pos, back_pos]).reshape(local_rows)
    key_front, key_back = layout_positions(
        block_len, ctx_size, jnp.arange(ctx_size, dtype=jnp.int32)[:, None]
    )
    key_pos = jnp.stack([key_front, key_back]).reshape(seq_len)
    allowed = (key_pos[None, None, :] <= query_pos[None, :, None]) & (
        key_pos[None, None, :] < lengths[:, None, None]
    )
    valid_rows = (query_pos[None, :] < lengths[:, None]).astype(f32).reshape(total_rows)
    query_heads = queries.reshape(groups, local_rows, head_count, head_dim).transpose(2, 0, 1, 3)
    key_heads = key_blocks.reshape(groups, seq_len, head_count, head_dim).transpose(2, 0, 1, 3)
    value_heads = value_blocks.reshape(groups, seq_len, head_count, head_dim).transpose(2, 0, 1, 3)
    prev_rows = prev_logits.reshape(groups, head_count, local_rows, seq_len)

    def scores_of(head_id):
        raw_scores = (
            jnp.einsum(
                "grd,gkd->grk", query_heads[head_id], key_heads[head_id], preferred_element_type=f32
            )
            * score_scale
        )
        raw_scores = raw_scores + lax.dynamic_index_in_dim(
            prev_rows, head_id, 1, keepdims=False
        ).astype(f32)
        return (raw_scores, jnp.where(allowed, raw_scores, NEG_BIG))

    def attend(head_id):
        raw_scores, masked = scores_of(head_id)
        row_max = jnp.max(masked, axis=-1, keepdims=True)
        exponent = jnp.exp(masked - row_max)
        row_total = jnp.sum(exponent, axis=-1, keepdims=True)
        probability = (exponent / row_total).astype(bf16)
        mixed_part = jnp.einsum(
            "grk,gkd->grd", probability, value_heads[head_id], preferred_element_type=f32
        )
        return (mixed_part, row_max[..., 0] + jnp.log(row_total[..., 0]), raw_scores.astype(bf16))

    mixed_heads, log_totals, raw_heads = lax.map(attend, jnp.arange(head_count))
    raw_logits = jnp.moveaxis(raw_heads, 0, 1).reshape(prev_logits.shape)
    mixed_rows = mixed_heads.transpose(1, 2, 0, 3).reshape(total_rows, model_width).astype(bf16)
    attn_out = jnp.dot(mixed_rows, output_matrix, preferred_element_type=f32) + output_add.astype(
        f32
    )
    first_normed, first_inverse = norm_forward(token_rows.astype(f32) + attn_out)
    first = first_normed * first_gain.astype(f32) + first_shift.astype(f32)
    first_low = first.astype(bf16)
    inner_pre = jnp.dot(first_low, inner_matrix, preferred_element_type=f32) + inner_add.astype(f32)
    active, gelu_back = jax.vjp(gelu_exact, inner_pre)
    active_low = active.astype(bf16)
    outer_pre = jnp.dot(active_low, outer_matrix, preferred_element_type=f32) + outer_add.astype(
        f32
    )
    second_normed, second_inverse = norm_forward(first + outer_pre)
    result = second_normed * second_gain.astype(f32) + second_shift.astype(f32)
    errors = (result - teacher.reshape(total_rows, model_width).astype(f32)) * valid_rows[:, None]
    square_sum, valid_total = lax.psum(
        (jnp.sum(errors * errors), jnp.sum(valid_rows)), ("dp", "ctx")
    )
    loss_value = square_sum / (valid_total * model_width)
    loss_scale = dp_size * groups * seq_len * model_width / 2.0
    grad_result = errors * (loss_scale * 2.0 / (valid_total * model_width))
    grad_second_gain = jnp.sum(grad_result * second_normed, axis=0)
    grad_second_shift = jnp.sum(grad_result, axis=0)
    grad_sum_two = norm_backward(
        grad_result * second_gain.astype(f32), second_normed, second_inverse
    )
    grad_outer = grad_sum_two.astype(bf16)
    grad_outer_matrix = weight_grad(active_low, grad_outer)
    grad_outer_add = column_sum(grad_outer)
    grad_active = back_product(grad_outer, outer_matrix)
    grad_inner = gelu_back(grad_active)[0].astype(bf16)
    grad_inner_matrix = weight_grad(first_low, grad_inner)
    grad_inner_add = column_sum(grad_inner)
    grad_first = grad_sum_two + back_product(grad_inner, inner_matrix)
    grad_first_gain = jnp.sum(grad_first * first_normed, axis=0)
    grad_first_shift = jnp.sum(grad_first, axis=0)
    grad_sum_one = norm_backward(grad_first * first_gain.astype(f32), first_normed, first_inverse)
    grad_attn = grad_sum_one.astype(bf16)
    grad_output_matrix = weight_grad(mixed_rows, grad_attn)
    grad_output_add = column_sum(grad_attn)
    grad_mixed = back_product(grad_attn, output_matrix).astype(bf16)
    grad_mixed_heads = grad_mixed.reshape(groups, local_rows, head_count, head_dim).transpose(
        2, 0, 1, 3
    )

    def attend_back(head_id):
        _, masked = scores_of(head_id)
        probability = jnp.exp(masked - log_totals[head_id][..., None])
        grad_part = grad_mixed_heads[head_id]
        grad_value_part = jnp.einsum(
            "grk,grd->gkd", probability.astype(bf16), grad_part, preferred_element_type=f32
        )
        grad_probs = jnp.einsum(
            "grd,gkd->grk", grad_part, value_heads[head_id], preferred_element_type=f32
        )
        row_dot = jnp.sum(probability * grad_probs, axis=-1, keepdims=True)
        grad_scores = (probability * (grad_probs - row_dot)).astype(bf16)
        grad_query_part = (
            jnp.einsum("grk,gkd->grd", grad_scores, key_heads[head_id], preferred_element_type=f32)
            * score_scale
        )
        grad_key_part = (
            jnp.einsum(
                "grk,grd->gkd", grad_scores, query_heads[head_id], preferred_element_type=f32
            )
            * score_scale
        )
        return (grad_scores, grad_query_part, grad_key_part, grad_value_part)

    grad_score_heads, grad_query_heads, grad_key_heads, grad_value_heads = lax.map(
        attend_back, jnp.arange(head_count)
    )
    grad_logits = jnp.moveaxis(grad_score_heads, 0, 1).reshape(prev_logits.shape)
    grad_queries = (
        grad_query_heads.transpose(1, 2, 0, 3).reshape(total_rows, model_width).astype(bf16)
    )
    key_terms = grad_key_heads.transpose(1, 2, 0, 3).reshape(
        groups, 2, ctx_size, block_len, model_width
    )
    value_terms = grad_value_heads.transpose(1, 2, 0, 3).reshape(
        groups, 2, ctx_size, block_len, model_width
    )
    key_sums, value_sums = (
        lax.psum_scatter(
            key_terms.astype(jnp.bfloat16), "ctx", scatter_dimension=2, tiled=True
        ).astype(jnp.float32),
        lax.psum_scatter(
            value_terms.astype(jnp.bfloat16), "ctx", scatter_dimension=2, tiled=True
        ).astype(jnp.float32),
    )
    grad_keys = key_sums.reshape(total_rows, model_width).astype(bf16)
    grad_values = value_sums.reshape(total_rows, model_width).astype(bf16)
    grad_query_matrix = weight_grad(token_rows, grad_queries)
    grad_key_matrix = weight_grad(token_rows, grad_keys)
    grad_value_matrix = weight_grad(token_rows, grad_values)
    grad_query_add = column_sum(grad_queries)
    grad_value_add = column_sum(grad_values)
    grad_token_rows = (
        grad_sum_one
        + back_product(grad_queries, query_matrix)
        + back_product(grad_keys, key_matrix)
        + back_product(grad_values, value_matrix)
    )
    matrix_grads = (
        grad_query_matrix,
        grad_key_matrix,
        grad_value_matrix,
        grad_output_matrix,
        grad_inner_matrix,
        grad_outer_matrix,
    )
    vector_grads = (
        grad_query_add,
        grad_value_add,
        grad_output_add,
        grad_first_gain,
        grad_first_shift,
        grad_inner_add,
        grad_outer_add,
        grad_second_gain,
        grad_second_shift,
    )
    summed = (
        lax.psum_scatter(
            matrix_grads[0].astype(jnp.bfloat16), "dp", scatter_dimension=0, tiled=True
        ).astype(jnp.float32),
        lax.psum_scatter(
            matrix_grads[1].astype(jnp.bfloat16), "dp", scatter_dimension=0, tiled=True
        ).astype(jnp.float32),
        lax.psum_scatter(
            matrix_grads[2].astype(jnp.bfloat16), "dp", scatter_dimension=0, tiled=True
        ).astype(jnp.float32),
        lax.psum_scatter(
            matrix_grads[3].astype(jnp.bfloat16), "dp", scatter_dimension=0, tiled=True
        ).astype(jnp.float32),
        lax.psum_scatter(
            matrix_grads[4].astype(jnp.bfloat16), "dp", scatter_dimension=0, tiled=True
        ).astype(jnp.float32),
        lax.psum_scatter(
            matrix_grads[5].astype(jnp.bfloat16), "dp", scatter_dimension=0, tiled=True
        ).astype(jnp.float32),
        lax.psum_scatter(
            vector_grads[0].astype(jnp.bfloat16), "dp", scatter_dimension=0, tiled=True
        ).astype(jnp.float32),
        lax.psum_scatter(
            vector_grads[1].astype(jnp.bfloat16), "dp", scatter_dimension=0, tiled=True
        ).astype(jnp.float32),
        lax.psum_scatter(
            vector_grads[2].astype(jnp.bfloat16), "dp", scatter_dimension=0, tiled=True
        ).astype(jnp.float32),
        lax.psum_scatter(
            vector_grads[3].astype(jnp.bfloat16), "dp", scatter_dimension=0, tiled=True
        ).astype(jnp.float32),
        lax.psum_scatter(
            vector_grads[4].astype(jnp.bfloat16), "dp", scatter_dimension=0, tiled=True
        ).astype(jnp.float32),
        lax.psum_scatter(
            vector_grads[5].astype(jnp.bfloat16), "dp", scatter_dimension=0, tiled=True
        ).astype(jnp.float32),
        lax.psum_scatter(
            vector_grads[6].astype(jnp.bfloat16), "dp", scatter_dimension=0, tiled=True
        ).astype(jnp.float32),
        lax.psum_scatter(
            vector_grads[7].astype(jnp.bfloat16), "dp", scatter_dimension=0, tiled=True
        ).astype(jnp.float32),
        lax.psum_scatter(
            vector_grads[8].astype(jnp.bfloat16), "dp", scatter_dimension=0, tiled=True
        ).astype(jnp.float32),
    )
    reduced = (
        lax.psum(summed[0].astype(jnp.bfloat16), "ctx").astype(jnp.float32),
        lax.psum(summed[1].astype(jnp.bfloat16), "ctx").astype(jnp.float32),
        lax.psum(summed[2].astype(jnp.bfloat16), "ctx").astype(jnp.float32),
        lax.psum(summed[3].astype(jnp.bfloat16), "ctx").astype(jnp.float32),
        lax.psum(summed[4].astype(jnp.bfloat16), "ctx").astype(jnp.float32),
        lax.psum(summed[5].astype(jnp.bfloat16), "ctx").astype(jnp.float32),
        lax.psum(summed[6].astype(jnp.bfloat16), "ctx").astype(jnp.float32),
        lax.psum(summed[7].astype(jnp.bfloat16), "ctx").astype(jnp.float32),
        lax.psum(summed[8].astype(jnp.bfloat16), "ctx").astype(jnp.float32),
        lax.psum(summed[9].astype(jnp.bfloat16), "ctx").astype(jnp.float32),
        lax.psum(summed[10].astype(jnp.bfloat16), "ctx").astype(jnp.float32),
        lax.psum(summed[11].astype(jnp.bfloat16), "ctx").astype(jnp.float32),
        lax.psum(summed[12].astype(jnp.bfloat16), "ctx").astype(jnp.float32),
        lax.psum(summed[13].astype(jnp.bfloat16), "ctx").astype(jnp.float32),
        lax.psum(summed[14].astype(jnp.bfloat16), "ctx").astype(jnp.float32),
    )
    return (
        result.astype(bf16).reshape(tokens.shape),
        raw_logits,
        loss_value,
        grad_token_rows.astype(bf16).reshape(tokens.shape),
        grad_logits,
        reduced[0],
        reduced[1],
        reduced[2],
        reduced[3],
        reduced[4],
        reduced[5],
        reduced[6],
        reduced[7],
        reduced[8],
        reduced[9],
        reduced[10],
        reduced[11],
        reduced[12],
        reduced[13],
        reduced[14],
    )


def local_fast(tokens, prev_logits, teacher, lengths, *parameters):
    weights, vectors = parameters[:6], parameters[6:]
    w_outer = weights[5]
    ctx_size = lax.axis_size("ctx")
    core = lax.axis_index("ctx")
    dp_size = lax.axis_size("dp")
    dp_rank = lax.axis_index("dp")
    block_len, width = tokens.shape[3], tokens.shape[4]
    head_count, seq_len = prev_logits.shape[1], prev_logits.shape[-1]
    head_dim = width // head_count
    rows = 2 * block_len
    shard = weights[0].shape[0]
    half = width // 2
    units = weights[4].shape[1] // width
    info = jnp.stack([core, dp_rank % 4, lengths[0]]).astype(jnp.int32)
    token_rows = tokens.reshape(rows, width)
    teacher_rows = teacher.reshape(rows, width)
    prev_rows = prev_logits.reshape(head_count, rows, seq_len)
    sizes = (block_len, ctx_size, head_dim)
    pairs = [(i, i) for i in range(head_count * head_dim // LANES)]
    (long_at,) = [i for i, v in enumerate(vectors) if v.shape[0] != shard]
    names = ("bq", "bv", "bo", "gain_one", "shift_one", "long", "b_outer", "gain_two", "shift_two", "count")
    rows_at = {name: i for i, name in enumerate(names)}
    rows_at["scale"] = float(dp_size * seq_len * width)

    chunk_a, chunk_c = pack(info, weights[:5], vectors)
    chunk_d = lax.dynamic_slice_in_dim(w_outer, core * half, half, 1)
    cross = lambda piece: flip(piece, "ctx", 1)
    next_a = flip(chunk_a, "dp", 4)
    next_c = flip(after(chunk_c, next_a), "dp", 4)
    pair_a = z_pair(chunk_a, next_a)
    over_a = flip(pair_a, "dp", 8)
    other_rows = cross(after(token_rows, next_a))
    column_a = z_column(pair_a, over_a)
    sides_a = side_columns(column_a)
    pair_c = z_pair(after(chunk_c, over_a), next_c)
    over_c = flip(pair_c, "dp", 8)
    sides_a, other_rows = together(sides_a, other_rows)
    corner_a = corner_column(sides_a)
    own_a = [column_a, *sides_a]
    oth_a = [cross(piece) for piece in own_a]
    next_d = flip(after(chunk_d, sides_a), "dp", 4)
    corner_a, oth_a = together(corner_a, oth_a)
    oth_a = [*oth_a, *[cross(piece) for piece in corner_a]]
    own_a = [*own_a, *corner_a]
    column_c = z_column(pair_c, over_c)
    column_c, next_d, oth_a = together(column_c, next_d, oth_a)
    sides_c = side_columns(column_c)
    pair_d = z_pair(chunk_d, next_d)
    over_d = flip(pair_d, "dp", 8)
    queries, keys, values, w_attn, table, long_table = project(
        info, token_rows, other_rows, own_a, oth_a, block_len, vectors[long_at].shape[0]
    )
    oth_c = [cross(column_c)]
    queries, sides_c, oth_c, pair_d, over_d = together(queries, sides_c, oth_c, pair_d, over_d)
    corner_c = corner_column(sides_c)
    column_d = z_column(pair_d, over_d)
    sides_d = side_columns(column_d)
    oth_c.append(cross(sides_c[0]))
    qkv = (queries, keys, values)
    carry = attend(info, qkv, prev_rows, pairs[:4], None, *sizes)
    carry, oth_c, corner_c, column_d, sides_d = together(carry, oth_c, corner_c, column_d, sides_d)
    corner_d = corner_column(sides_d)
    own_c = [column_c, *sides_c, *corner_c]
    oth_c = oth_c + [cross(piece) for piece in own_c[2:]]
    logits, probs, mixed = attend(info, qkv, prev_rows, pairs[4:], carry, *sizes)
    mixed, oth_c, corner_d = together(mixed, oth_c, corner_d)
    own_d = [column_d, *sides_d, *corner_d]
    oth_d = [cross(piece) for piece in own_d]
    result, grad_sum_one, grad_mixed, sums, *terms = feed(
        info, mixed, token_rows, teacher_rows, table, long_table, own_c, oth_c, own_d, oth_d, rows_at, ctx_size
    )

    back = lambda some, carry: attend_back(qkv, probs, grad_mixed, some, carry, *sizes)
    kept_d, sent_d, kept_c, sent_c = terms[:4], terms[4:8], terms[8:12], terms[12:]
    square = jnp.sum(sums[3]).reshape(1)
    came_d = {3: cross(sent_d[3])}
    sent_d, sent_c, square, came_d[3], grad_mixed = together(
        sent_d, sent_c, square, came_d[3], grad_mixed
    )
    corner_d = scatter_corner(kept_d[3], came_d[3])
    came_d[1], came_d[2], came_c = cross(sent_d[1]), cross(sent_d[2]), {3: cross(sent_c[3])}
    grads = back(pairs[:2], [])
    grads, corner_d, came_d, came_c, sent_d, sent_c, square = together(
        grads, corner_d, came_d, came_c, sent_d, sent_c, square
    )
    sides_d = scatter_sides((kept_d[1], came_d[1]), (kept_d[2], came_d[2]), corner_d)
    corner_c = scatter_corner(kept_c[3], came_c[3])
    came_d[0] = cross(sent_d[0])
    grad_logits, gq, gk, gv = back(pairs[2:], grads)
    gk, gv = [g.reshape(2, 2, block_len, width) for g in (gk, gv)]
    gq, sides_d, corner_c, came_d[0], sent_c, square = together(
        gq, sides_d, corner_c, came_d[0], sent_c, square
    )
    half_d = scatter_half((kept_d[0], came_d[0]), sides_d)
    came_c[1], came_c[2], came_c[0] = [cross(sent_c[i]) for i in (1, 2, 0)]
    square = square + cross(square)
    terms_a = token_weights(info, token_rows, other_rows, gq, gk, gv)
    kept_a, sent_a = terms_a[:4], terms_a[4:]
    kept_a, sent_a, came_c, square, half_d = together(kept_a, sent_a, came_c, square, half_d)
    came_a = {3: cross(sent_a[3])}
    sides_c = scatter_sides((kept_c[1], came_c[1]), (kept_c[2], came_c[2]), corner_c)
    sent_a, came_a[3], square = together(sent_a, came_a[3], square)
    corner_a = scatter_corner(kept_a[3], came_a[3])
    square = square + flip(square, "dp", 1)
    own_terms, sent_terms = token_terms(info, after(grad_sum_one, came_a[3]), gq, gk, gv, w_attn)
    own_terms, sent_terms, corner_a, sent_a, square = together(
        own_terms, sent_terms, corner_a, sent_a, square
    )
    came_a[1], came_a[2] = cross(sent_a[1]), cross(sent_a[2])
    sides_a = scatter_sides((kept_a[1], came_a[1]), (kept_a[2], came_a[2]), corner_a)
    sides_c, came_a, square, sent_a, sent_terms = together(sides_c, came_a, square, sent_a, sent_terms)
    half_c = scatter_half((kept_c[0], came_c[0]), sides_c)
    rank_d = scatter_rank(*half_d)
    square = square + flip(square, "dp", 2)
    came_a[0] = cross(sent_a[0])
    grad_tokens = (own_terms + cross(sent_terms).astype(f32)).astype(bf16)
    sides_a, came_a[0], rank_d, square = together(sides_a, came_a[0], rank_d, square)
    half_a = scatter_half((kept_a[0], came_a[0]), sides_a)
    total_d = scatter_total(*rank_d)
    square = square + flip(square, "dp", 4)
    half_c, total_d, square = together(half_c, total_d, square)
    rank_c = scatter_rank(*half_c)
    rank_c, half_a = together(rank_c, half_a)
    rank_a = scatter_rank(*half_a)
    total_c = scatter_total(*rank_c)
    square = square + flip(square, "dp", 8)
    total_a = scatter_total(*rank_a)
    pair_a, pair_c, pair_d = by_halves(*total_a), by_halves(*total_c), by_halves(*total_d)
    valid_total = jnp.sum(table[rows_at["count"]] * 32.0 + table[rows_at["count"] + 1]) / shard

    def unit(parts, index):
        return [part[index * shard : (index + 1) * shard] for part in parts]

    grad_w_inner = jnp.concatenate(
        [unit(pair_c[side : side + 1], i)[0] for side in range(2) for i in range(units)], axis=1
    )
    sums_c, sums_a = total_c[0][(units + 1) * shard :].astype(f32), total_a[0][3 * shard :].astype(f32)
    order = (6, 4, 5, None, 2, 0, 1)
    vector_totals = [sums_a[0, :shard], sums_a[1, :shard]]
    vector_totals += [
        sums_c[7, : vectors[long_at].shape[0]] if i is None else sums_c[i, :shard] for i in order
    ]
    return (
        result.reshape(tokens.shape),
        logits.reshape(prev_logits.shape),
        square[0] / (valid_total * width),
        grad_tokens.reshape(tokens.shape),
        grad_logits.reshape(prev_logits.shape),
        *[jnp.concatenate(unit(pair_a, i), axis=1) for i in range(3)],
        jnp.concatenate(unit(pair_c, units), axis=1),
        grad_w_inner,
        jnp.concatenate(pair_d, axis=1),
        *vector_totals,
    )


def local(tokens, prev_logits, teacher, lengths, *parameters):
    width, shard = tokens.shape[-1], parameters[0].shape[0]
    fits = (
        lax.axis_size("dp") == 16
        and lax.axis_size("ctx") == 2
        and tokens.shape[0] == 1
        and shard % 16 == 0
        and width % 256 == 0
    )
    chosen = local_fast if fits else local_plain
    return chosen(tokens, prev_logits, teacher, lengths, *parameters)


def solution(mesh):
    rows = P("dp", None, "ctx", None, None)
    scores = P("dp", None, None, "ctx", None, None)
    matrix, vector = P("dp", None), P("dp")
    return jax.shard_map(
        local,
        mesh=mesh,
        in_specs=(rows, scores, rows, vector) + (matrix,) * 6 + (vector,) * 9,
        out_specs=(rows, scores, P(), rows, scores) + (matrix,) * 6 + (vector,) * 9,
        check_vma=False,
    )
```

```python
import functools

import jax
import jax.numpy as jnp
from jax import lax
from jax.experimental import pallas as pl
from jax.experimental.pallas import tpu as pltpu
from jax.sharding import PartitionSpec as P

EPSILON = 1e-05
NEG_BIG = -1e30
POS_BIG = 3.0e38
LANES = 128
f32 = jnp.float32
bf16 = jnp.bfloat16
ANY = pl.BlockSpec(memory_space=pl.ANY)


def mm(left, right):
    return jnp.dot(left, right, preferred_element_type=f32)


def mm_tn(left, right):
    return lax.dot_general(left, right, (((0,), (0,)), ((), ())), preferred_element_type=f32)


def mm_nt(left, right):
    return lax.dot_general(left, right, (((1,), (1,)), ((), ())), preferred_element_type=f32)


def struct(shape, dtype):
    return jax.ShapeDtypeStruct(shape, dtype)


def params():
    return pltpu.CompilerParams(vmem_limit_bytes=56 << 20)


def cost(flops, bytes_accessed, transcendentals=0):
    return pl.CostEstimate(
        flops=int(flops), bytes_accessed=int(bytes_accessed), transcendentals=int(transcendentals)
    )


def together(*values):
    return lax.optimization_barrier(values)


def after(value, *others):
    return lax.optimization_barrier((value, others))[0]


def whole_block(array):
    rank = len(array.shape)
    return pl.BlockSpec(array.shape, lambda *_: (0,) * rank)


def side_lanes(info, side, width):
    half = info[0] if side == 0 else 1 - info[0]
    return pl.ds(pl.multiple_of(half * width, LANES), width)


def flip(array, axis_name, bit):
    size = lax.axis_size(axis_name)
    return lax.ppermute(array, axis_name, [(i, i ^ bit) for i in range(size)])


def z_bits():
    dp_rank = lax.axis_index("dp")
    return dp_rank // 4 % 2, dp_rank // 8


def z_pair(array, arrived):
    low = z_bits()[0] == 0
    return jnp.stack([jnp.where(low, array, arrived), jnp.where(low, arrived, array)])


def z_column(pair, arrived):
    low = z_bits()[1] == 0
    return jnp.concatenate([jnp.where(low, pair, arrived), jnp.where(low, arrived, pair)])


def z_triple(array):
    return [array] + [flip(array, "dp", 4 * step) for step in (1, 2, 3)]


def in_order(mine, parts):
    return jnp.stack([lax.select_n(mine ^ i, *parts) for i in range(4)])


def side_columns(column):
    return flip(column, "dp", 1), flip(column, "dp", 2)


def corner_column(sides):
    cut = split_row(sides[0].shape[1])
    return flip(sides[0][:, :cut], "dp", 2), flip(sides[1][:, cut:], "dp", 1)


def split_row(rows):
    return rows // 32 * 16


def scatter_corner(kept, arrived):
    cut = split_row(kept.shape[1])
    term = (kept.astype(f32) + arrived.astype(f32)).astype(bf16)
    return flip(term[:, :cut], "dp", 2), flip(term[:, cut:], "dp", 1)


def scatter_sides(kept, arrived, corner):
    upper, lower = [part.astype(f32) for part in corner]
    near = kept[0].astype(f32) + arrived[0].astype(f32)
    far = kept[1].astype(f32) + arrived[1].astype(f32)
    cut = upper.shape[1]
    near = jnp.concatenate([near[:, :cut] + upper, near[:, cut:]], axis=1)
    far = jnp.concatenate([far[:, :cut], far[:, cut:] + lower], axis=1)
    return near.astype(bf16), far.astype(bf16)


def send_sides(sides):
    return flip(sides[0], "dp", 1), flip(sides[1], "dp", 2)


def scatter_half(kept, arrived, sides):
    column = sum(part.astype(f32) for part in (kept[2], arrived[2], *sides))
    column = column.reshape(2, 2, *column.shape[1:])
    high = z_bits()[1]
    pick = lambda half: lax.dynamic_index_in_dim(column, half, 0, keepdims=False)
    return pick(high), pick(1 - high).astype(bf16)


def scatter_rank(kept, arrived):
    column = kept + arrived.astype(f32)
    low = z_bits()[0]
    pick = lambda half: lax.dynamic_index_in_dim(column, half, 0, keepdims=False)
    return pick(low), flip(pick(1 - low).astype(bf16), "dp", 4)


def scatter_total(kept, arrived):
    total = (kept + arrived.astype(f32)).astype(bf16)
    return total, flip(total, "ctx", 1)


def by_halves(total, across):
    core = lax.axis_index("ctx")
    return (
        jnp.where(core == 0, total, across).astype(f32),
        jnp.where(core == 0, across, total).astype(f32),
    )


def pack_kernel(info, *refs):
    vectors, outs = refs[6:-4], refs[-4:]
    half = outs[0].shape[1]
    shard = refs[0].shape[0]
    units = refs[4].shape[1] // (2 * half)
    lanes = side_lanes(info, 0, half)

    def unit(index):
        column = pl.multiple_of((info[0] * units + index) * half, LANES)
        return refs[4][:, pl.ds(column, half)]

    for index in range(3):
        outs[0][index * shard : (index + 1) * shard, :] = refs[index][:, lanes]
    count = units // 2
    for index in range(count):
        rows = slice(index * shard, (index + 1) * shard)
        outs[1][rows, :] = unit(index)
        outs[2][rows, :] = unit(count + index)
    outs[1][count * shard :, :] = refs[3][:, lanes]
    split = refs[5].shape[0] - outs[3].shape[0]
    outs[2][count * shard :, :] = refs[5][:split, lanes]
    outs[3][...] = refs[5][split:, lanes]
    row = lax.broadcasted_iota(jnp.int32, (16, half), 0)
    table = jnp.zeros((16, half), f32)
    for index, ref in enumerate(vectors):
        value = jnp.pad(ref[...].astype(f32), ((0, 0), (0, half - ref.shape[1])))
        table = jnp.where(row == index, value, table)
    table = jnp.where(row == len(vectors), (info[2] // 32).astype(f32), table)
    table = jnp.where(row == len(vectors) + 1, (info[2] % 32).astype(f32), table)
    outs[0][3 * shard :, :] = table.astype(bf16)


def pack(info, weights, vectors):
    shard, width = weights[0].shape
    half, count = width // 2, weights[4].shape[1] // width // 2
    deep = weights[5].shape[0]
    split = deep // 32 * 16
    sizes = (3 * shard + 16, (count + 1) * shard, count * shard + split, deep - split)
    shapes = [struct((size, half), bf16) for size in sizes]
    args = [*weights, *[v[None] for v in vectors]]
    return pl.pallas_call(
        pack_kernel,
        out_shape=shapes,
        grid_spec=pltpu.PrefetchScalarGridSpec(
            num_scalar_prefetch=1,
            grid=(1,),
            in_specs=[whole_block(a) for a in args],
            out_specs=[whole_block(s) for s in shapes],
        ),
        compiler_params=params(),
        cost_estimate=cost(0, 4 * sum(w.size for w in weights)),
        name="pack",
    )(info, *args)


def piece_parts(pieces, cut, plane, start, rows):
    parts = []
    for offset in range(3):
        ref, base = pieces[offset]
        parts.append((ref.at[:, pl.ds(base + start, rows)], plane ^ (0, 1, 2)[offset], 0, rows))
    (upper, base_up), (lower, base_low) = pieces[3:]
    if start < cut:
        count = min(start + rows, cut) - start
        parts.append((upper.at[:, pl.ds(base_up + start, count)], plane ^ 3, 0, count))
    if start + rows > cut:
        skip = max(start, cut)
        count = start + rows - skip
        parts.append((lower.at[:, pl.ds(base_low + skip - cut, count)], plane ^ 3, skip - start, count))
    return parts


def slot_start(slot, ctx_size, block_len):
    half, which = divmod(slot, ctx_size)
    return (which if half == 0 else 2 * ctx_size - 1 - which) * block_len


def head_lanes(which, head_dim):
    lane = lax.broadcasted_iota(jnp.int32, (1, LANES), 1)
    return (lane >= which * head_dim) & (lane < (which + 1) * head_dim)


def attend_kernel(
    block_len, ctx_size, head_dim, info, q_ref, k_ref, v_ref, prev_ref, logit_ref, prob_ref, mix_ref, limit_ref
):
    seq_len = 2 * ctx_size * block_len
    half = ctx_size * block_len
    heads = LANES // head_dim

    @pl.when(pl.program_id(0) == 0)
    def _():
        core, length = info[0], info[2]
        within = lax.broadcasted_iota(jnp.int32, (block_len, block_len), 1)
        row = lax.broadcasted_iota(jnp.int32, (block_len, block_len), 0)
        for part in range(2):
            start = core if part == 0 else 2 * ctx_size - 1 - core
            query_pos = row + start * block_len
            for slot in range(2 * ctx_size):
                key_pos = within + slot_start(slot, ctx_size, block_len)
                allowed = (key_pos <= query_pos) & (key_pos < length)
                limit_ref[
                    part * block_len : (part + 1) * block_len,
                    slot * block_len : (slot + 1) * block_len,
                ] = jnp.where(allowed, POS_BIG, NEG_BIG)

    scale = head_dim ** (-0.5)
    for part in range(2):
        rows = slice(part * block_len, (part + 1) * block_len)
        keys = half if part == 0 else seq_len
        mixed = jnp.zeros((block_len, LANES), f32)
        for which in range(heads):
            lanes = head_lanes(which, head_dim)
            query = jnp.where(lanes, q_ref[rows, :].astype(f32) * scale, 0.0).astype(bf16)
            raw = mm_nt(query, k_ref[...]) + prev_ref[which, rows, :].astype(f32)
            logit_ref[which, rows, :] = raw.astype(bf16)
            masked = jnp.minimum(raw[:, :keys], limit_ref[rows, :keys])
            top = jnp.max(masked, axis=-1, keepdims=True)
            exponent = jnp.exp(masked - top)
            total = jnp.sum(exponent, axis=-1, keepdims=True)
            probability = (exponent * (1.0 / total)).astype(bf16)
            prob_ref[which, rows, :keys] = probability
            mixed = jnp.where(lanes, mm(probability, v_ref[:keys, :]), mixed)
        mix_ref[rows, :] = mixed.astype(bf16)


def attend_back_kernel(
    block_len, ctx_size, head_dim, q_ref, k_ref, v_ref, prob_ref, gm_ref, gs_ref, gq_ref, gk_ref, gv_ref, gk_sum, gv_sum
):
    seq_len = 2 * ctx_size * block_len
    half = ctx_size * block_len
    heads = LANES // head_dim
    scale = head_dim ** (-0.5)
    gk_sum[...] = jnp.zeros_like(gk_sum)
    gv_sum[...] = jnp.zeros_like(gv_sum)
    for part in range(2):
        rows = slice(part * block_len, (part + 1) * block_len)
        keys = half if part == 0 else seq_len
        grad_query = jnp.zeros((block_len, LANES), f32)
        for which in range(heads):
            lanes = head_lanes(which, head_dim)
            grad_mix = jnp.where(lanes, gm_ref[rows, :], 0.0).astype(bf16)
            query = jnp.where(lanes, q_ref[rows, :], 0.0).astype(bf16)
            prob_low = prob_ref[which, rows, :keys]
            probability = prob_low.astype(f32)
            grad_prob = mm_nt(grad_mix, v_ref[:keys, :])
            term = probability * grad_prob
            row_dot = jnp.sum(term, axis=-1, keepdims=True)
            grad_score = (term - probability * row_dot).astype(bf16)
            gs_ref[which, rows, :keys] = grad_score
            if keys < seq_len:
                gs_ref[which, rows, keys:] = jnp.zeros((block_len, seq_len - keys), bf16)
            gv_sum[:keys, :] += mm_tn(prob_low, grad_mix)
            gk_sum[:keys, :] += mm_tn(grad_score, query)
            grad_query = jnp.where(lanes, mm(grad_score, k_ref[:keys, :]), grad_query)
        gq_ref[rows, :] = (grad_query * scale).astype(bf16)
    gk_ref[...] = (gk_sum[...] * scale).astype(bf16)
    gv_ref[...] = gv_sum[...].astype(bf16)


def pair_specs(rows, seq_len, heads, places):
    def at(h, which):
        index = places[-1][which]
        for i in range(len(places) - 1):
            index = jnp.where(h == i, places[i][which], index)
        return index

    wide = pl.BlockSpec((heads, rows, seq_len), lambda h, *_: (at(h, 0), 0, 0))
    mixed = pl.BlockSpec((rows, LANES), lambda h, *_: (0, at(h, 0)))
    narrow = pl.BlockSpec((rows, LANES), lambda h, *_: (0, at(h, 1)))
    whole = pl.BlockSpec((seq_len, LANES), lambda h, *_: (0, at(h, 1)))
    return wide, mixed, narrow, whole


def attend(info, qkv, prev, places, carry, block_len, ctx_size, head_dim):
    head_count, rows, seq_len = prev.shape
    heads, count = LANES // head_dim, len(places)
    wide, mixed, narrow, whole = pair_specs(rows, seq_len, heads, places)
    kernel = functools.partial(attend_kernel, block_len, ctx_size, head_dim)
    given = () if carry is None else carry
    mixed_shape = struct((rows, head_count * head_dim), bf16)
    return pl.pallas_call(
        drop_refs(kernel, 5, len(given)),
        out_shape=(struct(prev.shape, bf16), struct(prev.shape, bf16), mixed_shape),
        grid_spec=pltpu.PrefetchScalarGridSpec(
            num_scalar_prefetch=1,
            grid=(count,),
            in_specs=[narrow, whole, whole, wide] + [ANY] * len(given),
            out_specs=[wide, wide, mixed],
            scratch_shapes=[pltpu.VMEM((rows, seq_len), f32)],
        ),
        input_output_aliases={5 + i: i for i in range(len(given))},
        compiler_params=params(),
        cost_estimate=cost(
            8 * rows * seq_len * LANES * heads * count,
            6 * rows * seq_len * heads * count,
            rows * seq_len * heads * count,
        ),
        name="attend",
    )(info, *qkv, prev, *given)


def drop_refs(kernel, start, count):
    def run(*refs):
        kernel(*refs[:start], *refs[start + count :])

    return run if count else kernel


def attend_back(qkv, probs, grad_mixed, places, carry, block_len, ctx_size, head_dim):
    head_count, rows, seq_len = probs.shape
    heads, count = LANES // head_dim, len(places)
    wide, mixed, narrow, whole = pair_specs(rows, seq_len, heads, places)
    kernel = functools.partial(attend_back_kernel, block_len, ctx_size, head_dim)
    given = tuple(carry)
    return pl.pallas_call(
        drop_refs(kernel, 5, len(given)),
        out_shape=[struct(probs.shape, bf16)] + [struct(a.shape, bf16) for a in qkv],
        grid=(count,),
        in_specs=[narrow, whole, whole, wide, mixed] + [ANY] * len(given),
        out_specs=[wide, narrow, whole, whole],
        scratch_shapes=[pltpu.VMEM((seq_len, LANES), f32), pltpu.VMEM((seq_len, LANES), f32)],
        input_output_aliases={5 + i: i for i in range(len(given))},
        compiler_params=params(),
        cost_estimate=cost(
            16 * rows * seq_len * LANES * heads * count, 4 * rows * seq_len * heads * count
        ),
        name="attend_back",
    )(*qkv, probs, grad_mixed, *given)


def by_sides(ref, info, width):
    return jnp.concatenate(
        [ref[:, side_lanes(info, 0, width)], ref[:, side_lanes(info, 1, width)]], axis=1
    )


def project_kernel(info, own_tok, oth_tok, *refs):
    own, oth = [[(ref, 0) for ref in refs[i : i + 5]] for i in (0, 5)]
    cut = split_row(refs[0].shape[1])
    q_ref, k_ref, v_ref, w, table_ref, long_ref, table, sem = refs[10:]
    core, plane = info[0], info[1]
    block_len = k_ref.shape[2]
    rows, width = own_tok.shape
    half, shard = width // 2, width // 16
    cuts = [slice(0, half), slice(half, width)]
    copies = []

    def copy(source, dest):
        copies.append(pltpu.make_async_copy(source, dest, sem.at[len(copies)]))
        copies[-1].start()

    for source, where, _, _ in piece_parts(own, cut, plane, 3 * shard, 16):
        copy(source, table.at[:, where])
    for unit in range(3):
        for side, pieces in enumerate((own, oth)):
            for source, where, first, count in piece_parts(pieces, cut, plane, unit * shard, shard):
                copy(source, w.at[unit, :, where, pl.ds(first, count), cuts[side]])
    for item in copies:
        item.wait()
    long_span = long_ref.shape[1] // 16
    for rank in range(16):
        piece = table[rank // 4, rank % 4].astype(f32)
        table_ref[:, rank * shard : (rank + 1) * shard] = piece[:, :shard]
        long_ref[:, rank * long_span : (rank + 1) * long_span] = piece[:, :long_span]
    weights = [w[unit].reshape(width, width) for unit in range(3)]
    tokens = jnp.concatenate([own_tok[...], oth_tok[...]], axis=0)
    lanes = [side_lanes(info, side, half) for side in range(2)]
    query = mm(own_tok[...], weights[0])
    for side in range(2):
        q_ref[:, lanes[side]] = (query[:, cuts[side]] + table_ref[0:1, lanes[side]]).astype(bf16)
    for out, weight, row in ((k_ref, weights[1], None), (v_ref, weights[2], 1)):
        value = mm(tokens, weight)
        for side in range(2):
            piece = value[:, cuts[side]]
            if row is not None:
                piece = piece + table_ref[row : row + 1, lanes[side]]
            piece = piece.astype(bf16)
            for index in range(4):
                where = core if index < 2 else 1 - core
                out[index % 2, where, :, lanes[side]] = piece[index * block_len : (index + 1) * block_len]


def project(info, own_tok, oth_tok, own, oth, block_len, long_size):
    rows, width = own_tok.shape
    shard = width // 16
    q_shape = struct((rows, width), bf16)
    k_shape = struct((2, 2, block_len, width), bf16)
    shapes = [
        q_shape,
        k_shape,
        k_shape,
        struct((3, 4, 4, shard, width), bf16),
        struct((16, width), f32),
        struct((16, 16 * long_size), f32),
    ]
    q, k, v, w, table, long = pl.pallas_call(
        project_kernel,
        out_shape=shapes,
        grid_spec=pltpu.PrefetchScalarGridSpec(
            num_scalar_prefetch=1,
            grid=(1,),
            in_specs=[whole_block(own_tok)] * 2 + [ANY] * 10,
            out_specs=[whole_block(s) for s in shapes],
            scratch_shapes=[
                pltpu.VMEM((4, 4, 16, width // 2), bf16),
                pltpu.SemaphoreType.DMA((40,)),
            ],
        ),
        compiler_params=params(),
        cost_estimate=cost(10 * rows * width * width, 20 * rows * width + 12 * width * width),
        name="project",
    )(info, own_tok, oth_tok, *own, *oth)
    w = w.reshape(3, width, width)
    return q, k.reshape(2 * rows, width), v.reshape(2 * rows, width), w, table, long


def normalize(total):
    center = total - jnp.mean(total, axis=-1, keepdims=True)
    inverse = lax.rsqrt(jnp.mean(center * center, axis=-1, keepdims=True) + EPSILON)
    return center * inverse, inverse


def normalize_back(grad, normed, inverse):
    mean_grad = jnp.mean(grad, axis=-1, keepdims=True)
    mean_cross = jnp.mean(grad * normed, axis=-1, keepdims=True)
    return inverse * (grad - mean_grad - normed * mean_cross)


def gelu_parts(value):
    size = jnp.abs(value)
    near = 1.0 / (1.0 + (0.3275911 * 0.7071067811865476) * size)
    series = 0.5 * 1.061405429
    for factor in (-1.453152027, 1.421413741, -0.284496736, 0.254829592):
        series = series * near + 0.5 * factor
    bell = jnp.exp2((-0.5 * 1.4426950408889634) * (value * value))
    tail = series * near * bell
    active = jnp.maximum(value, 0.0) - size * tail
    below = jnp.where(value >= 0.0, 1.0 - tail, tail)
    return active, below + value * (bell * 0.3989422804014327)


def put_table(stage, start, sums, count, long_row=None):
    shard = sums.shape[1] // 16
    cols = stage.shape[4]
    low = sums[0:8, :]
    row = lax.broadcasted_iota(jnp.int32, (16, cols), 0)
    for rank in range(16):
        part = low[:, rank * shard : (rank + 1) * shard]
        part = jnp.pad(part, ((0, 8), (0, cols - shard)))
        table = jnp.where(row < count, part, 0.0)
        if long_row is not None:
            at = long_row + rank // 4
            span = sums.shape[1] // 4
            long = sums[at : at + 1, rank % 4 * span : (rank % 4 + 1) * span]
            table = jnp.where(row == count, jnp.pad(long, ((0, 0), (0, cols - span))), table)
        table = table.astype(bf16)
        for side in range(2):
            stage[side, rank // 4, rank % 4, start : start + 16, :] = table


def term_slots(outs, side):
    first, rest = outs[2 * side : 2 * side + 2]
    return [first, rest.at[0], rest.at[1], rest.at[2]]


def chunk_pieces(refs, rows_at, which):
    if which == "c":
        return [(refs[0], 0), (refs[1], 0), (refs[2], 0), (refs[3], 0), (refs[4], 0)]
    low = rows_at["rows_c"] - rows_at["cut_c"]
    return [(refs[5], 0), (refs[4], low), (refs[3], rows_at["cut_c"]), (refs[6], 0), (refs[7], 0)]


def feed_kernel(
    ctx_size, rows_at, info, mix, tok, teacher, table, long_table, *refs
):
    count_in = 12
    own, oth = refs[:count_in], refs[count_in : 2 * count_in]
    (
    out_ref, gs_ref, gm_ref, *terms, wc, wd, act, slope, value_ref, first, norm, inv, low, acc, go, stage_d, stage_c, sum_ref, sem,
    ) = refs[2 * count_in :]
    square_ref, *terms = terms
    terms_d, terms_c = terms[:4], terms[4:]
    core, plane = info[0], info[1]
    b_inner = long_table.at[pl.ds(rows_at["long"], 1)]
    units, rows_all, width = act.shape
    half = width // 2
    shard = width // 16
    block_len = rows_all // 2
    tile = 128
    tiles = [slice(start, start + tile) for start in range(0, rows_all, tile)]
    lanes = [side_lanes(info, side, half) for side in range(2)]
    cuts = [slice(0, half), slice(half, width)]
    count = [0]

    def start(source, dest):
        copy = pltpu.make_async_copy(source, dest, sem.at[count[0]])
        count[0] += 1
        copy.start()
        return copy

    def wait(copies):
        for copy in copies:
            copy.wait()

    def vector(index):
        row = rows_at[index]
        return table[row : row + 1, :]

    def unit_rows(side, unit):
        where = core if side == 0 else 1 - core
        return pl.ds(pl.multiple_of((where * units + unit) * half, LANES), half)

    def unit_parts(pieces, unit):
        split = units // 2
        if split <= unit < units:
            return piece_parts(
                chunk_pieces(pieces, rows_at, "d"), rows_at["cut_d"], plane, (unit - split) * shard, shard
            )
        at = split if unit == units else unit
        return piece_parts(chunk_pieces(pieces, rows_at, "c"), rows_at["cut_c"], plane, at * shard, shard)

    load_c = {}
    for unit in [units] + list(range(units)):
        load_c[unit] = [
            start(source, wc.at[unit, :, where, pl.ds(first_row, rows), cuts[side]])
            for side, pieces in enumerate((own, oth))
            for source, where, first_row, rows in unit_parts(pieces, unit)
        ]
    deep_d = rows_at["deep_d"]
    load_d = [
        start(source, wd.at[:, where, pl.ds(first_row, rows), cuts[side]])
        for side, pieces in enumerate((own, oth))
        for source, where, first_row, rows in piece_parts(
            chunk_pieces(pieces, rows_at, "d"), rows_at["cut_d"], plane, units // 2 * shard, deep_d
        )
    ]
    rest = pl.ds(deep_d, wd.shape[2] - deep_d)
    for side, pieces in enumerate((own, oth)):
        layers = pieces[8:12]
        load_d += [start(ref, wd.at[info[3] ^ i, :, rest, cuts[side]]) for i, ref in enumerate(layers)]

    def outer_unit(unit):
        ranks = half // wd.shape[2]
        blocks = []
        for side in range(2):
            where = core if side == 0 else 1 - core
            for index in range(ranks):
                rank = (where * units + unit) * ranks + index
                blocks.append(wd[rank // 4, rank % 4])
        return jnp.concatenate(blocks, axis=0)

    wait(load_c[units])
    value = mm(mix[...], wc[units].reshape(width, width))
    for side in range(2):
        acc[:, lanes[side]] = value[:, cuts[side]]
    for rows in tiles:
        normed, inverse = normalize(tok[rows, :].astype(f32) + (acc[rows, :] + vector("bo")))
        total = normed * vector("gain_one") + vector("shift_one")
        norm[rows, :] = normed
        inv[rows, :] = jnp.broadcast_to(inverse, (tile, LANES))
        first[rows, :] = total
        low[rows, :] = total.astype(bf16)

    for unit in range(units + 1):
        if unit < units:
            wait(load_c[unit])
            value = mm(low[...], wc[unit].reshape(width, width))
            for side in range(2):
                where = core if side == 0 else 1 - core
                column = pl.ds(pl.multiple_of((where * units + unit) * half, LANES), half)
                value_ref[unit % 2, :, cuts[side]] = value[:, cuts[side]] + b_inner[:, column]
        if unit > 0:
            for rows in tiles:
                active, steep = gelu_parts(value_ref[(unit - 1) % 2, rows, :])
                act[unit - 1, rows, :] = active.astype(bf16)
                slope[unit - 1, rows, :] = steep.astype(bf16)
    value = None
    wait(load_d)
    for unit in range(units):
        term = mm(act[unit], outer_unit(unit))
        value = term if value is None else value + term
    for side in range(2):
        acc[:, lanes[side]] = value[:, cuts[side]]

    valid_total = jnp.sum(
        vector("count") * 32.0 + table[rows_at["count"] + 1 : rows_at["count"] + 2, :], axis=-1, keepdims=True
    )
    factor = rows_at["scale"] * shard / (valid_total * width)
    sums = [jnp.zeros((8, width), f32) for _ in range(4)]
    for rows in tiles:
        part, inside = divmod(rows.start, block_len)
        base = (core if part == 0 else 2 * ctx_size - 1 - core) * block_len + inside
        position = lax.broadcasted_iota(jnp.int32, (tile, 1), 0) + base
        valid = (position < info[2]).astype(f32)
        normed, inverse = normalize(first[rows, :] + (acc[rows, :] + vector("b_outer")))
        result = normed * vector("gain_two") + vector("shift_two")
        out_ref[rows, :] = result.astype(bf16)
        error = (result - teacher[rows, :].astype(f32)) * valid
        grad_result = error * factor
        grad_sum = normalize_back(grad_result * vector("gain_two"), normed, inverse)
        grad_low = grad_sum.astype(bf16)
        acc[rows, :] = grad_sum
        go[rows, :] = grad_low
        terms = (grad_result * normed, grad_result, grad_low.astype(f32), error * error)
        for index, term in enumerate(terms):
            sums[index] = sums[index] + jnp.sum(term.reshape(tile // 8, 8, width), axis=0)
    for index in range(4):
        sum_ref[index : index + 1, :] = jnp.sum(sums[index], axis=0, keepdims=True)
    loss_part = jnp.sum(sum_ref[3:4, :], axis=-1, keepdims=True) * shard / (valid_total * width)
    square_ref[...] = jnp.broadcast_to(loss_part, (8, LANES))

    grad = by_sides(go, info, half)

    def put_c(term, unit):
        term = term.astype(bf16)
        rows = slice(unit * shard, (unit + 1) * shard)
        for side in range(2):
            stage_c[side, :, :, rows, :] = term[:, cuts[side]].reshape(4, 4, shard, half)

    def send(stage, outs):
        return [
            start(stage.at[side, :, plane ^ offset], dest)
            for side in (1, 0)
            for offset, dest in zip((3, 1, 2, 0), term_slots(outs, side))
        ]

    for unit in range(units):
        term = mm_tn(act[unit], grad).astype(bf16)
        deep = stage_d.shape[3]
        for side in range(2):
            where = core if side == 0 else 1 - core
            for index in range(half // deep):
                rank = (where * units + unit) * (half // deep) + index
                rows = slice(side * half + index * deep, side * half + (index + 1) * deep)
                for col in range(2):
                    stage_d[col, rank // 4, rank % 4] = term[rows, cuts[col]]
    sent = send(stage_d, terms_d)
    for unit in range(units):
        grad_active = mm_nt(grad, outer_unit(unit))
        grad_inner = (grad_active * slope[unit].astype(f32)).astype(bf16)
        slope[unit] = grad_inner
        total = jnp.sum(grad_inner.astype(f32), axis=0, keepdims=True)
        for side in range(2):
            column = (core if side == 0 else 1 - core) * units + unit
            at = pl.ds(pl.multiple_of((column % 2) * half, LANES), half)
            sum_ref[pl.ds(8 + column // 2, 1), at] = total[:, cuts[side]]
        put_c(mm_tn(low[...], slope[unit]), unit)
        acc[...] += mm_nt(slope[unit], wc[unit].reshape(width, width))

    sums = [jnp.zeros((8, width), f32) for _ in range(3)]
    for rows in tiles:
        normed, grad_first = norm[rows, :], acc[rows, :]
        grad_sum = normalize_back(grad_first * vector("gain_one"), normed, inv[rows, 0:1])
        grad_low = grad_sum.astype(bf16)
        gs_ref[rows, :] = grad_sum
        go[rows, :] = grad_low
        terms = (grad_first * normed, grad_first, grad_low.astype(f32))
        for index, term in enumerate(terms):
            sums[index] = sums[index] + jnp.sum(term.reshape(tile // 8, 8, width), axis=0)
    for index in range(3):
        sum_ref[4 + index : 5 + index, :] = jnp.sum(sums[index], axis=0, keepdims=True)
    grad = by_sides(go, info, half)
    put_c(mm_tn(mix[...], grad), units)
    put_table(stage_c, (units + 1) * shard, sum_ref, 7, 8)
    sent += send(stage_c, terms_c)
    gm_ref[...] = mm_nt(grad, wc[units].reshape(width, width)).astype(bf16)
    wait(sent)


def feed(info, mix, tok, teacher, table, long_table, own, oth, rows_at, ctx_size):
    rows, width = tok.shape
    half, units = width // 2, long_table.shape[1] // width
    shapes = [
        struct((rows, width), bf16),
        struct((rows, width), f32),
        struct((rows, width), bf16),
        struct((8, LANES), f32),
    ]
    deep = units * width // 16
    terms = []
    for size in (deep, width // 16 * (units + 1) + 16):
        terms += [struct((4, size, half), bf16), struct((3, 4, size, half), bf16)] * 2
    blocks = (mix, tok, teacher, table, long_table)
    flops = 2 * rows * width * (6 * units + 3) * width
    return pl.pallas_call(
        functools.partial(feed_kernel, ctx_size, rows_at),
        out_shape=shapes + terms,
        grid_spec=pltpu.PrefetchScalarGridSpec(
            num_scalar_prefetch=1,
            grid=(1,),
            in_specs=[whole_block(a) for a in blocks] + [ANY] * 24,
            out_specs=[whole_block(s) for s in shapes] + [ANY] * 8,
            scratch_shapes=[
                pltpu.VMEM((units + 1, 4, 4, width // 16, width), bf16),
                pltpu.VMEM((4, 4, deep, width), bf16),
                pltpu.VMEM((units, rows, width), bf16),
                pltpu.VMEM((units, rows, width), bf16),
                pltpu.VMEM((2, rows, width), f32),
                pltpu.VMEM((rows, width), f32),
                pltpu.VMEM((rows, width), f32),
                pltpu.VMEM((rows, LANES), f32),
                pltpu.VMEM((rows, width), bf16),
                pltpu.VMEM((rows, width), f32),
                pltpu.VMEM((rows, width), bf16),
                pltpu.VMEM((2, 4, 4, deep, half), bf16),
                pltpu.VMEM((2, 4, 4, width // 16 * (units + 1) + 16, half), bf16),
                pltpu.VMEM((16, width), f32),
                pltpu.SemaphoreType.DMA((12 * units + 60,)),
            ],
        ),
        compiler_params=params(),
        cost_estimate=cost(flops, 30 * width * width, 2 * rows * width * units),
        name="feed",
    )(info, *blocks, *own, *oth)


def slot_rows(ref, core, lanes):
    return jnp.concatenate(
        [ref[part, where, :, lanes] for where in (core, 1 - core) for part in range(2)], axis=0
    )


def token_back_kernel(info, own_tok, oth_tok, gq, gk, gv, gs_one, w, own_ref, send_ref, *refs):
    outs, stage, sum_ref, sem = refs[:4], refs[4], refs[5], refs[6]
    core, plane = info[0], info[1]
    width = own_tok.shape[1]
    half, shard = width // 2, width // 16
    tokens = jnp.concatenate([own_tok[...], oth_tok[...]], axis=0)

    def put(term, index):
        term = term.astype(bf16)
        rows = slice(index * shard, (index + 1) * shard)
        for side in range(2):
            cut = slice(side * half, (side + 1) * half)
            stage[side, :, :, rows, :] = term[:, cut].reshape(4, 4, shard, half)

    for index, grad in ((1, gk), (2, gv)):
        left = [slot_rows(grad, core, side_lanes(info, side, half)) for side in range(2)]
        put(mm_tn(tokens, jnp.concatenate(left, axis=1)), index)
    put(mm_tn(own_tok[...], by_sides(gq, info, half)), 0)
    sum_ref[0:1, :] = jnp.sum(gq[...].astype(f32), axis=0, keepdims=True)
    total = jnp.zeros((1, width), f32)
    for part in range(2):
        for where in range(2):
            total = total + jnp.sum(gv[part, where].astype(f32), axis=0, keepdims=True)
    sum_ref[1:2, :] = total
    put_table(stage, 3 * shard, sum_ref, 2)
    copies = []
    for side in (1, 0):
        for offset, dest in zip((3, 1, 2, 0), term_slots(outs, side)):
            copy = pltpu.make_async_copy(
                stage.at[side, :, plane ^ offset], dest, sem.at[len(copies)]
            )
            copy.start()
            copies.append(copy)
    rows = own_tok.shape[0]
    both = None
    for grad, weight in ((gk, w[1]), (gv, w[2])):
        left = [slot_rows(grad, core, side_lanes(info, side, half)) for side in range(2)]
        part = mm_nt(jnp.concatenate(left, axis=1), weight)
        both = part if both is None else both + part
    query = mm_nt(by_sides(gq, info, half), w[0])
    own_ref[...] = gs_one[...] + query + both[:rows]
    send_ref[...] = both[rows:].astype(bf16)
    for copy in copies:
        copy.wait()


def token_back(info, own_tok, oth_tok, gq, gk, gv, gs_one, w):
    rows, width = own_tok.shape
    deep, half = 3 * width // 16 + 16, width // 2
    args = (own_tok, oth_tok, gq, gk, gv, gs_one, w)
    shapes = [struct((rows, width), f32), struct((rows, width), bf16)]
    return pl.pallas_call(
        token_back_kernel,
        out_shape=shapes + [struct((4, deep, half), bf16), struct((3, 4, deep, half), bf16)] * 2,
        grid_spec=pltpu.PrefetchScalarGridSpec(
            num_scalar_prefetch=1,
            grid=(1,),
            in_specs=[whole_block(a) for a in args],
            out_specs=[whole_block(s) for s in shapes] + [ANY] * 4,
            scratch_shapes=[
                pltpu.VMEM((2, 4, 4, deep, half), bf16),
                pltpu.VMEM((8, width), f32),
                pltpu.SemaphoreType.DMA((8,)),
            ],
        ),
        compiler_params=params(),
        cost_estimate=cost(20 * rows * width * width, 40 * rows * width),
        name="token_back",
    )(info, *args)


def layout_positions(block_len, ctx_size, slot_index):
    within = jnp.arange(block_len, dtype=jnp.int32)
    front_pos = slot_index * block_len + within
    back_pos = (2 * ctx_size - 1 - slot_index) * block_len + within
    return (front_pos, back_pos)


def norm_forward(activation):
    center = activation - jnp.mean(activation, axis=-1, keepdims=True)
    inverse = lax.rsqrt(jnp.mean(center * center, axis=-1, keepdims=True) + EPSILON)
    return (center * inverse, inverse)


def norm_backward(grad_normed, normed, inverse):
    mean_grad = jnp.mean(grad_normed, axis=-1, keepdims=True)
    mean_cross = jnp.mean(grad_normed * normed, axis=-1, keepdims=True)
    return inverse * (grad_normed - mean_grad - normed * mean_cross)


def weight_grad(left, right):
    return lax.dot_general(
        left, right, (((0,), (0,)), ((), ())), preferred_element_type=jnp.float32
    )


def back_product(left, right):
    return lax.dot_general(
        left, right, (((1,), (1,)), ((), ())), preferred_element_type=jnp.float32
    )


def gelu_exact(inputs):
    return jax.nn.gelu(inputs, approximate=False)


def column_sum(matrix):
    return jnp.sum(matrix.astype(jnp.float32), axis=0)


def local_plain(
    tokens,
    prev_logits,
    teacher,
    lengths,
    w_query,
    w_key,
    w_value,
    w_output,
    w_inner,
    w_outer,
    bias_query,
    bias_value,
    bias_output,
    attn_gain,
    attn_shift,
    inner_bias,
    outer_bias,
    ffn_gain,
    ffn_shift,
):
    f32 = jnp.float32
    bf16 = jnp.bfloat16
    ctx_size = lax.axis_size("ctx")
    ctx_rank = lax.axis_index("ctx")
    dp_size = lax.axis_size("dp")
    groups = tokens.shape[0]
    block_len = tokens.shape[3]
    model_width = tokens.shape[4]
    head_count = prev_logits.shape[1]
    seq_len = prev_logits.shape[-1]
    head_dim = model_width // head_count
    local_rows = 2 * block_len
    total_rows = groups * local_rows
    score_scale = head_dim ** (-0.5)
    (
        query_matrix,
        key_matrix,
        value_matrix,
        output_matrix,
        query_add,
        value_add,
        output_add,
        first_gain,
        first_shift,
    ) = (
        lax.all_gather(w_query, "dp", axis=0, tiled=True),
        lax.all_gather(w_key, "dp", axis=0, tiled=True),
        lax.all_gather(w_value, "dp", axis=0, tiled=True),
        lax.all_gather(w_output, "dp", axis=0, tiled=True),
        lax.all_gather(bias_query, "dp", axis=0, tiled=True),
        lax.all_gather(bias_value, "dp", axis=0, tiled=True),
        lax.all_gather(bias_output, "dp", axis=0, tiled=True),
        lax.all_gather(attn_gain, "dp", axis=0, tiled=True),
        lax.all_gather(attn_shift, "dp", axis=0, tiled=True),
    )
    token_rows = tokens.reshape(total_rows, model_width)
    queries = (
        jnp.dot(token_rows, query_matrix, preferred_element_type=f32) + query_add.astype(f32)
    ).astype(bf16)
    key_rows = jnp.dot(token_rows, key_matrix, preferred_element_type=f32).astype(bf16)
    values = (
        jnp.dot(token_rows, value_matrix, preferred_element_type=f32) + value_add.astype(f32)
    ).astype(bf16)
    key_blocks, value_blocks = (
        lax.all_gather(
            key_rows.reshape(groups, 2, 1, block_len, model_width), "ctx", axis=2, tiled=True
        ),
        lax.all_gather(
            values.reshape(groups, 2, 1, block_len, model_width), "ctx", axis=2, tiled=True
        ),
    )
    inner_matrix, outer_matrix, inner_add, outer_add, second_gain, second_shift = (
        lax.all_gather(w_inner, "dp", axis=0, tiled=True),
        lax.all_gather(w_outer, "dp", axis=0, tiled=True),
        lax.all_gather(inner_bias, "dp", axis=0, tiled=True),
        lax.all_gather(outer_bias, "dp", axis=0, tiled=True),
        lax.all_gather(ffn_gain, "dp", axis=0, tiled=True),
        lax.all_gather(ffn_shift, "dp", axis=0, tiled=True),
    )
    front_pos, back_pos = layout_positions(block_len, ctx_size, ctx_rank)
    query_pos = jnp.stack([front_pos, back_pos]).reshape(local_rows)
    key_front, key_back = layout_positions(
        block_len, ctx_size, jnp.arange(ctx_size, dtype=jnp.int32)[:, None]
    )
    key_pos = jnp.stack([key_front, key_back]).reshape(seq_len)
    allowed = (key_pos[None, None, :] <= query_pos[None, :, None]) & (
        key_pos[None, None, :] < lengths[:, None, None]
    )
    valid_rows = (query_pos[None, :] < lengths[:, None]).astype(f32).reshape(total_rows)
    query_heads = queries.reshape(groups, local_rows, head_count, head_dim).transpose(2, 0, 1, 3)
    key_heads = key_blocks.reshape(groups, seq_len, head_count, head_dim).transpose(2, 0, 1, 3)
    value_heads = value_blocks.reshape(groups, seq_len, head_count, head_dim).transpose(2, 0, 1, 3)
    prev_rows = prev_logits.reshape(groups, head_count, local_rows, seq_len)

    def scores_of(head_id):
        raw_scores = (
            jnp.einsum(
                "grd,gkd->grk", query_heads[head_id], key_heads[head_id], preferred_element_type=f32
            )
            * score_scale
        )
        raw_scores = raw_scores + lax.dynamic_index_in_dim(
            prev_rows, head_id, 1, keepdims=False
        ).astype(f32)
        return (raw_scores, jnp.where(allowed, raw_scores, NEG_BIG))

    def attend(head_id):
        raw_scores, masked = scores_of(head_id)
        row_max = jnp.max(masked, axis=-1, keepdims=True)
        exponent = jnp.exp(masked - row_max)
        row_total = jnp.sum(exponent, axis=-1, keepdims=True)
        probability = (exponent / row_total).astype(bf16)
        mixed_part = jnp.einsum(
            "grk,gkd->grd", probability, value_heads[head_id], preferred_element_type=f32
        )
        return (mixed_part, row_max[..., 0] + jnp.log(row_total[..., 0]), raw_scores.astype(bf16))

    mixed_heads, log_totals, raw_heads = lax.map(attend, jnp.arange(head_count))
    raw_logits = jnp.moveaxis(raw_heads, 0, 1).reshape(prev_logits.shape)
    mixed_rows = mixed_heads.transpose(1, 2, 0, 3).reshape(total_rows, model_width).astype(bf16)
    attn_out = jnp.dot(mixed_rows, output_matrix, preferred_element_type=f32) + output_add.astype(
        f32
    )
    first_normed, first_inverse = norm_forward(token_rows.astype(f32) + attn_out)
    first = first_normed * first_gain.astype(f32) + first_shift.astype(f32)
    first_low = first.astype(bf16)
    inner_pre = jnp.dot(first_low, inner_matrix, preferred_element_type=f32) + inner_add.astype(f32)
    active, gelu_back = jax.vjp(gelu_exact, inner_pre)
    active_low = active.astype(bf16)
    outer_pre = jnp.dot(active_low, outer_matrix, preferred_element_type=f32) + outer_add.astype(
        f32
    )
    second_normed, second_inverse = norm_forward(first + outer_pre)
    result = second_normed * second_gain.astype(f32) + second_shift.astype(f32)
    errors = (result - teacher.reshape(total_rows, model_width).astype(f32)) * valid_rows[:, None]
    square_sum, valid_total = lax.psum(
        (jnp.sum(errors * errors), jnp.sum(valid_rows)), ("dp", "ctx")
    )
    loss_value = square_sum / (valid_total * model_width)
    loss_scale = dp_size * groups * seq_len * model_width / 2.0
    grad_result = errors * (loss_scale * 2.0 / (valid_total * model_width))
    grad_second_gain = jnp.sum(grad_result * second_normed, axis=0)
    grad_second_shift = jnp.sum(grad_result, axis=0)
    grad_sum_two = norm_backward(
        grad_result * second_gain.astype(f32), second_normed, second_inverse
    )
    grad_outer = grad_sum_two.astype(bf16)
    grad_outer_matrix = weight_grad(active_low, grad_outer)
    grad_outer_add = column_sum(grad_outer)
    grad_active = back_product(grad_outer, outer_matrix)
    grad_inner = gelu_back(grad_active)[0].astype(bf16)
    grad_inner_matrix = weight_grad(first_low, grad_inner)
    grad_inner_add = column_sum(grad_inner)
    grad_first = grad_sum_two + back_product(grad_inner, inner_matrix)
    grad_first_gain = jnp.sum(grad_first * first_normed, axis=0)
    grad_first_shift = jnp.sum(grad_first, axis=0)
    grad_sum_one = norm_backward(grad_first * first_gain.astype(f32), first_normed, first_inverse)
    grad_attn = grad_sum_one.astype(bf16)
    grad_output_matrix = weight_grad(mixed_rows, grad_attn)
    grad_output_add = column_sum(grad_attn)
    grad_mixed = back_product(grad_attn, output_matrix).astype(bf16)
    grad_mixed_heads = grad_mixed.reshape(groups, local_rows, head_count, head_dim).transpose(
        2, 0, 1, 3
    )

    def attend_back(head_id):
        _, masked = scores_of(head_id)
        probability = jnp.exp(masked - log_totals[head_id][..., None])
        grad_part = grad_mixed_heads[head_id]
        grad_value_part = jnp.einsum(
            "grk,grd->gkd", probability.astype(bf16), grad_part, preferred_element_type=f32
        )
        grad_probs = jnp.einsum(
            "grd,gkd->grk", grad_part, value_heads[head_id], preferred_element_type=f32
        )
        row_dot = jnp.sum(probability * grad_probs, axis=-1, keepdims=True)
        grad_scores = (probability * (grad_probs - row_dot)).astype(bf16)
        grad_query_part = (
            jnp.einsum("grk,gkd->grd", grad_scores, key_heads[head_id], preferred_element_type=f32)
            * score_scale
        )
        grad_key_part = (
            jnp.einsum(
                "grk,grd->gkd", grad_scores, query_heads[head_id], preferred_element_type=f32
            )
            * score_scale
        )
        return (grad_scores, grad_query_part, grad_key_part, grad_value_part)

    grad_score_heads, grad_query_heads, grad_key_heads, grad_value_heads = lax.map(
        attend_back, jnp.arange(head_count)
    )
    grad_logits = jnp.moveaxis(grad_score_heads, 0, 1).reshape(prev_logits.shape)
    grad_queries = (
        grad_query_heads.transpose(1, 2, 0, 3).reshape(total_rows, model_width).astype(bf16)
    )
    key_terms = grad_key_heads.transpose(1, 2, 0, 3).reshape(
        groups, 2, ctx_size, block_len, model_width
    )
    value_terms = grad_value_heads.transpose(1, 2, 0, 3).reshape(
        groups, 2, ctx_size, block_len, model_width
    )
    key_sums, value_sums = (
        lax.psum_scatter(
            key_terms.astype(jnp.bfloat16), "ctx", scatter_dimension=2, tiled=True
        ).astype(jnp.float32),
        lax.psum_scatter(
            value_terms.astype(jnp.bfloat16), "ctx", scatter_dimension=2, tiled=True
        ).astype(jnp.float32),
    )
    grad_keys = key_sums.reshape(total_rows, model_width).astype(bf16)
    grad_values = value_sums.reshape(total_rows, model_width).astype(bf16)
    grad_query_matrix = weight_grad(token_rows, grad_queries)
    grad_key_matrix = weight_grad(token_rows, grad_keys)
    grad_value_matrix = weight_grad(token_rows, grad_values)
    grad_query_add = column_sum(grad_queries)
    grad_value_add = column_sum(grad_values)
    grad_token_rows = (
        grad_sum_one
        + back_product(grad_queries, query_matrix)
        + back_product(grad_keys, key_matrix)
        + back_product(grad_values, value_matrix)
    )
    matrix_grads = (
        grad_query_matrix,
        grad_key_matrix,
        grad_value_matrix,
        grad_output_matrix,
        grad_inner_matrix,
        grad_outer_matrix,
    )
    vector_grads = (
        grad_query_add,
        grad_value_add,
        grad_output_add,
        grad_first_gain,
        grad_first_shift,
        grad_inner_add,
        grad_outer_add,
        grad_second_gain,
        grad_second_shift,
    )
    summed = (
        lax.psum_scatter(
            matrix_grads[0].astype(jnp.bfloat16), "dp", scatter_dimension=0, tiled=True
        ).astype(jnp.float32),
        lax.psum_scatter(
            matrix_grads[1].astype(jnp.bfloat16), "dp", scatter_dimension=0, tiled=True
        ).astype(jnp.float32),
        lax.psum_scatter(
            matrix_grads[2].astype(jnp.bfloat16), "dp", scatter_dimension=0, tiled=True
        ).astype(jnp.float32),
        lax.psum_scatter(
            matrix_grads[3].astype(jnp.bfloat16), "dp", scatter_dimension=0, tiled=True
        ).astype(jnp.float32),
        lax.psum_scatter(
            matrix_grads[4].astype(jnp.bfloat16), "dp", scatter_dimension=0, tiled=True
        ).astype(jnp.float32),
        lax.psum_scatter(
            matrix_grads[5].astype(jnp.bfloat16), "dp", scatter_dimension=0, tiled=True
        ).astype(jnp.float32),
        lax.psum_scatter(
            vector_grads[0].astype(jnp.bfloat16), "dp", scatter_dimension=0, tiled=True
        ).astype(jnp.float32),
        lax.psum_scatter(
            vector_grads[1].astype(jnp.bfloat16), "dp", scatter_dimension=0, tiled=True
        ).astype(jnp.float32),
        lax.psum_scatter(
            vector_grads[2].astype(jnp.bfloat16), "dp", scatter_dimension=0, tiled=True
        ).astype(jnp.float32),
        lax.psum_scatter(
            vector_grads[3].astype(jnp.bfloat16), "dp", scatter_dimension=0, tiled=True
        ).astype(jnp.float32),
        lax.psum_scatter(
            vector_grads[4].astype(jnp.bfloat16), "dp", scatter_dimension=0, tiled=True
        ).astype(jnp.float32),
        lax.psum_scatter(
            vector_grads[5].astype(jnp.bfloat16), "dp", scatter_dimension=0, tiled=True
        ).astype(jnp.float32),
        lax.psum_scatter(
            vector_grads[6].astype(jnp.bfloat16), "dp", scatter_dimension=0, tiled=True
        ).astype(jnp.float32),
        lax.psum_scatter(
            vector_grads[7].astype(jnp.bfloat16), "dp", scatter_dimension=0, tiled=True
        ).astype(jnp.float32),
        lax.psum_scatter(
            vector_grads[8].astype(jnp.bfloat16), "dp", scatter_dimension=0, tiled=True
        ).astype(jnp.float32),
    )
    reduced = (
        lax.psum(summed[0].astype(jnp.bfloat16), "ctx").astype(jnp.float32),
        lax.psum(summed[1].astype(jnp.bfloat16), "ctx").astype(jnp.float32),
        lax.psum(summed[2].astype(jnp.bfloat16), "ctx").astype(jnp.float32),
        lax.psum(summed[3].astype(jnp.bfloat16), "ctx").astype(jnp.float32),
        lax.psum(summed[4].astype(jnp.bfloat16), "ctx").astype(jnp.float32),
        lax.psum(summed[5].astype(jnp.bfloat16), "ctx").astype(jnp.float32),
        lax.psum(summed[6].astype(jnp.bfloat16), "ctx").astype(jnp.float32),
        lax.psum(summed[7].astype(jnp.bfloat16), "ctx").astype(jnp.float32),
        lax.psum(summed[8].astype(jnp.bfloat16), "ctx").astype(jnp.float32),
        lax.psum(summed[9].astype(jnp.bfloat16), "ctx").astype(jnp.float32),
        lax.psum(summed[10].astype(jnp.bfloat16), "ctx").astype(jnp.float32),
        lax.psum(summed[11].astype(jnp.bfloat16), "ctx").astype(jnp.float32),
        lax.psum(summed[12].astype(jnp.bfloat16), "ctx").astype(jnp.float32),
        lax.psum(summed[13].astype(jnp.bfloat16), "ctx").astype(jnp.float32),
        lax.psum(summed[14].astype(jnp.bfloat16), "ctx").astype(jnp.float32),
    )
    return (
        result.astype(bf16).reshape(tokens.shape),
        raw_logits,
        loss_value,
        grad_token_rows.astype(bf16).reshape(tokens.shape),
        grad_logits,
        reduced[0],
        reduced[1],
        reduced[2],
        reduced[3],
        reduced[4],
        reduced[5],
        reduced[6],
        reduced[7],
        reduced[8],
        reduced[9],
        reduced[10],
        reduced[11],
        reduced[12],
        reduced[13],
        reduced[14],
    )


def local_fast(tokens, prev_logits, teacher, lengths, *parameters):
    weights, vectors = parameters[:6], parameters[6:]
    w_outer = weights[5]
    ctx_size = lax.axis_size("ctx")
    core = lax.axis_index("ctx")
    dp_size = lax.axis_size("dp")
    dp_rank = lax.axis_index("dp")
    block_len, width = tokens.shape[3], tokens.shape[4]
    head_count, seq_len = prev_logits.shape[1], prev_logits.shape[-1]
    head_dim = width // head_count
    rows = 2 * block_len
    shard = weights[0].shape[0]
    half = width // 2
    units = weights[4].shape[1] // width
    info = jnp.stack([core, dp_rank % 4, lengths[0], dp_rank // 4]).astype(jnp.int32)
    token_rows = tokens.reshape(rows, width)
    teacher_rows = teacher.reshape(rows, width)
    prev_rows = prev_logits.reshape(head_count, rows, seq_len)
    sizes = (block_len, ctx_size, head_dim)
    pairs = [(i, i) for i in range(head_count * head_dim // LANES)]
    (long_at,) = [i for i, v in enumerate(vectors) if v.shape[0] != shard]
    names = ("bq", "bv", "bo", "gain_one", "shift_one", "long", "b_outer", "gain_two", "shift_two", "count")
    rows_at = {name: i for i, name in enumerate(names)}
    rows_at["scale"] = float(dp_size * seq_len * width)

    chunk_a, chunk_c, chunk_d, chunk_e = pack(info, weights, vectors)
    cut_c, cut_d = split_row(chunk_c.shape[0]), split_row(chunk_d.shape[0])
    rows_at.update(
        rows_c=chunk_c.shape[0], cut_c=cut_c, cut_d=cut_d, deep_d=w_outer.shape[0] - chunk_e.shape[0]
    )
    cross = lambda piece: flip(piece, "ctx", 1)
    parts_a = z_triple(chunk_a)
    parts_e = [chunk_e] + [flip(chunk_e, "dp", step) for step in (1, 2, 3)]
    parts_a, parts_e, token_rows, chunk_c, chunk_d = together(
        parts_a, parts_e, token_rows, chunk_c, chunk_d
    )
    column_a = in_order(dp_rank // 4, parts_a)
    sides_a = side_columns(column_a)
    next_c = flip(chunk_c, "dp", 4)
    other_rows = cross(token_rows)
    pair_c = z_pair(chunk_c, next_c)
    over_c = flip(pair_c, "dp", 8)
    sides_a, other_rows, over_c, chunk_d = together(sides_a, other_rows, over_c, chunk_d)
    corner_a = corner_column(sides_a)
    own_a = [column_a, *sides_a]
    oth_a = [cross(piece) for piece in own_a]
    next_d = flip(chunk_d, "dp", 4)
    corner_a, oth_a, next_d, parts_e = together(corner_a, oth_a, next_d, parts_e)
    oth_a = [*oth_a, *[cross(piece) for piece in corner_a]]
    own_a = [*own_a, *corner_a]
    column_c = z_column(pair_c, over_c)
    sides_c = side_columns(column_c)
    pair_d = z_pair(chunk_d, next_d)
    over_d = flip(pair_d, "dp", 8)
    plane_e = in_order(dp_rank % 4, parts_e)
    next_e = flip(plane_e, "dp", 4)
    oth_e = [cross(plane_e)]
    queries, keys, values, w_attn, table, long_table = project(
        info, token_rows, other_rows, own_a, oth_a, block_len, vectors[long_at].shape[0]
    )
    queries, sides_c, pair_d, over_d, plane_e, next_e, oth_e = together(
        queries, sides_c, pair_d, over_d, plane_e, next_e, oth_e
    )
    column_d = z_column(pair_d, over_d)
    far_up = flip(jnp.concatenate([sides_c[0][:, :cut_c], column_d], axis=1), "dp", 2)
    near_low = flip(jnp.concatenate([sides_c[1][:, cut_c:], column_d], axis=1), "dp", 1)
    over_e = [flip(plane_e, "dp", 8)]
    oth_c = [cross(column_c), cross(sides_c[0])]
    qkv = (queries, keys, values)
    carry = attend(info, qkv, prev_rows, pairs[:4], None, *sizes)
    carry, oth_c, column_d, far_up, near_low, over_e = together(
        carry, oth_c, column_d, far_up, near_low, over_e
    )
    near_d = near_low[:, chunk_c.shape[0] - cut_c :]
    far_d = far_up[:, cut_c:]
    corner_d = [flip(near_d[:, :cut_d], "dp", 2), flip(far_d[:, cut_d:], "dp", 1)]
    over_e.append(flip(next_e, "dp", 8))
    late = [far_up, near_low]
    oth_late = [cross(piece) for piece in late]
    logits, probs, mixed = attend(info, qkv, prev_rows, pairs[4:], carry, *sizes)
    mixed, oth_c, oth_late, corner_d, over_e, column_d, next_e, sides_c = together(
        mixed, oth_c, oth_late, corner_d, over_e, column_d, next_e, sides_c
    )
    own_c = [column_c, *sides_c, far_up, near_low]
    own_d = [column_d, *corner_d, plane_e, next_e, *over_e]
    oth_c += [cross(sides_c[1]), *oth_late]
    oth_d = [cross(piece) for piece in own_d[:3]] + oth_e + [cross(piece) for piece in own_d[4:]]
    result, grad_sum_one, grad_mixed, square, *terms = feed(
        info, mixed, token_rows, teacher_rows, table, long_table,
        [*own_c, *own_d], [*oth_c, *oth_d], rows_at, ctx_size,
    )

    back = lambda some, carry: attend_back(qkv, probs, grad_mixed, some, carry, *sizes)
    kept_d, sent_d, kept_c, sent_c = terms[:2], terms[2:4], terms[4:6], terms[6:8]
    came_d = [cross(sent_d[0])]
    square = square + cross(square)
    sent_d, sent_c, square, came_d, grad_mixed = together(sent_d, sent_c, square, came_d, grad_mixed)
    corner_d = scatter_corner(kept_d[0], came_d[0])
    came_d.append(cross(sent_d[1]))
    came_c = [cross(part) for part in sent_c]
    grads = back(pairs[:2], [])
    grads, corner_d, came_d, came_c, square = together(grads, corner_d, came_d, came_c, square)
    sides_d = send_sides(scatter_sides(kept_d[1], came_d[1], corner_d))
    corner_c = scatter_corner(kept_c[0], came_c[0])
    square = square + flip(square, "dp", 8)
    grad_logits, gq, gk, gv = back(pairs[2:], grads)
    gk, gv = [g.reshape(2, 2, block_len, width) for g in (gk, gv)]
    gq, sides_d, corner_c, square = together(gq, sides_d, corner_c, square)
    sides_c = scatter_sides(kept_c[1], came_c[1], corner_c)
    half_d = scatter_half(kept_d[1], came_d[1], sides_d)
    sides_c, half_d, gq = together(sides_c, half_d, gq)
    sides_c, half_d = send_sides(sides_c), (half_d[0], flip(half_d[1], "dp", 8))
    own_terms, sent_terms, *terms_a = token_back(
        info, token_rows, other_rows, gq, gk, gv, grad_sum_one, w_attn
    )
    own_terms, sent_terms, terms_a, sides_c, half_d = together(
        own_terms, sent_terms, terms_a, sides_c, half_d
    )
    kept_a, sent_a = terms_a[:2], terms_a[2:4]
    came_a = [cross(part) for part in sent_a]
    corner_a = scatter_corner(kept_a[0], came_a[0])
    half_c = scatter_half(kept_c[1], came_c[1], sides_c)
    half_c = (half_c[0], flip(half_c[1], "dp", 8))
    rank_d = scatter_rank(*half_d)
    corner_a, rank_d, sent_terms = together(corner_a, rank_d, sent_terms)
    sides_a = send_sides(scatter_sides(kept_a[1], came_a[1], corner_a))
    grad_tokens = (own_terms + cross(sent_terms).astype(f32)).astype(bf16)
    sides_a, half_c, square, grad_tokens = together(sides_a, half_c, square, grad_tokens)
    half_a = scatter_half(kept_a[1], came_a[1], sides_a)
    half_a = (half_a[0], flip(half_a[1], "dp", 8))
    rank_c = scatter_rank(*half_c)
    total_d = scatter_total(*rank_d)
    square = square + flip(square, "dp", 1)
    square = square + flip(square, "dp", 2)
    half_a, rank_c, square, total_d = together(half_a, rank_c, square, total_d)
    rank_a = scatter_rank(*half_a)
    total_c = scatter_total(*rank_c)
    square = square + flip(square, "dp", 4)
    total_a = scatter_total(*rank_a)
    pair_a, pair_c, pair_d = by_halves(*total_a), by_halves(*total_c), by_halves(*total_d)
    def unit(parts, index):
        return [part[index * shard : (index + 1) * shard] for part in parts]

    grad_w_inner = jnp.concatenate(
        [unit(pair_c[side : side + 1], i)[0] for side in range(2) for i in range(units)], axis=1
    )
    sums_c, sums_a = total_c[0][(units + 1) * shard :].astype(f32), total_a[0][3 * shard :].astype(f32)
    order = (6, 4, 5, None, 2, 0, 1)
    vector_totals = [sums_a[0, :shard], sums_a[1, :shard]]
    vector_totals += [
        sums_c[7, : vectors[long_at].shape[0]] if i is None else sums_c[i, :shard] for i in order
    ]
    return (
        result.reshape(tokens.shape),
        logits.reshape(prev_logits.shape),
        square[0, 0],
        grad_tokens.reshape(tokens.shape),
        grad_logits.reshape(prev_logits.shape),
        *[jnp.concatenate(unit(pair_a, i), axis=1) for i in range(3)],
        jnp.concatenate(unit(pair_c, units), axis=1),
        grad_w_inner,
        jnp.concatenate(pair_d, axis=1),
        *vector_totals,
    )


def local(tokens, prev_logits, teacher, lengths, *parameters):
    width, shard = tokens.shape[-1], parameters[0].shape[0]
    fits = (
        lax.axis_size("dp") == 16
        and lax.axis_size("ctx") == 2
        and tokens.shape[0] == 1
        and shard % 16 == 0
        and width % 256 == 0
    )
    chosen = local_fast if fits else local_plain
    return chosen(tokens, prev_logits, teacher, lengths, *parameters)


def solution(mesh):
    rows = P("dp", None, "ctx", None, None)
    scores = P("dp", None, None, "ctx", None, None)
    matrix, vector = P("dp", None), P("dp")
    return jax.shard_map(
        local,
        mesh=mesh,
        in_specs=(rows, scores, rows, vector) + (matrix,) * 6 + (vector,) * 9,
        out_specs=(rows, scores, P(), rows, scores) + (matrix,) * 6 + (vector,) * 9,
        check_vma=False,
    )
```

```python
import functools

import jax
import jax.numpy as jnp
from jax import lax
from jax.experimental import pallas as pl
from jax.experimental.pallas import tpu as pltpu
from jax.sharding import PartitionSpec as P

EPSILON = 1e-05
NEG_BIG = -1e30
POS_BIG = 3.0e38
LANES = 128
f32 = jnp.float32
bf16 = jnp.bfloat16
ANY = pl.BlockSpec(memory_space=pl.ANY)


def mm(left, right):
    return jnp.dot(left, right, preferred_element_type=f32)


def mm_tn(left, right):
    return lax.dot_general(left, right, (((0,), (0,)), ((), ())), preferred_element_type=f32)


def mm_nt(left, right):
    return lax.dot_general(left, right, (((1,), (1,)), ((), ())), preferred_element_type=f32)


def struct(shape, dtype):
    return jax.ShapeDtypeStruct(shape, dtype)


def params():
    return pltpu.CompilerParams(vmem_limit_bytes=56 << 20)


def cost(flops, bytes_accessed, transcendentals=0):
    return pl.CostEstimate(
        flops=int(flops), bytes_accessed=int(bytes_accessed), transcendentals=int(transcendentals)
    )


def together(*values):
    return lax.optimization_barrier(values)


def after(value, *others):
    return lax.optimization_barrier((value, others))[0]


def whole_block(array):
    rank = len(array.shape)
    return pl.BlockSpec(array.shape, lambda *_: (0,) * rank)


def side_lanes(info, side, width):
    half = info[0] if side == 0 else 1 - info[0]
    return pl.ds(pl.multiple_of(half * width, LANES), width)


def flip(array, axis_name, bit):
    size = lax.axis_size(axis_name)
    return lax.ppermute(array, axis_name, [(i, i ^ bit) for i in range(size)])


def z_bits():
    dp_rank = lax.axis_index("dp")
    return dp_rank // 4 % 2, dp_rank // 8


def z_pair(array, arrived):
    low = z_bits()[0] == 0
    return jnp.stack([jnp.where(low, array, arrived), jnp.where(low, arrived, array)])


def z_column(pair, arrived):
    low = z_bits()[1] == 0
    return jnp.concatenate([jnp.where(low, pair, arrived), jnp.where(low, arrived, pair)])


def z_triple(array):
    return [array] + [flip(array, "dp", 4 * step) for step in (1, 2, 3)]


def in_order(mine, parts):
    return jnp.stack([lax.select_n(mine ^ i, *parts) for i in range(4)])


def side_columns(column):
    return flip(column, "dp", 1), flip(column, "dp", 2)


def corner_column(sides):
    cut = split_row(sides[0].shape[1])
    return flip(sides[0][:, :cut], "dp", 2), flip(sides[1][:, cut:], "dp", 1)


def split_row(rows):
    return rows // 32 * 16


def scatter_corner(kept, arrived):
    cut = split_row(kept.shape[1])
    term = (kept.astype(f32) + arrived.astype(f32)).astype(bf16)
    return flip(term[:, :cut], "dp", 2), flip(term[:, cut:], "dp", 1)


def scatter_sides(kept, arrived, corner):
    upper, lower = [part.astype(f32) for part in corner]
    near = kept[0].astype(f32) + arrived[0].astype(f32)
    far = kept[1].astype(f32) + arrived[1].astype(f32)
    cut = upper.shape[1]
    near = jnp.concatenate([near[:, :cut] + upper, near[:, cut:]], axis=1)
    far = jnp.concatenate([far[:, :cut], far[:, cut:] + lower], axis=1)
    return near.astype(bf16), far.astype(bf16)


def send_sides(sides):
    return flip(sides[0], "dp", 1), flip(sides[1], "dp", 2)


def scatter_half(kept, arrived, sides):
    column = sum(part.astype(f32) for part in (kept[2], arrived[2], *sides))
    column = column.reshape(2, 2, *column.shape[1:])
    high = z_bits()[1]
    pick = lambda half: lax.dynamic_index_in_dim(column, half, 0, keepdims=False)
    return pick(high), pick(1 - high).astype(bf16)


def scatter_rank(kept, arrived):
    column = kept + arrived.astype(f32)
    low = z_bits()[0]
    pick = lambda half: lax.dynamic_index_in_dim(column, half, 0, keepdims=False)
    return pick(low), flip(pick(1 - low).astype(bf16), "dp", 4)


def scatter_triple(kept, arrived, sides):
    mine = lax.axis_index("dp") // 4
    column = sum(part.astype(f32) for part in (kept[2], arrived[2], *sides))
    pick = lambda z: lax.dynamic_index_in_dim(column, z, 0, keepdims=False)
    return pick(mine), [flip(pick(mine ^ step).astype(bf16), "dp", 4 * step) for step in (2, 3, 1)]


def scatter_total(kept, arrived):
    total = kept
    for part in arrived:
        total = total + part.astype(f32)
    total = total.astype(bf16)
    return total, flip(total, "ctx", 1)


def by_halves(total, across):
    core = lax.axis_index("ctx")
    return (
        jnp.where(core == 0, total, across).astype(f32),
        jnp.where(core == 0, across, total).astype(f32),
    )


def pack_kernel(info, *refs):
    vectors, outs = refs[6:-4], refs[-4:]
    half = outs[0].shape[1]
    shard = refs[0].shape[0]
    units = refs[4].shape[1] // (2 * half)
    lanes = side_lanes(info, 0, half)

    def unit(index):
        column = pl.multiple_of((info[0] * units + index) * half, LANES)
        return refs[4][:, pl.ds(column, half)]

    for index in range(3):
        outs[0][index * shard : (index + 1) * shard, :] = refs[index][:, lanes]
    count = units // 2
    for index in range(count):
        rows = slice(index * shard, (index + 1) * shard)
        outs[1][rows, :] = unit(index)
        outs[2][rows, :] = unit(count + index)
    outs[1][count * shard :, :] = refs[3][:, lanes]
    split = refs[5].shape[0] - outs[3].shape[0]
    outs[2][count * shard :, :] = refs[5][:split, lanes]
    outs[3][...] = refs[5][split:, lanes]
    row = lax.broadcasted_iota(jnp.int32, (16, half), 0)
    table = jnp.zeros((16, half), f32)
    for index, ref in enumerate(vectors):
        value = jnp.pad(ref[...].astype(f32), ((0, 0), (0, half - ref.shape[1])))
        table = jnp.where(row == index, value, table)
    table = jnp.where(row == len(vectors), (info[2] // 32).astype(f32), table)
    table = jnp.where(row == len(vectors) + 1, (info[2] % 32).astype(f32), table)
    outs[0][3 * shard :, :] = table.astype(bf16)


def pack(info, weights, vectors):
    shard, width = weights[0].shape
    half, count = width // 2, weights[4].shape[1] // width // 2
    deep = weights[5].shape[0]
    split = deep // 32 * 16
    sizes = (3 * shard + 16, (count + 1) * shard, count * shard + split, deep - split)
    shapes = [struct((size, half), bf16) for size in sizes]
    args = [*weights, *[v[None] for v in vectors]]
    return pl.pallas_call(
        pack_kernel,
        out_shape=shapes,
        grid_spec=pltpu.PrefetchScalarGridSpec(
            num_scalar_prefetch=1,
            grid=(1,),
            in_specs=[whole_block(a) for a in args],
            out_specs=[whole_block(s) for s in shapes],
        ),
        compiler_params=params(),
        cost_estimate=cost(0, 4 * sum(w.size for w in weights)),
        name="pack",
    )(info, *args)


def piece_parts(pieces, cut, plane, start, rows):
    parts = []
    for offset in range(3):
        ref, base = pieces[offset]
        parts.append((ref.at[:, pl.ds(base + start, rows)], plane ^ (0, 1, 2)[offset], 0, rows))
    (upper, base_up), (lower, base_low) = pieces[3:]
    if start < cut:
        count = min(start + rows, cut) - start
        parts.append((upper.at[:, pl.ds(base_up + start, count)], plane ^ 3, 0, count))
    if start + rows > cut:
        skip = max(start, cut)
        count = start + rows - skip
        parts.append((lower.at[:, pl.ds(base_low + skip - cut, count)], plane ^ 3, skip - start, count))
    return parts


def slot_start(slot, ctx_size, block_len):
    half, which = divmod(slot, ctx_size)
    return (which if half == 0 else 2 * ctx_size - 1 - which) * block_len


def head_lanes(which, head_dim):
    lane = lax.broadcasted_iota(jnp.int32, (1, LANES), 1)
    return (lane >= which * head_dim) & (lane < (which + 1) * head_dim)


def attend_kernel(
    block_len, ctx_size, head_dim, info, q_ref, k_ref, v_ref, prev_ref, logit_ref, prob_ref, mix_ref, limit_ref
):
    seq_len = 2 * ctx_size * block_len
    half = ctx_size * block_len
    heads = LANES // head_dim

    @pl.when(pl.program_id(0) == 0)
    def _():
        core, length = info[0], info[2]
        within = lax.broadcasted_iota(jnp.int32, (block_len, block_len), 1)
        row = lax.broadcasted_iota(jnp.int32, (block_len, block_len), 0)
        for part in range(2):
            start = core if part == 0 else 2 * ctx_size - 1 - core
            query_pos = row + start * block_len
            for slot in range(2 * ctx_size):
                key_pos = within + slot_start(slot, ctx_size, block_len)
                allowed = (key_pos <= query_pos) & (key_pos < length)
                limit_ref[
                    part * block_len : (part + 1) * block_len,
                    slot * block_len : (slot + 1) * block_len,
                ] = jnp.where(allowed, POS_BIG, NEG_BIG)

    scale = head_dim ** (-0.5)
    masks = [head_lanes(which, head_dim) for which in range(heads)]
    values = [jnp.where(mask, v_ref[...], 0.0).astype(bf16) for mask in masks]
    scores = []
    for which in range(heads):
        query = jnp.where(masks[which], q_ref[...].astype(f32) * scale, 0.0).astype(bf16)
        scores.append(mm_nt(query, k_ref[...]))
    for part in range(2):
        rows = slice(part * block_len, (part + 1) * block_len)
        keys = half if part == 0 else seq_len
        probabilities = []
        for which in range(heads):
            raw = scores[which][rows, :] + prev_ref[which, rows, :].astype(f32)
            logit_ref[which, rows, :] = raw.astype(bf16)
            masked = jnp.minimum(raw[:, :keys], limit_ref[rows, :keys])
            top = jnp.max(masked, axis=-1, keepdims=True)
            exponent = jnp.exp(masked - top)
            total = jnp.sum(exponent, axis=-1, keepdims=True)
            probability = (exponent * (1.0 / total)).astype(bf16)
            prob_ref[which, rows, :keys] = probability
            probabilities.append(probability)
        mixed = mm(
            jnp.concatenate(probabilities, axis=1),
            jnp.concatenate([value[:keys] for value in values], axis=0),
        )
        mix_ref[rows, :] = mixed.astype(bf16)


def attend_back_kernel(
    block_len, ctx_size, head_dim, q_ref, k_ref, v_ref, prob_ref, gm_ref, gs_ref, gq_ref, gk_ref, gv_ref, gk_sum, gv_sum
):
    seq_len = 2 * ctx_size * block_len
    half = ctx_size * block_len
    heads = LANES // head_dim
    scale = head_dim ** (-0.5)
    masks = [head_lanes(which, head_dim) for which in range(heads)]
    keys_in = [jnp.where(mask, k_ref[...], 0.0).astype(bf16) for mask in masks]
    for part in (1, 0):
        rows = slice(part * block_len, (part + 1) * block_len)
        keys = half if part == 0 else seq_len
        grads, queries, probs, grad_mixes = [], [], [], []
        for which in range(heads):
            grad_mix = jnp.where(masks[which], gm_ref[rows, :], 0.0).astype(bf16)
            prob_low = prob_ref[which, rows, :keys]
            probability = prob_low.astype(f32)
            grad_prob = mm_nt(grad_mix, v_ref[:keys, :])
            term = probability * grad_prob
            row_dot = jnp.sum(term, axis=-1, keepdims=True)
            grad_score = (term - probability * row_dot).astype(bf16)
            gs_ref[which, rows, :keys] = grad_score
            if keys < seq_len:
                gs_ref[which, rows, keys:] = jnp.zeros((block_len, seq_len - keys), bf16)
            grads.append(grad_score)
            queries.append(jnp.where(masks[which], q_ref[rows, :], 0.0).astype(bf16))
            probs.append(prob_low)
            grad_mixes.append(grad_mix)
        grad_value = mm_tn(jnp.concatenate(probs, axis=0), jnp.concatenate(grad_mixes, axis=0))
        grad_key = mm_tn(jnp.concatenate(grads, axis=0), jnp.concatenate(queries, axis=0))
        if part == 1:
            gv_sum[...] = grad_value
            gk_sum[...] = grad_key
        else:
            gv_sum[:keys, :] += grad_value
            gk_sum[:keys, :] += grad_key
        grad_query = mm(
            jnp.concatenate(grads, axis=1), jnp.concatenate([key[:keys] for key in keys_in], axis=0)
        )
        gq_ref[rows, :] = (grad_query * scale).astype(bf16)
    gk_ref[...] = (gk_sum[...] * scale).astype(bf16)
    gv_ref[...] = gv_sum[...].astype(bf16)


def pair_specs(rows, seq_len, heads, places):
    def at(h, which):
        index = places[-1][which]
        for i in range(len(places) - 1):
            index = jnp.where(h == i, places[i][which], index)
        return index

    wide = pl.BlockSpec((heads, rows, seq_len), lambda h, *_: (at(h, 0), 0, 0))
    mixed = pl.BlockSpec((rows, LANES), lambda h, *_: (0, at(h, 0)))
    narrow = pl.BlockSpec((rows, LANES), lambda h, *_: (0, at(h, 1)))
    whole = pl.BlockSpec((seq_len, LANES), lambda h, *_: (0, at(h, 1)))
    return wide, mixed, narrow, whole


def attend(info, qkv, prev, places, carry, block_len, ctx_size, head_dim):
    head_count, rows, seq_len = prev.shape
    heads, count = LANES // head_dim, len(places)
    wide, mixed, narrow, whole = pair_specs(rows, seq_len, heads, places)
    kernel = functools.partial(attend_kernel, block_len, ctx_size, head_dim)
    given = () if carry is None else carry
    mixed_shape = struct((rows, head_count * head_dim), bf16)
    return pl.pallas_call(
        drop_refs(kernel, 5, len(given)),
        out_shape=(struct(prev.shape, bf16), struct(prev.shape, bf16), mixed_shape),
        grid_spec=pltpu.PrefetchScalarGridSpec(
            num_scalar_prefetch=1,
            grid=(count,),
            in_specs=[narrow, whole, whole, wide] + [ANY] * len(given),
            out_specs=[wide, wide, mixed],
            scratch_shapes=[pltpu.VMEM((rows, seq_len), f32)],
        ),
        input_output_aliases={5 + i: i for i in range(len(given))},
        compiler_params=params(),
        cost_estimate=cost(
            8 * rows * seq_len * LANES * heads * count,
            6 * rows * seq_len * heads * count,
            rows * seq_len * heads * count,
        ),
        name="attend",
    )(info, *qkv, prev, *given)


def drop_refs(kernel, start, count):
    def run(*refs):
        kernel(*refs[:start], *refs[start + count :])

    return run if count else kernel


def attend_back(qkv, probs, grad_mixed, places, carry, block_len, ctx_size, head_dim):
    head_count, rows, seq_len = probs.shape
    heads, count = LANES // head_dim, len(places)
    wide, mixed, narrow, whole = pair_specs(rows, seq_len, heads, places)
    kernel = functools.partial(attend_back_kernel, block_len, ctx_size, head_dim)
    given = tuple(carry)
    return pl.pallas_call(
        drop_refs(kernel, 5, len(given)),
        out_shape=[struct(probs.shape, bf16)] + [struct(a.shape, bf16) for a in qkv],
        grid=(count,),
        in_specs=[narrow, whole, whole, wide, mixed] + [ANY] * len(given),
        out_specs=[wide, narrow, whole, whole],
        scratch_shapes=[pltpu.VMEM((seq_len, LANES), f32), pltpu.VMEM((seq_len, LANES), f32)],
        input_output_aliases={5 + i: i for i in range(len(given))},
        compiler_params=params(),
        cost_estimate=cost(
            16 * rows * seq_len * LANES * heads * count, 4 * rows * seq_len * heads * count
        ),
        name="attend_back",
    )(*qkv, probs, grad_mixed, *given)


def by_sides(ref, info, width):
    return jnp.concatenate(
        [ref[:, side_lanes(info, 0, width)], ref[:, side_lanes(info, 1, width)]], axis=1
    )


def project_kernel(info, own_tok, oth_tok, *refs):
    own, oth = [[(ref, 0) for ref in refs[i : i + 5]] for i in (0, 5)]
    cut = split_row(refs[0].shape[1])
    q_ref, k_ref, v_ref, w, table_ref, long_ref, table, sem = refs[10:]
    core, plane = info[0], info[1]
    block_len = k_ref.shape[2]
    rows, width = own_tok.shape
    half, shard = width // 2, width // 16
    cuts = [slice(0, half), slice(half, width)]
    copies = []

    def copy(source, dest):
        copies.append(pltpu.make_async_copy(source, dest, sem.at[len(copies)]))
        copies[-1].start()

    for source, where, _, _ in piece_parts(own, cut, plane, 3 * shard, 16):
        copy(source, table.at[:, where])
    for unit in range(3):
        for side, pieces in enumerate((own, oth)):
            for source, where, first, count in piece_parts(pieces, cut, plane, unit * shard, shard):
                copy(source, w.at[unit, :, where, pl.ds(first, count), cuts[side]])
    for item in copies:
        item.wait()
    long_span = long_ref.shape[1] // 16
    for rank in range(16):
        piece = table[rank // 4, rank % 4].astype(f32)
        table_ref[:, rank * shard : (rank + 1) * shard] = piece[:, :shard]
        long_ref[:, rank * long_span : (rank + 1) * long_span] = piece[:, :long_span]
    weights = [w[unit].reshape(width, width) for unit in range(3)]
    tokens = jnp.concatenate([own_tok[...], oth_tok[...]], axis=0)
    lanes = [side_lanes(info, side, half) for side in range(2)]
    query = mm(own_tok[...], weights[0])
    for side in range(2):
        q_ref[:, lanes[side]] = (query[:, cuts[side]] + table_ref[0:1, lanes[side]]).astype(bf16)
    for out, weight, row in ((k_ref, weights[1], None), (v_ref, weights[2], 1)):
        value = mm(tokens, weight)
        for side in range(2):
            piece = value[:, cuts[side]]
            if row is not None:
                piece = piece + table_ref[row : row + 1, lanes[side]]
            piece = piece.astype(bf16)
            for index in range(4):
                where = core if index < 2 else 1 - core
                out[index % 2, where, :, lanes[side]] = piece[index * block_len : (index + 1) * block_len]


def project(info, own_tok, oth_tok, own, oth, block_len, long_size):
    rows, width = own_tok.shape
    shard = width // 16
    q_shape = struct((rows, width), bf16)
    k_shape = struct((2, 2, block_len, width), bf16)
    shapes = [
        q_shape,
        k_shape,
        k_shape,
        struct((3, 4, 4, shard, width), bf16),
        struct((16, width), f32),
        struct((16, 16 * long_size), f32),
    ]
    q, k, v, w, table, long = pl.pallas_call(
        project_kernel,
        out_shape=shapes,
        grid_spec=pltpu.PrefetchScalarGridSpec(
            num_scalar_prefetch=1,
            grid=(1,),
            in_specs=[whole_block(own_tok)] * 2 + [ANY] * 10,
            out_specs=[whole_block(s) for s in shapes],
            scratch_shapes=[
                pltpu.VMEM((4, 4, 16, width // 2), bf16),
                pltpu.SemaphoreType.DMA((40,)),
            ],
        ),
        compiler_params=params(),
        cost_estimate=cost(10 * rows * width * width, 20 * rows * width + 12 * width * width),
        name="project",
    )(info, own_tok, oth_tok, *own, *oth)
    w = w.reshape(3, width, width)
    return q, k.reshape(2 * rows, width), v.reshape(2 * rows, width), w, table, long


def normalize(total):
    center = total - jnp.mean(total, axis=-1, keepdims=True)
    inverse = lax.rsqrt(jnp.mean(center * center, axis=-1, keepdims=True) + EPSILON)
    return center * inverse, inverse


def normalize_back(grad, normed, inverse):
    mean_grad = jnp.mean(grad, axis=-1, keepdims=True)
    mean_cross = jnp.mean(grad * normed, axis=-1, keepdims=True)
    return inverse * (grad - mean_grad - normed * mean_cross)


def gelu_parts(value):
    size = jnp.abs(value)
    near = 1.0 / (1.0 + (0.3275911 * 0.7071067811865476) * size)
    series = 0.5 * 1.061405429
    for factor in (-1.453152027, 1.421413741, -0.284496736, 0.254829592):
        series = series * near + 0.5 * factor
    bell = jnp.exp2((-0.5 * 1.4426950408889634) * (value * value))
    tail = series * near * bell
    active = jnp.maximum(value, 0.0) - size * tail
    below = jnp.where(value >= 0.0, 1.0 - tail, tail)
    return active, below + value * (bell * 0.3989422804014327)


def put_table(stage, start, sums, count, long_row=None):
    shard = sums.shape[1] // 16
    cols = stage.shape[4]
    low = sums[0:8, :]
    row = lax.broadcasted_iota(jnp.int32, (16, cols), 0)
    for rank in range(16):
        part = low[:, rank * shard : (rank + 1) * shard]
        part = jnp.pad(part, ((0, 8), (0, cols - shard)))
        table = jnp.where(row < count, part, 0.0)
        if long_row is not None:
            at = long_row + rank // 4
            span = sums.shape[1] // 4
            long = sums[at : at + 1, rank % 4 * span : (rank % 4 + 1) * span]
            table = jnp.where(row == count, jnp.pad(long, ((0, 0), (0, cols - span))), table)
        table = table.astype(bf16)
        for side in range(2):
            stage[side, rank // 4, rank % 4, start : start + 16, :] = table


def term_slots(outs, side):
    first, rest = outs[2 * side : 2 * side + 2]
    return [first, rest.at[0], rest.at[1], rest.at[2]]


def chunk_pieces(refs, rows_at, which):
    if which == "c":
        return [(refs[0], 0), (refs[1], 0), (refs[2], 0), (refs[3], 0), (refs[4], 0)]
    low = rows_at["rows_c"] - rows_at["cut_c"]
    return [(refs[5], 0), (refs[4], low), (refs[3], rows_at["cut_c"]), (refs[6], 0), (refs[7], 0)]


def feed_kernel(
    ctx_size, rows_at, info, mix, tok, teacher, table, long_table, *refs
):
    count_in = 12
    own, oth = refs[:count_in], refs[count_in : 2 * count_in]
    (
    out_ref, gs_ref, gm_ref, *terms, wc, wd, act, slope, value_ref, first, norm, inv, low, acc, go, stage_d, stage_c, sum_ref, sem,
    ) = refs[2 * count_in :]
    square_ref, *terms = terms
    terms_d, terms_c = terms[:4], terms[4:]
    core, plane = info[0], info[1]
    b_inner = long_table.at[pl.ds(rows_at["long"], 1)]
    units, rows_all, width = act.shape
    half = width // 2
    shard = width // 16
    block_len = rows_all // 2
    tile = 64
    tiles = [slice(start, start + tile) for start in range(0, rows_all, tile)]
    lanes = [side_lanes(info, side, half) for side in range(2)]
    cuts = [slice(0, half), slice(half, width)]
    count = [0]

    def start(source, dest):
        copy = pltpu.make_async_copy(source, dest, sem.at[count[0]])
        count[0] += 1
        copy.start()
        return copy

    def wait(copies):
        for copy in copies:
            copy.wait()

    def vector(index):
        row = rows_at[index]
        return table[row : row + 1, :]

    def unit_rows(side, unit):
        where = core if side == 0 else 1 - core
        return pl.ds(pl.multiple_of((where * units + unit) * half, LANES), half)

    def unit_parts(pieces, unit):
        split = units // 2
        if split <= unit < units:
            return piece_parts(
                chunk_pieces(pieces, rows_at, "d"), rows_at["cut_d"], plane, (unit - split) * shard, shard
            )
        at = split if unit == units else unit
        return piece_parts(chunk_pieces(pieces, rows_at, "c"), rows_at["cut_c"], plane, at * shard, shard)

    load_c = {}
    for unit in [units] + list(range(units)):
        load_c[unit] = [
            start(source, wc.at[unit, :, where, pl.ds(first_row, rows), cuts[side]])
            for side, pieces in enumerate((own, oth))
            for source, where, first_row, rows in unit_parts(pieces, unit)
        ]
    deep_d = rows_at["deep_d"]
    load_d = [
        start(source, wd.at[:, where, pl.ds(first_row, rows), cuts[side]])
        for side, pieces in enumerate((own, oth))
        for source, where, first_row, rows in piece_parts(
            chunk_pieces(pieces, rows_at, "d"), rows_at["cut_d"], plane, units // 2 * shard, deep_d
        )
    ]
    rest = pl.ds(deep_d, wd.shape[2] - deep_d)
    for side, pieces in enumerate((own, oth)):
        layers = pieces[8:12]
        load_d += [start(ref, wd.at[info[3] ^ i, :, rest, cuts[side]]) for i, ref in enumerate(layers)]

    def outer_unit(unit):
        ranks = half // wd.shape[2]
        blocks = []
        for side in range(2):
            where = core if side == 0 else 1 - core
            for index in range(ranks):
                rank = (where * units + unit) * ranks + index
                blocks.append(wd[rank // 4, rank % 4])
        return jnp.concatenate(blocks, axis=0)

    wait(load_c[units])
    value = mm(mix[...], wc[units].reshape(width, width))
    for side in range(2):
        acc[:, lanes[side]] = value[:, cuts[side]]
    for rows in tiles:
        normed, inverse = normalize(tok[rows, :].astype(f32) + (acc[rows, :] + vector("bo")))
        total = normed * vector("gain_one") + vector("shift_one")
        norm[rows, :] = normed
        inv[rows, :] = jnp.broadcast_to(inverse, (tile, LANES))
        first[rows, :] = total
        low[rows, :] = total.astype(bf16)

    for unit in range(units + 1):
        if unit < units:
            wait(load_c[unit])
        for part in range(2):
            block = slice(part * block_len, (part + 1) * block_len)
            if unit < units:
                value = mm(low[block, :], wc[unit].reshape(width, width))
                for side in range(2):
                    where = core if side == 0 else 1 - core
                    column = pl.ds(pl.multiple_of((where * units + unit) * half, LANES), half)
                    value_ref[unit % 2, block, cuts[side]] = value[:, cuts[side]] + b_inner[:, column]
            if unit > 0:
                for rows in [slice(at, at + 32) for at in range(block.start, block.stop, 32)]:
                    active, steep = gelu_parts(value_ref[(unit - 1) % 2, rows, :])
                    act[unit - 1, rows, :] = active.astype(bf16)
                    slope[unit - 1, rows, :] = steep.astype(bf16)
    value = None
    wait(load_d)
    for unit in range(units):
        term = mm(act[unit], outer_unit(unit))
        value = term if value is None else value + term
    for side in range(2):
        acc[:, lanes[side]] = value[:, cuts[side]]

    valid_total = jnp.sum(
        vector("count") * 32.0 + table[rows_at["count"] + 1 : rows_at["count"] + 2, :], axis=-1, keepdims=True
    )
    factor = rows_at["scale"] * shard / (valid_total * width)
    sums = [jnp.zeros((8, width), f32) for _ in range(4)]
    for rows in tiles:
        part, inside = divmod(rows.start, block_len)
        base = (core if part == 0 else 2 * ctx_size - 1 - core) * block_len + inside
        position = lax.broadcasted_iota(jnp.int32, (tile, 1), 0) + base
        valid = (position < info[2]).astype(f32)
        normed, inverse = normalize(first[rows, :] + (acc[rows, :] + vector("b_outer")))
        result = normed * vector("gain_two") + vector("shift_two")
        out_ref[rows, :] = result.astype(bf16)
        error = (result - teacher[rows, :].astype(f32)) * valid
        grad_result = error * factor
        grad_sum = normalize_back(grad_result * vector("gain_two"), normed, inverse)
        grad_low = grad_sum.astype(bf16)
        acc[rows, :] = grad_sum
        go[rows, :] = grad_low
        terms = (grad_result * normed, grad_result, grad_low.astype(f32), error * error)
        for index, term in enumerate(terms):
            sums[index] = sums[index] + jnp.sum(term.reshape(tile // 8, 8, width), axis=0)
    for index in range(4):
        sum_ref[index : index + 1, :] = jnp.sum(sums[index], axis=0, keepdims=True)
    loss_part = jnp.sum(sum_ref[3:4, :], axis=-1, keepdims=True) * shard / (valid_total * width)
    square_ref[...] = jnp.broadcast_to(loss_part, (8, LANES))

    grad = by_sides(go, info, half)

    def put_c(term, unit):
        term = term.astype(bf16)
        rows = slice(unit * shard, (unit + 1) * shard)
        for side in range(2):
            stage_c[side, :, :, rows, :] = term[:, cuts[side]].reshape(4, 4, shard, half)

    def send(stage, outs):
        return [
            start(stage.at[side, :, plane ^ offset], dest)
            for side in (1, 0)
            for offset, dest in zip((3, 1, 2, 0), term_slots(outs, side))
        ]

    for unit in range(units):
        term = mm_tn(act[unit], grad).astype(bf16)
        deep = stage_d.shape[3]
        for side in range(2):
            where = core if side == 0 else 1 - core
            for index in range(half // deep):
                rank = (where * units + unit) * (half // deep) + index
                rows = slice(side * half + index * deep, side * half + (index + 1) * deep)
                for col in range(2):
                    stage_d[col, rank // 4, rank % 4] = term[rows, cuts[col]]
    sent = send(stage_d, terms_d)
    for unit in range(units):
        grad_active = mm_nt(grad, outer_unit(unit))
        grad_inner = (grad_active * slope[unit].astype(f32)).astype(bf16)
        slope[unit] = grad_inner
        total = jnp.sum(grad_inner.astype(f32), axis=0, keepdims=True)
        for side in range(2):
            column = (core if side == 0 else 1 - core) * units + unit
            at = pl.ds(pl.multiple_of((column % 2) * half, LANES), half)
            sum_ref[pl.ds(8 + column // 2, 1), at] = total[:, cuts[side]]
        put_c(mm_tn(low[...], slope[unit]), unit)
        acc[...] += mm_nt(slope[unit], wc[unit].reshape(width, width))

    sums = [jnp.zeros((8, width), f32) for _ in range(3)]
    for rows in tiles:
        normed, grad_first = norm[rows, :], acc[rows, :]
        grad_sum = normalize_back(grad_first * vector("gain_one"), normed, inv[rows, 0:1])
        grad_low = grad_sum.astype(bf16)
        gs_ref[rows, :] = grad_sum
        go[rows, :] = grad_low
        terms = (grad_first * normed, grad_first, grad_low.astype(f32))
        for index, term in enumerate(terms):
            sums[index] = sums[index] + jnp.sum(term.reshape(tile // 8, 8, width), axis=0)
    for index in range(3):
        sum_ref[4 + index : 5 + index, :] = jnp.sum(sums[index], axis=0, keepdims=True)
    grad = by_sides(go, info, half)
    put_c(mm_tn(mix[...], grad), units)
    put_table(stage_c, (units + 1) * shard, sum_ref, 7, 8)
    sent += send(stage_c, terms_c)
    gm_ref[...] = mm_nt(grad, wc[units].reshape(width, width)).astype(bf16)
    wait(sent)


def feed(info, mix, tok, teacher, table, long_table, own, oth, rows_at, ctx_size):
    rows, width = tok.shape
    half, units = width // 2, long_table.shape[1] // width
    shapes = [
        struct((rows, width), bf16),
        struct((rows, width), f32),
        struct((rows, width), bf16),
        struct((8, LANES), f32),
    ]
    deep = units * width // 16
    terms = []
    for size in (deep, width // 16 * (units + 1) + 16):
        terms += [struct((4, size, half), bf16), struct((3, 4, size, half), bf16)] * 2
    blocks = (mix, tok, teacher, table, long_table)
    flops = 2 * rows * width * (6 * units + 3) * width
    return pl.pallas_call(
        functools.partial(feed_kernel, ctx_size, rows_at),
        out_shape=shapes + terms,
        grid_spec=pltpu.PrefetchScalarGridSpec(
            num_scalar_prefetch=1,
            grid=(1,),
            in_specs=[whole_block(a) for a in blocks] + [ANY] * 24,
            out_specs=[whole_block(s) for s in shapes] + [ANY] * 8,
            scratch_shapes=[
                pltpu.VMEM((units + 1, 4, 4, width // 16, width), bf16),
                pltpu.VMEM((4, 4, deep, width), bf16),
                pltpu.VMEM((units, rows, width), bf16),
                pltpu.VMEM((units, rows, width), bf16),
                pltpu.VMEM((2, rows, width), f32),
                pltpu.VMEM((rows, width), f32),
                pltpu.VMEM((rows, width), f32),
                pltpu.VMEM((rows, LANES), f32),
                pltpu.VMEM((rows, width), bf16),
                pltpu.VMEM((rows, width), f32),
                pltpu.VMEM((rows, width), bf16),
                pltpu.VMEM((2, 4, 4, deep, half), bf16),
                pltpu.VMEM((2, 4, 4, width // 16 * (units + 1) + 16, half), bf16),
                pltpu.VMEM((16, width), f32),
                pltpu.SemaphoreType.DMA((12 * units + 60,)),
            ],
        ),
        compiler_params=params(),
        cost_estimate=cost(flops, 30 * width * width, 2 * rows * width * units),
        name="feed",
    )(info, *blocks, *own, *oth)


def slot_rows(ref, core, lanes):
    return jnp.concatenate(
        [ref[part, where, :, lanes] for where in (core, 1 - core) for part in range(2)], axis=0
    )


def token_back_kernel(info, own_tok, oth_tok, gq, gk, gv, gs_one, w, own_ref, send_ref, *refs):
    outs, stage, sum_ref, sem = refs[:4], refs[4], refs[5], refs[6]
    core, plane = info[0], info[1]
    width = own_tok.shape[1]
    half, shard = width // 2, width // 16
    tokens = jnp.concatenate([own_tok[...], oth_tok[...]], axis=0)

    def put(term, index):
        term = term.astype(bf16)
        rows = slice(index * shard, (index + 1) * shard)
        for side in range(2):
            cut = slice(side * half, (side + 1) * half)
            stage[side, :, :, rows, :] = term[:, cut].reshape(4, 4, shard, half)

    for index, grad in ((1, gk), (2, gv)):
        left = [slot_rows(grad, core, side_lanes(info, side, half)) for side in range(2)]
        put(mm_tn(tokens, jnp.concatenate(left, axis=1)), index)
    put(mm_tn(own_tok[...], by_sides(gq, info, half)), 0)
    sum_ref[0:1, :] = jnp.sum(gq[...].astype(f32), axis=0, keepdims=True)
    total = jnp.zeros((1, width), f32)
    for part in range(2):
        for where in range(2):
            total = total + jnp.sum(gv[part, where].astype(f32), axis=0, keepdims=True)
    sum_ref[1:2, :] = total
    put_table(stage, 3 * shard, sum_ref, 2)
    copies = []
    for side in (1, 0):
        for offset, dest in zip((3, 1, 2, 0), term_slots(outs, side)):
            copy = pltpu.make_async_copy(
                stage.at[side, :, plane ^ offset], dest, sem.at[len(copies)]
            )
            copy.start()
            copies.append(copy)
    rows = own_tok.shape[0]
    both = None
    for grad, weight in ((gk, w[1]), (gv, w[2])):
        left = [slot_rows(grad, core, side_lanes(info, side, half)) for side in range(2)]
        part = mm_nt(jnp.concatenate(left, axis=1), weight)
        both = part if both is None else both + part
    query = mm_nt(by_sides(gq, info, half), w[0])
    own_ref[...] = gs_one[...] + query + both[:rows]
    send_ref[...] = both[rows:].astype(bf16)
    for copy in copies:
        copy.wait()


def token_back(info, own_tok, oth_tok, gq, gk, gv, gs_one, w):
    rows, width = own_tok.shape
    deep, half = 3 * width // 16 + 16, width // 2
    args = (own_tok, oth_tok, gq, gk, gv, gs_one, w)
    shapes = [struct((rows, width), f32), struct((rows, width), bf16)]
    return pl.pallas_call(
        token_back_kernel,
        out_shape=shapes + [struct((4, deep, half), bf16), struct((3, 4, deep, half), bf16)] * 2,
        grid_spec=pltpu.PrefetchScalarGridSpec(
            num_scalar_prefetch=1,
            grid=(1,),
            in_specs=[whole_block(a) for a in args],
            out_specs=[whole_block(s) for s in shapes] + [ANY] * 4,
            scratch_shapes=[
                pltpu.VMEM((2, 4, 4, deep, half), bf16),
                pltpu.VMEM((8, width), f32),
                pltpu.SemaphoreType.DMA((8,)),
            ],
        ),
        compiler_params=params(),
        cost_estimate=cost(20 * rows * width * width, 40 * rows * width),
        name="token_back",
    )(info, *args)


def layout_positions(block_len, ctx_size, slot_index):
    within = jnp.arange(block_len, dtype=jnp.int32)
    front_pos = slot_index * block_len + within
    back_pos = (2 * ctx_size - 1 - slot_index) * block_len + within
    return (front_pos, back_pos)


def norm_forward(activation):
    center = activation - jnp.mean(activation, axis=-1, keepdims=True)
    inverse = lax.rsqrt(jnp.mean(center * center, axis=-1, keepdims=True) + EPSILON)
    return (center * inverse, inverse)


def norm_backward(grad_normed, normed, inverse):
    mean_grad = jnp.mean(grad_normed, axis=-1, keepdims=True)
    mean_cross = jnp.mean(grad_normed * normed, axis=-1, keepdims=True)
    return inverse * (grad_normed - mean_grad - normed * mean_cross)


def weight_grad(left, right):
    return lax.dot_general(
        left, right, (((0,), (0,)), ((), ())), preferred_element_type=jnp.float32
    )


def back_product(left, right):
    return lax.dot_general(
        left, right, (((1,), (1,)), ((), ())), preferred_element_type=jnp.float32
    )


def gelu_exact(inputs):
    return jax.nn.gelu(inputs, approximate=False)


def column_sum(matrix):
    return jnp.sum(matrix.astype(jnp.float32), axis=0)


def local_plain(
    tokens,
    prev_logits,
    teacher,
    lengths,
    w_query,
    w_key,
    w_value,
    w_output,
    w_inner,
    w_outer,
    bias_query,
    bias_value,
    bias_output,
    attn_gain,
    attn_shift,
    inner_bias,
    outer_bias,
    ffn_gain,
    ffn_shift,
):
    f32 = jnp.float32
    bf16 = jnp.bfloat16
    ctx_size = lax.axis_size("ctx")
    ctx_rank = lax.axis_index("ctx")
    dp_size = lax.axis_size("dp")
    groups = tokens.shape[0]
    block_len = tokens.shape[3]
    model_width = tokens.shape[4]
    head_count = prev_logits.shape[1]
    seq_len = prev_logits.shape[-1]
    head_dim = model_width // head_count
    local_rows = 2 * block_len
    total_rows = groups * local_rows
    score_scale = head_dim ** (-0.5)
    (
        query_matrix,
        key_matrix,
        value_matrix,
        output_matrix,
        query_add,
        value_add,
        output_add,
        first_gain,
        first_shift,
    ) = (
        lax.all_gather(w_query, "dp", axis=0, tiled=True),
        lax.all_gather(w_key, "dp", axis=0, tiled=True),
        lax.all_gather(w_value, "dp", axis=0, tiled=True),
        lax.all_gather(w_output, "dp", axis=0, tiled=True),
        lax.all_gather(bias_query, "dp", axis=0, tiled=True),
        lax.all_gather(bias_value, "dp", axis=0, tiled=True),
        lax.all_gather(bias_output, "dp", axis=0, tiled=True),
        lax.all_gather(attn_gain, "dp", axis=0, tiled=True),
        lax.all_gather(attn_shift, "dp", axis=0, tiled=True),
    )
    token_rows = tokens.reshape(total_rows, model_width)
    queries = (
        jnp.dot(token_rows, query_matrix, preferred_element_type=f32) + query_add.astype(f32)
    ).astype(bf16)
    key_rows = jnp.dot(token_rows, key_matrix, preferred_element_type=f32).astype(bf16)
    values = (
        jnp.dot(token_rows, value_matrix, preferred_element_type=f32) + value_add.astype(f32)
    ).astype(bf16)
    key_blocks, value_blocks = (
        lax.all_gather(
            key_rows.reshape(groups, 2, 1, block_len, model_width), "ctx", axis=2, tiled=True
        ),
        lax.all_gather(
            values.reshape(groups, 2, 1, block_len, model_width), "ctx", axis=2, tiled=True
        ),
    )
    inner_matrix, outer_matrix, inner_add, outer_add, second_gain, second_shift = (
        lax.all_gather(w_inner, "dp", axis=0, tiled=True),
        lax.all_gather(w_outer, "dp", axis=0, tiled=True),
        lax.all_gather(inner_bias, "dp", axis=0, tiled=True),
        lax.all_gather(outer_bias, "dp", axis=0, tiled=True),
        lax.all_gather(ffn_gain, "dp", axis=0, tiled=True),
        lax.all_gather(ffn_shift, "dp", axis=0, tiled=True),
    )
    front_pos, back_pos = layout_positions(block_len, ctx_size, ctx_rank)
    query_pos = jnp.stack([front_pos, back_pos]).reshape(local_rows)
    key_front, key_back = layout_positions(
        block_len, ctx_size, jnp.arange(ctx_size, dtype=jnp.int32)[:, None]
    )
    key_pos = jnp.stack([key_front, key_back]).reshape(seq_len)
    allowed = (key_pos[None, None, :] <= query_pos[None, :, None]) & (
        key_pos[None, None, :] < lengths[:, None, None]
    )
    valid_rows = (query_pos[None, :] < lengths[:, None]).astype(f32).reshape(total_rows)
    query_heads = queries.reshape(groups, local_rows, head_count, head_dim).transpose(2, 0, 1, 3)
    key_heads = key_blocks.reshape(groups, seq_len, head_count, head_dim).transpose(2, 0, 1, 3)
    value_heads = value_blocks.reshape(groups, seq_len, head_count, head_dim).transpose(2, 0, 1, 3)
    prev_rows = prev_logits.reshape(groups, head_count, local_rows, seq_len)

    def scores_of(head_id):
        raw_scores = (
            jnp.einsum(
                "grd,gkd->grk", query_heads[head_id], key_heads[head_id], preferred_element_type=f32
            )
            * score_scale
        )
        raw_scores = raw_scores + lax.dynamic_index_in_dim(
            prev_rows, head_id, 1, keepdims=False
        ).astype(f32)
        return (raw_scores, jnp.where(allowed, raw_scores, NEG_BIG))

    def attend(head_id):
        raw_scores, masked = scores_of(head_id)
        row_max = jnp.max(masked, axis=-1, keepdims=True)
        exponent = jnp.exp(masked - row_max)
        row_total = jnp.sum(exponent, axis=-1, keepdims=True)
        probability = (exponent / row_total).astype(bf16)
        mixed_part = jnp.einsum(
            "grk,gkd->grd", probability, value_heads[head_id], preferred_element_type=f32
        )
        return (mixed_part, row_max[..., 0] + jnp.log(row_total[..., 0]), raw_scores.astype(bf16))

    mixed_heads, log_totals, raw_heads = lax.map(attend, jnp.arange(head_count))
    raw_logits = jnp.moveaxis(raw_heads, 0, 1).reshape(prev_logits.shape)
    mixed_rows = mixed_heads.transpose(1, 2, 0, 3).reshape(total_rows, model_width).astype(bf16)
    attn_out = jnp.dot(mixed_rows, output_matrix, preferred_element_type=f32) + output_add.astype(
        f32
    )
    first_normed, first_inverse = norm_forward(token_rows.astype(f32) + attn_out)
    first = first_normed * first_gain.astype(f32) + first_shift.astype(f32)
    first_low = first.astype(bf16)
    inner_pre = jnp.dot(first_low, inner_matrix, preferred_element_type=f32) + inner_add.astype(f32)
    active, gelu_back = jax.vjp(gelu_exact, inner_pre)
    active_low = active.astype(bf16)
    outer_pre = jnp.dot(active_low, outer_matrix, preferred_element_type=f32) + outer_add.astype(
        f32
    )
    second_normed, second_inverse = norm_forward(first + outer_pre)
    result = second_normed * second_gain.astype(f32) + second_shift.astype(f32)
    errors = (result - teacher.reshape(total_rows, model_width).astype(f32)) * valid_rows[:, None]
    square_sum, valid_total = lax.psum(
        (jnp.sum(errors * errors), jnp.sum(valid_rows)), ("dp", "ctx")
    )
    loss_value = square_sum / (valid_total * model_width)
    loss_scale = dp_size * groups * seq_len * model_width / 2.0
    grad_result = errors * (loss_scale * 2.0 / (valid_total * model_width))
    grad_second_gain = jnp.sum(grad_result * second_normed, axis=0)
    grad_second_shift = jnp.sum(grad_result, axis=0)
    grad_sum_two = norm_backward(
        grad_result * second_gain.astype(f32), second_normed, second_inverse
    )
    grad_outer = grad_sum_two.astype(bf16)
    grad_outer_matrix = weight_grad(active_low, grad_outer)
    grad_outer_add = column_sum(grad_outer)
    grad_active = back_product(grad_outer, outer_matrix)
    grad_inner = gelu_back(grad_active)[0].astype(bf16)
    grad_inner_matrix = weight_grad(first_low, grad_inner)
    grad_inner_add = column_sum(grad_inner)
    grad_first = grad_sum_two + back_product(grad_inner, inner_matrix)
    grad_first_gain = jnp.sum(grad_first * first_normed, axis=0)
    grad_first_shift = jnp.sum(grad_first, axis=0)
    grad_sum_one = norm_backward(grad_first * first_gain.astype(f32), first_normed, first_inverse)
    grad_attn = grad_sum_one.astype(bf16)
    grad_output_matrix = weight_grad(mixed_rows, grad_attn)
    grad_output_add = column_sum(grad_attn)
    grad_mixed = back_product(grad_attn, output_matrix).astype(bf16)
    grad_mixed_heads = grad_mixed.reshape(groups, local_rows, head_count, head_dim).transpose(
        2, 0, 1, 3
    )

    def attend_back(head_id):
        _, masked = scores_of(head_id)
        probability = jnp.exp(masked - log_totals[head_id][..., None])
        grad_part = grad_mixed_heads[head_id]
        grad_value_part = jnp.einsum(
            "grk,grd->gkd", probability.astype(bf16), grad_part, preferred_element_type=f32
        )
        grad_probs = jnp.einsum(
            "grd,gkd->grk", grad_part, value_heads[head_id], preferred_element_type=f32
        )
        row_dot = jnp.sum(probability * grad_probs, axis=-1, keepdims=True)
        grad_scores = (probability * (grad_probs - row_dot)).astype(bf16)
        grad_query_part = (
            jnp.einsum("grk,gkd->grd", grad_scores, key_heads[head_id], preferred_element_type=f32)
            * score_scale
        )
        grad_key_part = (
            jnp.einsum(
                "grk,grd->gkd", grad_scores, query_heads[head_id], preferred_element_type=f32
            )
            * score_scale
        )
        return (grad_scores, grad_query_part, grad_key_part, grad_value_part)

    grad_score_heads, grad_query_heads, grad_key_heads, grad_value_heads = lax.map(
        attend_back, jnp.arange(head_count)
    )
    grad_logits = jnp.moveaxis(grad_score_heads, 0, 1).reshape(prev_logits.shape)
    grad_queries = (
        grad_query_heads.transpose(1, 2, 0, 3).reshape(total_rows, model_width).astype(bf16)
    )
    key_terms = grad_key_heads.transpose(1, 2, 0, 3).reshape(
        groups, 2, ctx_size, block_len, model_width
    )
    value_terms = grad_value_heads.transpose(1, 2, 0, 3).reshape(
        groups, 2, ctx_size, block_len, model_width
    )
    key_sums, value_sums = (
        lax.psum_scatter(
            key_terms.astype(jnp.bfloat16), "ctx", scatter_dimension=2, tiled=True
        ).astype(jnp.float32),
        lax.psum_scatter(
            value_terms.astype(jnp.bfloat16), "ctx", scatter_dimension=2, tiled=True
        ).astype(jnp.float32),
    )
    grad_keys = key_sums.reshape(total_rows, model_width).astype(bf16)
    grad_values = value_sums.reshape(total_rows, model_width).astype(bf16)
    grad_query_matrix = weight_grad(token_rows, grad_queries)
    grad_key_matrix = weight_grad(token_rows, grad_keys)
    grad_value_matrix = weight_grad(token_rows, grad_values)
    grad_query_add = column_sum(grad_queries)
    grad_value_add = column_sum(grad_values)
    grad_token_rows = (
        grad_sum_one
        + back_product(grad_queries, query_matrix)
        + back_product(grad_keys, key_matrix)
        + back_product(grad_values, value_matrix)
    )
    matrix_grads = (
        grad_query_matrix,
        grad_key_matrix,
        grad_value_matrix,
        grad_output_matrix,
        grad_inner_matrix,
        grad_outer_matrix,
    )
    vector_grads = (
        grad_query_add,
        grad_value_add,
        grad_output_add,
        grad_first_gain,
        grad_first_shift,
        grad_inner_add,
        grad_outer_add,
        grad_second_gain,
        grad_second_shift,
    )
    summed = (
        lax.psum_scatter(
            matrix_grads[0].astype(jnp.bfloat16), "dp", scatter_dimension=0, tiled=True
        ).astype(jnp.float32),
        lax.psum_scatter(
            matrix_grads[1].astype(jnp.bfloat16), "dp", scatter_dimension=0, tiled=True
        ).astype(jnp.float32),
        lax.psum_scatter(
            matrix_grads[2].astype(jnp.bfloat16), "dp", scatter_dimension=0, tiled=True
        ).astype(jnp.float32),
        lax.psum_scatter(
            matrix_grads[3].astype(jnp.bfloat16), "dp", scatter_dimension=0, tiled=True
        ).astype(jnp.float32),
        lax.psum_scatter(
            matrix_grads[4].astype(jnp.bfloat16), "dp", scatter_dimension=0, tiled=True
        ).astype(jnp.float32),
        lax.psum_scatter(
            matrix_grads[5].astype(jnp.bfloat16), "dp", scatter_dimension=0, tiled=True
        ).astype(jnp.float32),
        lax.psum_scatter(
            vector_grads[0].astype(jnp.bfloat16), "dp", scatter_dimension=0, tiled=True
        ).astype(jnp.float32),
        lax.psum_scatter(
            vector_grads[1].astype(jnp.bfloat16), "dp", scatter_dimension=0, tiled=True
        ).astype(jnp.float32),
        lax.psum_scatter(
            vector_grads[2].astype(jnp.bfloat16), "dp", scatter_dimension=0, tiled=True
        ).astype(jnp.float32),
        lax.psum_scatter(
            vector_grads[3].astype(jnp.bfloat16), "dp", scatter_dimension=0, tiled=True
        ).astype(jnp.float32),
        lax.psum_scatter(
            vector_grads[4].astype(jnp.bfloat16), "dp", scatter_dimension=0, tiled=True
        ).astype(jnp.float32),
        lax.psum_scatter(
            vector_grads[5].astype(jnp.bfloat16), "dp", scatter_dimension=0, tiled=True
        ).astype(jnp.float32),
        lax.psum_scatter(
            vector_grads[6].astype(jnp.bfloat16), "dp", scatter_dimension=0, tiled=True
        ).astype(jnp.float32),
        lax.psum_scatter(
            vector_grads[7].astype(jnp.bfloat16), "dp", scatter_dimension=0, tiled=True
        ).astype(jnp.float32),
        lax.psum_scatter(
            vector_grads[8].astype(jnp.bfloat16), "dp", scatter_dimension=0, tiled=True
        ).astype(jnp.float32),
    )
    reduced = (
        lax.psum(summed[0].astype(jnp.bfloat16), "ctx").astype(jnp.float32),
        lax.psum(summed[1].astype(jnp.bfloat16), "ctx").astype(jnp.float32),
        lax.psum(summed[2].astype(jnp.bfloat16), "ctx").astype(jnp.float32),
        lax.psum(summed[3].astype(jnp.bfloat16), "ctx").astype(jnp.float32),
        lax.psum(summed[4].astype(jnp.bfloat16), "ctx").astype(jnp.float32),
        lax.psum(summed[5].astype(jnp.bfloat16), "ctx").astype(jnp.float32),
        lax.psum(summed[6].astype(jnp.bfloat16), "ctx").astype(jnp.float32),
        lax.psum(summed[7].astype(jnp.bfloat16), "ctx").astype(jnp.float32),
        lax.psum(summed[8].astype(jnp.bfloat16), "ctx").astype(jnp.float32),
        lax.psum(summed[9].astype(jnp.bfloat16), "ctx").astype(jnp.float32),
        lax.psum(summed[10].astype(jnp.bfloat16), "ctx").astype(jnp.float32),
        lax.psum(summed[11].astype(jnp.bfloat16), "ctx").astype(jnp.float32),
        lax.psum(summed[12].astype(jnp.bfloat16), "ctx").astype(jnp.float32),
        lax.psum(summed[13].astype(jnp.bfloat16), "ctx").astype(jnp.float32),
        lax.psum(summed[14].astype(jnp.bfloat16), "ctx").astype(jnp.float32),
    )
    return (
        result.astype(bf16).reshape(tokens.shape),
        raw_logits,
        loss_value,
        grad_token_rows.astype(bf16).reshape(tokens.shape),
        grad_logits,
        reduced[0],
        reduced[1],
        reduced[2],
        reduced[3],
        reduced[4],
        reduced[5],
        reduced[6],
        reduced[7],
        reduced[8],
        reduced[9],
        reduced[10],
        reduced[11],
        reduced[12],
        reduced[13],
        reduced[14],
    )


def local_fast(tokens, prev_logits, teacher, lengths, *parameters):
    weights, vectors = parameters[:6], parameters[6:]
    w_outer = weights[5]
    ctx_size = lax.axis_size("ctx")
    core = lax.axis_index("ctx")
    dp_size = lax.axis_size("dp")
    dp_rank = lax.axis_index("dp")
    block_len, width = tokens.shape[3], tokens.shape[4]
    head_count, seq_len = prev_logits.shape[1], prev_logits.shape[-1]
    head_dim = width // head_count
    rows = 2 * block_len
    shard = weights[0].shape[0]
    half = width // 2
    units = weights[4].shape[1] // width
    info = jnp.stack([core, dp_rank % 4, lengths[0], dp_rank // 4]).astype(jnp.int32)
    token_rows = tokens.reshape(rows, width)
    teacher_rows = teacher.reshape(rows, width)
    prev_rows = prev_logits.reshape(head_count, rows, seq_len)
    sizes = (block_len, ctx_size, head_dim)
    pairs = [(i, i) for i in range(head_count * head_dim // LANES)]
    (long_at,) = [i for i, v in enumerate(vectors) if v.shape[0] != shard]
    names = ("bq", "bv", "bo", "gain_one", "shift_one", "long", "b_outer", "gain_two", "shift_two", "count")
    rows_at = {name: i for i, name in enumerate(names)}
    rows_at["scale"] = float(dp_size * seq_len * width)

    chunk_a, chunk_c, chunk_d, chunk_e = pack(info, weights, vectors)
    cut_c, cut_d = split_row(chunk_c.shape[0]), split_row(chunk_d.shape[0])
    rows_at.update(
        rows_c=chunk_c.shape[0], cut_c=cut_c, cut_d=cut_d, deep_d=w_outer.shape[0] - chunk_e.shape[0]
    )
    cross = lambda piece: flip(piece, "ctx", 1)
    parts_a = z_triple(chunk_a)
    parts_e = [chunk_e] + [flip(chunk_e, "dp", step) for step in (1, 2, 3)]
    parts_a, parts_e, token_rows, chunk_c, chunk_d = together(
        parts_a, parts_e, token_rows, chunk_c, chunk_d
    )
    column_a = in_order(dp_rank // 4, parts_a)
    sides_a = side_columns(column_a)
    next_c = flip(chunk_c, "dp", 4)
    other_rows = cross(token_rows)
    pair_c = z_pair(chunk_c, next_c)
    over_c = flip(pair_c, "dp", 8)
    sides_a, other_rows, over_c, chunk_d = together(sides_a, other_rows, over_c, chunk_d)
    corner_a = corner_column(sides_a)
    own_a = [column_a, *sides_a]
    oth_a = [cross(piece) for piece in own_a]
    next_d = flip(chunk_d, "dp", 4)
    corner_a, oth_a, next_d, parts_e = together(corner_a, oth_a, next_d, parts_e)
    oth_a = [*oth_a, *[cross(piece) for piece in corner_a]]
    own_a = [*own_a, *corner_a]
    column_c = z_column(pair_c, over_c)
    sides_c = side_columns(column_c)
    pair_d = z_pair(chunk_d, next_d)
    over_d = flip(pair_d, "dp", 8)
    plane_e = in_order(dp_rank % 4, parts_e)
    next_e = flip(plane_e, "dp", 4)
    oth_e = [cross(plane_e)]
    queries, keys, values, w_attn, table, long_table = project(
        info, token_rows, other_rows, own_a, oth_a, block_len, vectors[long_at].shape[0]
    )
    queries, sides_c, pair_d, over_d, plane_e, next_e, oth_e = together(
        queries, sides_c, pair_d, over_d, plane_e, next_e, oth_e
    )
    column_d = z_column(pair_d, over_d)
    far_up = flip(jnp.concatenate([sides_c[0][:, :cut_c], column_d], axis=1), "dp", 2)
    near_low = flip(jnp.concatenate([sides_c[1][:, cut_c:], column_d], axis=1), "dp", 1)
    over_e = [flip(plane_e, "dp", 8)]
    oth_c = [cross(column_c), cross(sides_c[0])]
    qkv = (queries, keys, values)
    carry = attend(info, qkv, prev_rows, pairs[:4], None, *sizes)
    carry, oth_c, column_d, far_up, near_low, over_e = together(
        carry, oth_c, column_d, far_up, near_low, over_e
    )
    near_d = near_low[:, chunk_c.shape[0] - cut_c :]
    far_d = far_up[:, cut_c:]
    corner_d = [flip(near_d[:, :cut_d], "dp", 2), flip(far_d[:, cut_d:], "dp", 1)]
    over_e.append(flip(next_e, "dp", 8))
    late = [far_up, near_low]
    oth_late = [cross(piece) for piece in late]
    logits, probs, mixed = attend(info, qkv, prev_rows, pairs[4:], carry, *sizes)
    mixed, oth_c, oth_late, corner_d, over_e, column_d, next_e, sides_c = together(
        mixed, oth_c, oth_late, corner_d, over_e, column_d, next_e, sides_c
    )
    own_c = [column_c, *sides_c, far_up, near_low]
    own_d = [column_d, *corner_d, plane_e, next_e, *over_e]
    oth_c += [cross(sides_c[1]), *oth_late]
    oth_d = [cross(piece) for piece in own_d[:3]] + oth_e + [cross(piece) for piece in own_d[4:]]
    result, grad_sum_one, grad_mixed, square, *terms = feed(
        info, mixed, token_rows, teacher_rows, table, long_table,
        [*own_c, *own_d], [*oth_c, *oth_d], rows_at, ctx_size,
    )

    back = lambda some, carry: attend_back(qkv, probs, grad_mixed, some, carry, *sizes)
    kept_d, sent_d, kept_c, sent_c = terms[:2], terms[2:4], terms[4:6], terms[6:8]
    came_d = [cross(sent_d[0])]
    square = square + cross(square)
    sent_d, sent_c, square, came_d, grad_mixed = together(sent_d, sent_c, square, came_d, grad_mixed)
    corner_d = scatter_corner(kept_d[0], came_d[0])
    came_d.append(cross(sent_d[1]))
    came_c = [cross(part) for part in sent_c]
    grads = back(pairs[:2], [])
    grads, corner_d, came_d, came_c, square = together(grads, corner_d, came_d, came_c, square)
    sides_d = send_sides(scatter_sides(kept_d[1], came_d[1], corner_d))
    corner_c = scatter_corner(kept_c[0], came_c[0])
    square = square + flip(square, "dp", 8)
    grad_logits, gq, gk, gv = back(pairs[2:], grads)
    gk, gv = [g.reshape(2, 2, block_len, width) for g in (gk, gv)]
    gq, sides_d, corner_c, square = together(gq, sides_d, corner_c, square)
    sides_c = scatter_sides(kept_c[1], came_c[1], corner_c)
    half_d = scatter_half(kept_d[1], came_d[1], sides_d)
    sides_c, half_d, gq = together(sides_c, half_d, gq)
    sides_c, half_d = send_sides(sides_c), (half_d[0], flip(half_d[1], "dp", 8))
    own_terms, sent_terms, *terms_a = token_back(
        info, token_rows, other_rows, gq, gk, gv, grad_sum_one, w_attn
    )
    own_terms, sent_terms, terms_a, sides_c, half_d = together(
        own_terms, sent_terms, terms_a, sides_c, half_d
    )
    kept_a, sent_a = terms_a[:2], terms_a[2:4]
    came_a = [cross(part) for part in sent_a]
    half_c = scatter_half(kept_c[1], came_c[1], sides_c)
    half_c = (half_c[0], flip(half_c[1], "dp", 8))
    rank_d = scatter_rank(*half_d)
    came_a, rank_d, sent_terms = together(came_a, rank_d, sent_terms)
    corner_a = scatter_corner(kept_a[0], came_a[0])
    total_d = scatter_total(rank_d[0], [rank_d[1]])
    grad_tokens = (own_terms + cross(sent_terms).astype(f32)).astype(bf16)
    corner_a, total_d, grad_tokens = together(corner_a, total_d, grad_tokens)
    sides_a = send_sides(scatter_sides(kept_a[1], came_a[1], corner_a))
    rank_c = scatter_rank(*half_c)
    sides_a, rank_c, square = together(sides_a, rank_c, square)
    triple_a = scatter_triple(kept_a[1], came_a[1], sides_a)
    total_c = scatter_total(rank_c[0], [rank_c[1]])
    square = square + flip(square, "dp", 1)
    square = square + flip(square, "dp", 2)
    triple_a, square, total_c = together(triple_a, square, total_c)
    square = square + flip(square, "dp", 4)
    total_a = scatter_total(*triple_a)
    pair_a, pair_c, pair_d = by_halves(*total_a), by_halves(*total_c), by_halves(*total_d)
    def unit(parts, index):
        return [part[index * shard : (index + 1) * shard] for part in parts]

    grad_w_inner = jnp.concatenate(
        [unit(pair_c[side : side + 1], i)[0] for side in range(2) for i in range(units)], axis=1
    )
    sums_c, sums_a = total_c[0][(units + 1) * shard :].astype(f32), total_a[0][3 * shard :].astype(f32)
    order = (6, 4, 5, None, 2, 0, 1)
    vector_totals = [sums_a[0, :shard], sums_a[1, :shard]]
    vector_totals += [
        sums_c[7, : vectors[long_at].shape[0]] if i is None else sums_c[i, :shard] for i in order
    ]
    return (
        result.reshape(tokens.shape),
        logits.reshape(prev_logits.shape),
        square[0, 0],
        grad_tokens.reshape(tokens.shape),
        grad_logits.reshape(prev_logits.shape),
        *[jnp.concatenate(unit(pair_a, i), axis=1) for i in range(3)],
        jnp.concatenate(unit(pair_c, units), axis=1),
        grad_w_inner,
        jnp.concatenate(pair_d, axis=1),
        *vector_totals,
    )


def local(tokens, prev_logits, teacher, lengths, *parameters):
    width, shard = tokens.shape[-1], parameters[0].shape[0]
    fits = (
        lax.axis_size("dp") == 16
        and lax.axis_size("ctx") == 2
        and tokens.shape[0] == 1
        and shard % 16 == 0
        and width % 256 == 0
    )
    chosen = local_fast if fits else local_plain
    return chosen(tokens, prev_logits, teacher, lengths, *parameters)


def solution(mesh):
    rows = P("dp", None, "ctx", None, None)
    scores = P("dp", None, None, "ctx", None, None)
    matrix, vector = P("dp", None), P("dp")
    return jax.shard_map(
        local,
        mesh=mesh,
        in_specs=(rows, scores, rows, vector) + (matrix,) * 6 + (vector,) * 9,
        out_specs=(rows, scores, P(), rows, scores) + (matrix,) * 6 + (vector,) * 9,
        check_vma=False,
    )
```

```python
import functools

import jax
import jax.numpy as jnp
from jax import lax
from jax.experimental import pallas as pl
from jax.experimental.pallas import tpu as pltpu
from jax.sharding import PartitionSpec as P

EPSILON = 1e-05
NEG_BIG = -1e30
POS_BIG = 3.0e38
LANES = 128
f32 = jnp.float32
bf16 = jnp.bfloat16
ANY = pl.BlockSpec(memory_space=pl.ANY)


def mm(left, right):
    return jnp.dot(left, right, preferred_element_type=f32)


def mm_tn(left, right):
    return lax.dot_general(left, right, (((0,), (0,)), ((), ())), preferred_element_type=f32)


def mm_nt(left, right):
    return lax.dot_general(left, right, (((1,), (1,)), ((), ())), preferred_element_type=f32)


def struct(shape, dtype):
    return jax.ShapeDtypeStruct(shape, dtype)


def params():
    return pltpu.CompilerParams(vmem_limit_bytes=56 << 20)


def cost(flops, bytes_accessed, transcendentals=0):
    return pl.CostEstimate(
        flops=int(flops), bytes_accessed=int(bytes_accessed), transcendentals=int(transcendentals)
    )


def together(*values):
    return lax.optimization_barrier(values)


def after(value, *others):
    return lax.optimization_barrier((value, others))[0]


def whole_block(array):
    rank = len(array.shape)
    return pl.BlockSpec(array.shape, lambda *_: (0,) * rank)


def side_lanes(info, side, width):
    half = info[0] if side == 0 else 1 - info[0]
    return pl.ds(pl.multiple_of(half * width, LANES), width)


def flip(array, axis_name, bit):
    size = lax.axis_size(axis_name)
    return lax.ppermute(array, axis_name, [(i, i ^ bit) for i in range(size)])


def z_bits():
    dp_rank = lax.axis_index("dp")
    return dp_rank // 4 % 2, dp_rank // 8


def z_pair(array, arrived):
    low = z_bits()[0] == 0
    return jnp.stack([jnp.where(low, array, arrived), jnp.where(low, arrived, array)])


def z_column(pair, arrived):
    low = z_bits()[1] == 0
    return jnp.concatenate([jnp.where(low, pair, arrived), jnp.where(low, arrived, pair)])


def z_triple(array):
    return [array] + [flip(array, "dp", 4 * step) for step in (1, 2, 3)]


def in_order(mine, parts):
    return jnp.stack([lax.select_n(mine ^ i, *parts) for i in range(4)])


def side_columns(column):
    return flip(column, "dp", 1), flip(column, "dp", 2)


def corner_column(sides):
    cut = split_row(sides[0].shape[1])
    return flip(sides[0][:, :cut], "dp", 2), flip(sides[1][:, cut:], "dp", 1)


def split_row(rows):
    return rows // 32 * 16


def scatter_corner(kept, arrived):
    cut = split_row(kept.shape[1])
    term = (kept.astype(f32) + arrived.astype(f32)).astype(bf16)
    return flip(term[:, :cut], "dp", 2), flip(term[:, cut:], "dp", 1)


def scatter_sides(kept, arrived, corner):
    upper, lower = [part.astype(f32) for part in corner]
    near = kept[0].astype(f32) + arrived[0].astype(f32)
    far = kept[1].astype(f32) + arrived[1].astype(f32)
    cut = upper.shape[1]
    near = jnp.concatenate([near[:, :cut] + upper, near[:, cut:]], axis=1)
    far = jnp.concatenate([far[:, :cut], far[:, cut:] + lower], axis=1)
    return near.astype(bf16), far.astype(bf16)


def send_sides(sides):
    return flip(sides[0], "dp", 1), flip(sides[1], "dp", 2)


def scatter_half(kept, arrived, sides):
    column = sum(part.astype(f32) for part in (kept[2], arrived[2], *sides))
    column = column.reshape(2, 2, *column.shape[1:])
    high = z_bits()[1]
    pick = lambda half: lax.dynamic_index_in_dim(column, half, 0, keepdims=False)
    return pick(high), pick(1 - high).astype(bf16)


def scatter_rank(kept, arrived):
    column = kept + arrived.astype(f32)
    low = z_bits()[0]
    pick = lambda half: lax.dynamic_index_in_dim(column, half, 0, keepdims=False)
    return pick(low), flip(pick(1 - low).astype(bf16), "dp", 4)


def scatter_triple(kept, arrived, sides):
    mine = lax.axis_index("dp") // 4
    column = sum(part.astype(f32) for part in (kept[2], arrived[2], *sides))
    pick = lambda z: lax.dynamic_index_in_dim(column, z, 0, keepdims=False)
    return pick(mine), [flip(pick(mine ^ step).astype(bf16), "dp", 4 * step) for step in (2, 3, 1)]


def scatter_total(kept, arrived):
    total = kept
    for part in arrived:
        total = total + part.astype(f32)
    total = total.astype(bf16)
    return total, flip(total, "ctx", 1)


def by_halves(total, across):
    core = lax.axis_index("ctx")
    return (
        jnp.where(core == 0, total, across).astype(f32),
        jnp.where(core == 0, across, total).astype(f32),
    )


def pack_kernel(info, *refs):
    vectors, outs = refs[6:-4], refs[-4:]
    half = outs[0].shape[1]
    shard = refs[0].shape[0]
    units = refs[4].shape[1] // (2 * half)
    lanes = side_lanes(info, 0, half)

    def unit(index):
        column = pl.multiple_of((info[0] * units + index) * half, LANES)
        return refs[4][:, pl.ds(column, half)]

    for index in range(3):
        outs[0][index * shard : (index + 1) * shard, :] = refs[index][:, lanes]
    count = units // 2
    for index in range(count):
        rows = slice(index * shard, (index + 1) * shard)
        outs[1][rows, :] = unit(index)
        outs[2][rows, :] = unit(count + index)
    outs[1][count * shard :, :] = refs[3][:, lanes]
    split = refs[5].shape[0] - outs[3].shape[0]
    outs[2][count * shard :, :] = refs[5][:split, lanes]
    outs[3][...] = refs[5][split:, lanes]
    row = lax.broadcasted_iota(jnp.int32, (16, half), 0)
    table = jnp.zeros((16, half), f32)
    for index, ref in enumerate(vectors):
        value = jnp.pad(ref[...].astype(f32), ((0, 0), (0, half - ref.shape[1])))
        table = jnp.where(row == index, value, table)
    table = jnp.where(row == len(vectors), (info[2] // 32).astype(f32), table)
    table = jnp.where(row == len(vectors) + 1, (info[2] % 32).astype(f32), table)
    outs[0][3 * shard :, :] = table.astype(bf16)


def pack(info, weights, vectors):
    shard, width = weights[0].shape
    half, count = width // 2, weights[4].shape[1] // width // 2
    deep = weights[5].shape[0]
    split = deep // 32 * 16
    sizes = (3 * shard + 16, (count + 1) * shard, count * shard + split, deep - split)
    shapes = [struct((size, half), bf16) for size in sizes]
    args = [*weights, *[v[None] for v in vectors]]
    return pl.pallas_call(
        pack_kernel,
        out_shape=shapes,
        grid_spec=pltpu.PrefetchScalarGridSpec(
            num_scalar_prefetch=1,
            grid=(1,),
            in_specs=[whole_block(a) for a in args],
            out_specs=[whole_block(s) for s in shapes],
        ),
        compiler_params=params(),
        cost_estimate=cost(0, 4 * sum(w.size for w in weights)),
        name="pack",
    )(info, *args)


def piece_parts(pieces, cut, plane, start, rows):
    parts = []
    for offset in range(3):
        ref, base = pieces[offset]
        parts.append((ref.at[:, pl.ds(base + start, rows)], plane ^ (0, 1, 2)[offset], 0, rows))
    (upper, base_up), (lower, base_low) = pieces[3:]
    if start < cut:
        count = min(start + rows, cut) - start
        parts.append((upper.at[:, pl.ds(base_up + start, count)], plane ^ 3, 0, count))
    if start + rows > cut:
        skip = max(start, cut)
        count = start + rows - skip
        parts.append((lower.at[:, pl.ds(base_low + skip - cut, count)], plane ^ 3, skip - start, count))
    return parts


def slot_start(slot, ctx_size, block_len):
    half, which = divmod(slot, ctx_size)
    return (which if half == 0 else 2 * ctx_size - 1 - which) * block_len


def head_lanes(which, head_dim):
    lane = lax.broadcasted_iota(jnp.int32, (1, LANES), 1)
    return (lane >= which * head_dim) & (lane < (which + 1) * head_dim)


def attend_kernel(
    block_len, ctx_size, head_dim, info, q_ref, k_ref, v_ref, prev_ref, logit_ref, prob_ref, mix_ref, limit_ref
):
    seq_len = 2 * ctx_size * block_len
    half = ctx_size * block_len
    heads = LANES // head_dim

    @pl.when(pl.program_id(0) == 0)
    def _():
        core, length = info[0], info[2]
        within = lax.broadcasted_iota(jnp.int32, (block_len, block_len), 1)
        row = lax.broadcasted_iota(jnp.int32, (block_len, block_len), 0)
        for part in range(2):
            start = core if part == 0 else 2 * ctx_size - 1 - core
            query_pos = row + start * block_len
            for slot in range(2 * ctx_size):
                key_pos = within + slot_start(slot, ctx_size, block_len)
                allowed = (key_pos <= query_pos) & (key_pos < length)
                limit_ref[
                    part * block_len : (part + 1) * block_len,
                    slot * block_len : (slot + 1) * block_len,
                ] = jnp.where(allowed, POS_BIG, NEG_BIG)

    scale = head_dim ** (-0.5)
    masks = [head_lanes(which, head_dim) for which in range(heads)]
    values = [jnp.where(mask, v_ref[...], 0.0).astype(bf16) for mask in masks]
    scores = []
    for which in range(heads):
        query = jnp.where(masks[which], q_ref[...].astype(f32) * scale, 0.0).astype(bf16)
        scores.append(mm_nt(query, k_ref[...]))
    for part in range(2):
        rows = slice(part * block_len, (part + 1) * block_len)
        keys = half if part == 0 else seq_len
        probabilities = []
        for which in range(heads):
            raw = scores[which][rows, :] + prev_ref[which, rows, :].astype(f32)
            logit_ref[which, rows, :] = raw.astype(bf16)
            masked = jnp.minimum(raw[:, :keys], limit_ref[rows, :keys])
            top = jnp.max(masked, axis=-1, keepdims=True)
            exponent = jnp.exp(masked - top)
            total = jnp.sum(exponent, axis=-1, keepdims=True)
            probability = (exponent * (1.0 / total)).astype(bf16)
            prob_ref[which, rows, :keys] = probability
            probabilities.append(probability)
        mixed = mm(
            jnp.concatenate(probabilities, axis=1),
            jnp.concatenate([value[:keys] for value in values], axis=0),
        )
        mix_ref[rows, :] = mixed.astype(bf16)


def attend_back_kernel(
    block_len, ctx_size, head_dim, q_ref, k_ref, v_ref, prob_ref, gm_ref, gs_ref, gq_ref, gk_ref, gv_ref, gk_sum, gv_sum
):
    seq_len = 2 * ctx_size * block_len
    half = ctx_size * block_len
    heads = LANES // head_dim
    scale = head_dim ** (-0.5)
    masks = [head_lanes(which, head_dim) for which in range(heads)]
    keys_in = [jnp.where(mask, k_ref[...], 0.0).astype(bf16) for mask in masks]
    for part in (1, 0):
        rows = slice(part * block_len, (part + 1) * block_len)
        keys = half if part == 0 else seq_len
        grads, queries, probs, grad_mixes = [], [], [], []
        for which in range(heads):
            grad_mix = jnp.where(masks[which], gm_ref[rows, :], 0.0).astype(bf16)
            prob_low = prob_ref[which, rows, :keys]
            probability = prob_low.astype(f32)
            grad_prob = mm_nt(grad_mix, v_ref[:keys, :])
            term = probability * grad_prob
            row_dot = jnp.sum(term, axis=-1, keepdims=True)
            grad_score = (term - probability * row_dot).astype(bf16)
            gs_ref[which, rows, :keys] = grad_score
            if keys < seq_len:
                gs_ref[which, rows, keys:] = jnp.zeros((block_len, seq_len - keys), bf16)
            grads.append(grad_score)
            queries.append(jnp.where(masks[which], q_ref[rows, :], 0.0).astype(bf16))
            probs.append(prob_low)
            grad_mixes.append(grad_mix)
        grad_value = mm_tn(jnp.concatenate(probs, axis=0), jnp.concatenate(grad_mixes, axis=0))
        grad_key = mm_tn(jnp.concatenate(grads, axis=0), jnp.concatenate(queries, axis=0))
        if part == 1:
            gv_sum[...] = grad_value
            gk_sum[...] = grad_key
        else:
            gv_sum[:keys, :] += grad_value
            gk_sum[:keys, :] += grad_key
        grad_query = mm(
            jnp.concatenate(grads, axis=1), jnp.concatenate([key[:keys] for key in keys_in], axis=0)
        )
        gq_ref[rows, :] = (grad_query * scale).astype(bf16)
    gk_ref[...] = (gk_sum[...] * scale).astype(bf16)
    gv_ref[...] = gv_sum[...].astype(bf16)


def pair_specs(rows, seq_len, heads, places):
    def at(h, which):
        index = places[-1][which]
        for i in range(len(places) - 1):
            index = jnp.where(h == i, places[i][which], index)
        return index

    wide = pl.BlockSpec((heads, rows, seq_len), lambda h, *_: (at(h, 0), 0, 0))
    mixed = pl.BlockSpec((rows, LANES), lambda h, *_: (0, at(h, 0)))
    narrow = pl.BlockSpec((rows, LANES), lambda h, *_: (0, at(h, 1)))
    whole = pl.BlockSpec((seq_len, LANES), lambda h, *_: (0, at(h, 1)))
    return wide, mixed, narrow, whole


def attend(info, qkv, prev, places, carry, block_len, ctx_size, head_dim):
    head_count, rows, seq_len = prev.shape
    heads, count = LANES // head_dim, len(places)
    wide, mixed, narrow, whole = pair_specs(rows, seq_len, heads, places)
    kernel = functools.partial(attend_kernel, block_len, ctx_size, head_dim)
    given = () if carry is None else carry
    mixed_shape = struct((rows, head_count * head_dim), bf16)
    return pl.pallas_call(
        drop_refs(kernel, 5, len(given)),
        out_shape=(struct(prev.shape, bf16), struct(prev.shape, bf16), mixed_shape),
        grid_spec=pltpu.PrefetchScalarGridSpec(
            num_scalar_prefetch=1,
            grid=(count,),
            in_specs=[narrow, whole, whole, wide] + [ANY] * len(given),
            out_specs=[wide, wide, mixed],
            scratch_shapes=[pltpu.VMEM((rows, seq_len), f32)],
        ),
        input_output_aliases={5 + i: i for i in range(len(given))},
        compiler_params=params(),
        cost_estimate=cost(
            8 * rows * seq_len * LANES * heads * count,
            6 * rows * seq_len * heads * count,
            rows * seq_len * heads * count,
        ),
        name="attend",
    )(info, *qkv, prev, *given)


def drop_refs(kernel, start, count):
    def run(*refs):
        kernel(*refs[:start], *refs[start + count :])

    return run if count else kernel


def attend_back(qkv, probs, grad_mixed, places, carry, block_len, ctx_size, head_dim):
    head_count, rows, seq_len = probs.shape
    heads, count = LANES // head_dim, len(places)
    wide, mixed, narrow, whole = pair_specs(rows, seq_len, heads, places)
    kernel = functools.partial(attend_back_kernel, block_len, ctx_size, head_dim)
    given = tuple(carry)
    return pl.pallas_call(
        drop_refs(kernel, 5, len(given)),
        out_shape=[struct(probs.shape, bf16)] + [struct(a.shape, bf16) for a in qkv],
        grid=(count,),
        in_specs=[narrow, whole, whole, wide, mixed] + [ANY] * len(given),
        out_specs=[wide, narrow, whole, whole],
        scratch_shapes=[pltpu.VMEM((seq_len, LANES), f32), pltpu.VMEM((seq_len, LANES), f32)],
        input_output_aliases={5 + i: i for i in range(len(given))},
        compiler_params=params(),
        cost_estimate=cost(
            16 * rows * seq_len * LANES * heads * count, 4 * rows * seq_len * heads * count
        ),
        name="attend_back",
    )(*qkv, probs, grad_mixed, *given)


def by_sides(ref, info, width):
    return jnp.concatenate(
        [ref[:, side_lanes(info, 0, width)], ref[:, side_lanes(info, 1, width)]], axis=1
    )


def project_kernel(info, own_tok, oth_tok, *refs):
    own, oth = [[(ref, 0) for ref in refs[i : i + 5]] for i in (0, 5)]
    cut = split_row(refs[0].shape[1])
    q_ref, k_ref, v_ref, w, table_ref, long_ref, table, sem = refs[10:]
    core, plane = info[0], info[1]
    block_len = k_ref.shape[2]
    rows, width = own_tok.shape
    half, shard = width // 2, width // 16
    cuts = [slice(0, half), slice(half, width)]
    copies = []

    def copy(source, dest):
        copies.append(pltpu.make_async_copy(source, dest, sem.at[len(copies)]))
        copies[-1].start()

    for source, where, _, _ in piece_parts(own, cut, plane, 3 * shard, 16):
        copy(source, table.at[:, where])
    for unit in range(3):
        for side, pieces in enumerate((own, oth)):
            for source, where, first, count in piece_parts(pieces, cut, plane, unit * shard, shard):
                copy(source, w.at[unit, :, where, pl.ds(first, count), cuts[side]])
    for item in copies:
        item.wait()
    long_span = long_ref.shape[1] // 16
    for rank in range(16):
        piece = table[rank // 4, rank % 4].astype(f32)
        table_ref[:, rank * shard : (rank + 1) * shard] = piece[:, :shard]
        long_ref[:, rank * long_span : (rank + 1) * long_span] = piece[:, :long_span]
    weights = [w[unit].reshape(width, width) for unit in range(3)]
    tokens = jnp.concatenate([own_tok[...], oth_tok[...]], axis=0)
    lanes = [side_lanes(info, side, half) for side in range(2)]
    query = mm(own_tok[...], weights[0])
    for side in range(2):
        q_ref[:, lanes[side]] = (query[:, cuts[side]] + table_ref[0:1, lanes[side]]).astype(bf16)
    for out, weight, row in ((k_ref, weights[1], None), (v_ref, weights[2], 1)):
        value = mm(tokens, weight)
        for side in range(2):
            piece = value[:, cuts[side]]
            if row is not None:
                piece = piece + table_ref[row : row + 1, lanes[side]]
            piece = piece.astype(bf16)
            for index in range(4):
                where = core if index < 2 else 1 - core
                out[index % 2, where, :, lanes[side]] = piece[index * block_len : (index + 1) * block_len]


def project(info, own_tok, oth_tok, own, oth, block_len, long_size):
    rows, width = own_tok.shape
    shard = width // 16
    q_shape = struct((rows, width), bf16)
    k_shape = struct((2, 2, block_len, width), bf16)
    shapes = [
        q_shape,
        k_shape,
        k_shape,
        struct((3, 4, 4, shard, width), bf16),
        struct((16, width), f32),
        struct((16, 16 * long_size), f32),
    ]
    q, k, v, w, table, long = pl.pallas_call(
        project_kernel,
        out_shape=shapes,
        grid_spec=pltpu.PrefetchScalarGridSpec(
            num_scalar_prefetch=1,
            grid=(1,),
            in_specs=[whole_block(own_tok)] * 2 + [ANY] * 10,
            out_specs=[whole_block(s) for s in shapes],
            scratch_shapes=[
                pltpu.VMEM((4, 4, 16, width // 2), bf16),
                pltpu.SemaphoreType.DMA((40,)),
            ],
        ),
        compiler_params=params(),
        cost_estimate=cost(10 * rows * width * width, 20 * rows * width + 12 * width * width),
        name="project",
    )(info, own_tok, oth_tok, *own, *oth)
    w = w.reshape(3, width, width)
    return q, k.reshape(2 * rows, width), v.reshape(2 * rows, width), w, table, long


def normalize(total):
    center = total - jnp.mean(total, axis=-1, keepdims=True)
    inverse = lax.rsqrt(jnp.mean(center * center, axis=-1, keepdims=True) + EPSILON)
    return center * inverse, inverse


def normalize_back(grad, normed, inverse):
    mean_grad = jnp.mean(grad, axis=-1, keepdims=True)
    mean_cross = jnp.mean(grad * normed, axis=-1, keepdims=True)
    return inverse * (grad - mean_grad - normed * mean_cross)


def gelu_parts(value):
    size = jnp.abs(value)
    near = 1.0 / (1.0 + (0.3275911 * 0.7071067811865476) * size)
    series = 0.5 * 1.061405429
    for factor in (-1.453152027, 1.421413741, -0.284496736, 0.254829592):
        series = series * near + 0.5 * factor
    bell = jnp.exp2((-0.5 * 1.4426950408889634) * (value * value))
    tail = series * near * bell
    active = jnp.maximum(value, 0.0) - size * tail
    below = jnp.where(value >= 0.0, 1.0 - tail, tail)
    return active, below + value * (bell * 0.3989422804014327)


def put_table(stage, start, sums, count, long_row=None):
    shard = sums.shape[1] // 16
    cols = stage.shape[4]
    low = sums[0:8, :]
    row = lax.broadcasted_iota(jnp.int32, (16, cols), 0)
    for rank in range(16):
        part = low[:, rank * shard : (rank + 1) * shard]
        part = jnp.pad(part, ((0, 8), (0, cols - shard)))
        table = jnp.where(row < count, part, 0.0)
        if long_row is not None:
            at = long_row + rank // 4
            span = sums.shape[1] // 4
            long = sums[at : at + 1, rank % 4 * span : (rank % 4 + 1) * span]
            table = jnp.where(row == count, jnp.pad(long, ((0, 0), (0, cols - span))), table)
        table = table.astype(bf16)
        for side in range(2):
            stage[side, rank // 4, rank % 4, start : start + 16, :] = table


def term_slots(outs, side):
    first, rest = outs[2 * side : 2 * side + 2]
    return [first, rest.at[0], rest.at[1], rest.at[2]]


def chunk_pieces(refs, rows_at, which):
    if which == "c":
        return [(refs[0], 0), (refs[1], 0), (refs[2], 0), (refs[3], 0), (refs[4], 0)]
    low = rows_at["rows_c"] - rows_at["cut_c"]
    return [(refs[5], 0), (refs[4], low), (refs[3], rows_at["cut_c"]), (refs[6], 0), (refs[7], 0)]


def feed_kernel(
    ctx_size, rows_at, info, mix, tok, teacher, table, long_table, *refs
):
    count_in = 12
    own, oth = refs[:count_in], refs[count_in : 2 * count_in]
    (
    out_ref, gs_ref, gm_ref, *terms, wc, wd, act, slope, value_ref, first, norm, inv, low, acc, go, stage_d, stage_c, sum_ref, sem,
    ) = refs[2 * count_in :]
    square_ref, *terms = terms
    terms_d, terms_c = terms[:4], terms[4:]
    core, plane = info[0], info[1]
    b_inner = long_table.at[pl.ds(rows_at["long"], 1)]
    units, rows_all, width = act.shape
    half = width // 2
    shard = width // 16
    block_len = rows_all // 2
    tile = 64
    tiles = [slice(start, start + tile) for start in range(0, rows_all, tile)]
    lanes = [side_lanes(info, side, half) for side in range(2)]
    cuts = [slice(0, half), slice(half, width)]
    count = [0]

    def start(source, dest):
        copy = pltpu.make_async_copy(source, dest, sem.at[count[0]])
        count[0] += 1
        copy.start()
        return copy

    def wait(copies):
        for copy in copies:
            copy.wait()

    def vector(index):
        row = rows_at[index]
        return table[row : row + 1, :]

    def unit_rows(side, unit):
        where = core if side == 0 else 1 - core
        return pl.ds(pl.multiple_of((where * units + unit) * half, LANES), half)

    def unit_parts(pieces, unit):
        split = units // 2
        if split <= unit < units:
            return piece_parts(
                chunk_pieces(pieces, rows_at, "d"), rows_at["cut_d"], plane, (unit - split) * shard, shard
            )
        at = split if unit == units else unit
        return piece_parts(chunk_pieces(pieces, rows_at, "c"), rows_at["cut_c"], plane, at * shard, shard)

    load_c = {}
    for unit in [units] + list(range(units)):
        load_c[unit] = [
            start(source, wc.at[unit, :, where, pl.ds(first_row, rows), cuts[side]])
            for side, pieces in enumerate((own, oth))
            for source, where, first_row, rows in unit_parts(pieces, unit)
        ]
    deep_d = rows_at["deep_d"]
    load_d = [
        start(source, wd.at[:, where, pl.ds(first_row, rows), cuts[side]])
        for side, pieces in enumerate((own, oth))
        for source, where, first_row, rows in piece_parts(
            chunk_pieces(pieces, rows_at, "d"), rows_at["cut_d"], plane, units // 2 * shard, deep_d
        )
    ]
    rest = pl.ds(deep_d, wd.shape[2] - deep_d)
    for side, pieces in enumerate((own, oth)):
        layers = pieces[8:12]
        load_d += [start(ref, wd.at[info[3] ^ i, :, rest, cuts[side]]) for i, ref in enumerate(layers)]

    def outer_unit(unit):
        ranks = half // wd.shape[2]
        blocks = []
        for side in range(2):
            where = core if side == 0 else 1 - core
            for index in range(ranks):
                rank = (where * units + unit) * ranks + index
                blocks.append(wd[rank // 4, rank % 4])
        return jnp.concatenate(blocks, axis=0)

    wait(load_c[units])
    value = mm(mix[...], wc[units].reshape(width, width))
    for side in range(2):
        acc[:, lanes[side]] = value[:, cuts[side]]
    for rows in tiles:
        normed, inverse = normalize(tok[rows, :].astype(f32) + (acc[rows, :] + vector("bo")))
        total = normed * vector("gain_one") + vector("shift_one")
        norm[rows, :] = normed
        inv[rows, :] = jnp.broadcast_to(inverse, (tile, LANES))
        first[rows, :] = total
        low[rows, :] = total.astype(bf16)

    for unit in range(units + 1):
        if unit < units:
            wait(load_c[unit])
        for part in range(2):
            block = slice(part * block_len, (part + 1) * block_len)
            if unit < units:
                value = mm(low[block, :], wc[unit].reshape(width, width))
                for side in range(2):
                    where = core if side == 0 else 1 - core
                    column = pl.ds(pl.multiple_of((where * units + unit) * half, LANES), half)
                    value_ref[unit % 2, block, cuts[side]] = value[:, cuts[side]] + b_inner[:, column]
            if unit > 0:
                for rows in [slice(at, at + 32) for at in range(block.start, block.stop, 32)]:
                    active, steep = gelu_parts(value_ref[(unit - 1) % 2, rows, :])
                    act[unit - 1, rows, :] = active.astype(bf16)
                    slope[unit - 1, rows, :] = steep.astype(bf16)
    value = None
    wait(load_d)
    for unit in range(units):
        term = mm(act[unit], outer_unit(unit))
        value = term if value is None else value + term
    for side in range(2):
        acc[:, lanes[side]] = value[:, cuts[side]]

    valid_total = jnp.sum(
        vector("count") * 32.0 + table[rows_at["count"] + 1 : rows_at["count"] + 2, :], axis=-1, keepdims=True
    )
    factor = rows_at["scale"] * shard / (valid_total * width)
    sums = [jnp.zeros((8, width), f32) for _ in range(4)]
    for rows in tiles:
        part, inside = divmod(rows.start, block_len)
        base = (core if part == 0 else 2 * ctx_size - 1 - core) * block_len + inside
        position = lax.broadcasted_iota(jnp.int32, (tile, 1), 0) + base
        valid = (position < info[2]).astype(f32)
        normed, inverse = normalize(first[rows, :] + (acc[rows, :] + vector("b_outer")))
        result = normed * vector("gain_two") + vector("shift_two")
        out_ref[rows, :] = result.astype(bf16)
        error = (result - teacher[rows, :].astype(f32)) * valid
        grad_result = error * factor
        grad_sum = normalize_back(grad_result * vector("gain_two"), normed, inverse)
        grad_low = grad_sum.astype(bf16)
        acc[rows, :] = grad_sum
        go[rows, :] = grad_low
        terms = (grad_result * normed, grad_result, grad_low.astype(f32), error * error)
        for index, term in enumerate(terms):
            sums[index] = sums[index] + jnp.sum(term.reshape(tile // 8, 8, width), axis=0)
    for index in range(4):
        sum_ref[index : index + 1, :] = jnp.sum(sums[index], axis=0, keepdims=True)
    loss_part = jnp.sum(sum_ref[3:4, :], axis=-1, keepdims=True) * shard / (valid_total * width)
    square_ref[...] = jnp.broadcast_to(loss_part, (8, LANES))

    grad = by_sides(go, info, half)

    def put_c(term, unit):
        term = term.astype(bf16)
        rows = slice(unit * shard, (unit + 1) * shard)
        for side in range(2):
            stage_c[side, :, :, rows, :] = term[:, cuts[side]].reshape(4, 4, shard, half)

    def send(stage, outs):
        return [
            start(stage.at[side, :, plane ^ offset], dest)
            for side in (1, 0)
            for offset, dest in zip((3, 1, 2, 0), term_slots(outs, side))
        ]

    for unit in range(units):
        term = mm_tn(act[unit], grad).astype(bf16)
        deep = stage_d.shape[3]
        for side in range(2):
            where = core if side == 0 else 1 - core
            for index in range(half // deep):
                rank = (where * units + unit) * (half // deep) + index
                rows = slice(side * half + index * deep, side * half + (index + 1) * deep)
                for col in range(2):
                    stage_d[col, rank // 4, rank % 4] = term[rows, cuts[col]]
    sent = send(stage_d, terms_d)
    for unit in range(units):
        grad_active = mm_nt(grad, outer_unit(unit))
        grad_inner = (grad_active * slope[unit].astype(f32)).astype(bf16)
        slope[unit] = grad_inner
        total = jnp.sum(grad_inner.astype(f32), axis=0, keepdims=True)
        for side in range(2):
            column = (core if side == 0 else 1 - core) * units + unit
            at = pl.ds(pl.multiple_of((column % 2) * half, LANES), half)
            sum_ref[pl.ds(8 + column // 2, 1), at] = total[:, cuts[side]]
        put_c(mm_tn(low[...], slope[unit]), unit)
        acc[...] += mm_nt(slope[unit], wc[unit].reshape(width, width))

    sums = [jnp.zeros((8, width), f32) for _ in range(3)]
    for rows in tiles:
        normed, grad_first = norm[rows, :], acc[rows, :]
        grad_sum = normalize_back(grad_first * vector("gain_one"), normed, inv[rows, 0:1])
        grad_low = grad_sum.astype(bf16)
        gs_ref[rows, :] = grad_sum
        go[rows, :] = grad_low
        terms = (grad_first * normed, grad_first, grad_low.astype(f32))
        for index, term in enumerate(terms):
            sums[index] = sums[index] + jnp.sum(term.reshape(tile // 8, 8, width), axis=0)
    for index in range(3):
        sum_ref[4 + index : 5 + index, :] = jnp.sum(sums[index], axis=0, keepdims=True)
    grad = by_sides(go, info, half)
    put_c(mm_tn(mix[...], grad), units)
    put_table(stage_c, (units + 1) * shard, sum_ref, 7, 8)
    sent += send(stage_c, terms_c)
    gm_ref[...] = mm_nt(grad, wc[units].reshape(width, width)).astype(bf16)
    wait(sent)


def feed(info, mix, tok, teacher, table, long_table, own, oth, rows_at, ctx_size):
    rows, width = tok.shape
    half, units = width // 2, long_table.shape[1] // width
    shapes = [
        struct((rows, width), bf16),
        struct((rows, width), f32),
        struct((rows, width), bf16),
        struct((8, LANES), f32),
    ]
    deep = units * width // 16
    terms = []
    for size in (deep, width // 16 * (units + 1) + 16):
        terms += [struct((4, size, half), bf16), struct((3, 4, size, half), bf16)] * 2
    blocks = (mix, tok, teacher, table, long_table)
    flops = 2 * rows * width * (6 * units + 3) * width
    return pl.pallas_call(
        functools.partial(feed_kernel, ctx_size, rows_at),
        out_shape=shapes + terms,
        grid_spec=pltpu.PrefetchScalarGridSpec(
            num_scalar_prefetch=1,
            grid=(1,),
            in_specs=[whole_block(a) for a in blocks] + [ANY] * 24,
            out_specs=[whole_block(s) for s in shapes] + [ANY] * 8,
            scratch_shapes=[
                pltpu.VMEM((units + 1, 4, 4, width // 16, width), bf16),
                pltpu.VMEM((4, 4, deep, width), bf16),
                pltpu.VMEM((units, rows, width), bf16),
                pltpu.VMEM((units, rows, width), bf16),
                pltpu.VMEM((2, rows, width), f32),
                pltpu.VMEM((rows, width), f32),
                pltpu.VMEM((rows, width), f32),
                pltpu.VMEM((rows, LANES), f32),
                pltpu.VMEM((rows, width), bf16),
                pltpu.VMEM((rows, width), f32),
                pltpu.VMEM((rows, width), bf16),
                pltpu.VMEM((2, 4, 4, deep, half), bf16),
                pltpu.VMEM((2, 4, 4, width // 16 * (units + 1) + 16, half), bf16),
                pltpu.VMEM((16, width), f32),
                pltpu.SemaphoreType.DMA((12 * units + 60,)),
            ],
        ),
        compiler_params=params(),
        cost_estimate=cost(flops, 30 * width * width, 2 * rows * width * units),
        name="feed",
    )(info, *blocks, *own, *oth)


def slot_rows(ref, core, lanes):
    return jnp.concatenate(
        [ref[part, where, :, lanes] for where in (core, 1 - core) for part in range(2)], axis=0
    )


def token_back_kernel(info, own_tok, oth_tok, gq, gk, gv, gs_in, w_in, own_ref, send_ref, *refs):
    outs, stage, sum_ref, gs_one, w, sem = refs[:4], refs[4], refs[5], refs[6], refs[7], refs[8]
    late = [
        pltpu.make_async_copy(gs_in, gs_one, sem.at[8]),
        pltpu.make_async_copy(w_in, w, sem.at[9]),
    ]
    for copy in late:
        copy.start()
    core, plane = info[0], info[1]
    width = own_tok.shape[1]
    half, shard = width // 2, width // 16
    tokens = jnp.concatenate([own_tok[...], oth_tok[...]], axis=0)

    def put(term, index):
        term = term.astype(bf16)
        rows = slice(index * shard, (index + 1) * shard)
        for side in range(2):
            cut = slice(side * half, (side + 1) * half)
            stage[side, :, :, rows, :] = term[:, cut].reshape(4, 4, shard, half)

    for index, grad in ((1, gk), (2, gv)):
        left = [slot_rows(grad, core, side_lanes(info, side, half)) for side in range(2)]
        put(mm_tn(tokens, jnp.concatenate(left, axis=1)), index)
    put(mm_tn(own_tok[...], by_sides(gq, info, half)), 0)
    sum_ref[0:1, :] = jnp.sum(gq[...].astype(f32), axis=0, keepdims=True)
    total = jnp.zeros((1, width), f32)
    for part in range(2):
        for where in range(2):
            total = total + jnp.sum(gv[part, where].astype(f32), axis=0, keepdims=True)
    sum_ref[1:2, :] = total
    put_table(stage, 3 * shard, sum_ref, 2)
    copies = []
    for side in (1, 0):
        for offset, dest in zip((3, 1, 2, 0), term_slots(outs, side)):
            copy = pltpu.make_async_copy(
                stage.at[side, :, plane ^ offset], dest, sem.at[len(copies)]
            )
            copy.start()
            copies.append(copy)
    rows = own_tok.shape[0]
    for copy in late:
        copy.wait()
    both = None
    for grad, weight in ((gk, w[1]), (gv, w[2])):
        left = [slot_rows(grad, core, side_lanes(info, side, half)) for side in range(2)]
        part = mm_nt(jnp.concatenate(left, axis=1), weight)
        both = part if both is None else both + part
    query = mm_nt(by_sides(gq, info, half), w[0])
    own_ref[...] = gs_one[...] + query + both[:rows]
    send_ref[...] = both[rows:].astype(bf16)
    for copy in copies:
        copy.wait()


def token_back(info, own_tok, oth_tok, gq, gk, gv, gs_one, w):
    rows, width = own_tok.shape
    deep, half = 3 * width // 16 + 16, width // 2
    args = (own_tok, oth_tok, gq, gk, gv, gs_one, w)
    shapes = [struct((rows, width), f32), struct((rows, width), bf16)]
    return pl.pallas_call(
        token_back_kernel,
        out_shape=shapes + [struct((4, deep, half), bf16), struct((3, 4, deep, half), bf16)] * 2,
        grid_spec=pltpu.PrefetchScalarGridSpec(
            num_scalar_prefetch=1,
            grid=(1,),
            in_specs=[whole_block(a) for a in args[:5]] + [ANY] * 2,
            out_specs=[whole_block(s) for s in shapes] + [ANY] * 4,
            scratch_shapes=[
                pltpu.VMEM((2, 4, 4, deep, half), bf16),
                pltpu.VMEM((8, width), f32),
                pltpu.VMEM(gs_one.shape, f32),
                pltpu.VMEM(w.shape, bf16),
                pltpu.SemaphoreType.DMA((10,)),
            ],
        ),
        compiler_params=params(),
        cost_estimate=cost(20 * rows * width * width, 40 * rows * width),
        name="token_back",
    )(info, *args)


def layout_positions(block_len, ctx_size, slot_index):
    within = jnp.arange(block_len, dtype=jnp.int32)
    front_pos = slot_index * block_len + within
    back_pos = (2 * ctx_size - 1 - slot_index) * block_len + within
    return (front_pos, back_pos)


def norm_forward(activation):
    center = activation - jnp.mean(activation, axis=-1, keepdims=True)
    inverse = lax.rsqrt(jnp.mean(center * center, axis=-1, keepdims=True) + EPSILON)
    return (center * inverse, inverse)


def norm_backward(grad_normed, normed, inverse):
    mean_grad = jnp.mean(grad_normed, axis=-1, keepdims=True)
    mean_cross = jnp.mean(grad_normed * normed, axis=-1, keepdims=True)
    return inverse * (grad_normed - mean_grad - normed * mean_cross)


def weight_grad(left, right):
    return lax.dot_general(
        left, right, (((0,), (0,)), ((), ())), preferred_element_type=jnp.float32
    )


def back_product(left, right):
    return lax.dot_general(
        left, right, (((1,), (1,)), ((), ())), preferred_element_type=jnp.float32
    )


def gelu_exact(inputs):
    return jax.nn.gelu(inputs, approximate=False)


def column_sum(matrix):
    return jnp.sum(matrix.astype(jnp.float32), axis=0)


def local_plain(
    tokens,
    prev_logits,
    teacher,
    lengths,
    w_query,
    w_key,
    w_value,
    w_output,
    w_inner,
    w_outer,
    bias_query,
    bias_value,
    bias_output,
    attn_gain,
    attn_shift,
    inner_bias,
    outer_bias,
    ffn_gain,
    ffn_shift,
):
    f32 = jnp.float32
    bf16 = jnp.bfloat16
    ctx_size = lax.axis_size("ctx")
    ctx_rank = lax.axis_index("ctx")
    dp_size = lax.axis_size("dp")
    groups = tokens.shape[0]
    block_len = tokens.shape[3]
    model_width = tokens.shape[4]
    head_count = prev_logits.shape[1]
    seq_len = prev_logits.shape[-1]
    head_dim = model_width // head_count
    local_rows = 2 * block_len
    total_rows = groups * local_rows
    score_scale = head_dim ** (-0.5)
    (
        query_matrix,
        key_matrix,
        value_matrix,
        output_matrix,
        query_add,
        value_add,
        output_add,
        first_gain,
        first_shift,
    ) = (
        lax.all_gather(w_query, "dp", axis=0, tiled=True),
        lax.all_gather(w_key, "dp", axis=0, tiled=True),
        lax.all_gather(w_value, "dp", axis=0, tiled=True),
        lax.all_gather(w_output, "dp", axis=0, tiled=True),
        lax.all_gather(bias_query, "dp", axis=0, tiled=True),
        lax.all_gather(bias_value, "dp", axis=0, tiled=True),
        lax.all_gather(bias_output, "dp", axis=0, tiled=True),
        lax.all_gather(attn_gain, "dp", axis=0, tiled=True),
        lax.all_gather(attn_shift, "dp", axis=0, tiled=True),
    )
    token_rows = tokens.reshape(total_rows, model_width)
    queries = (
        jnp.dot(token_rows, query_matrix, preferred_element_type=f32) + query_add.astype(f32)
    ).astype(bf16)
    key_rows = jnp.dot(token_rows, key_matrix, preferred_element_type=f32).astype(bf16)
    values = (
        jnp.dot(token_rows, value_matrix, preferred_element_type=f32) + value_add.astype(f32)
    ).astype(bf16)
    key_blocks, value_blocks = (
        lax.all_gather(
            key_rows.reshape(groups, 2, 1, block_len, model_width), "ctx", axis=2, tiled=True
        ),
        lax.all_gather(
            values.reshape(groups, 2, 1, block_len, model_width), "ctx", axis=2, tiled=True
        ),
    )
    inner_matrix, outer_matrix, inner_add, outer_add, second_gain, second_shift = (
        lax.all_gather(w_inner, "dp", axis=0, tiled=True),
        lax.all_gather(w_outer, "dp", axis=0, tiled=True),
        lax.all_gather(inner_bias, "dp", axis=0, tiled=True),
        lax.all_gather(outer_bias, "dp", axis=0, tiled=True),
        lax.all_gather(ffn_gain, "dp", axis=0, tiled=True),
        lax.all_gather(ffn_shift, "dp", axis=0, tiled=True),
    )
    front_pos, back_pos = layout_positions(block_len, ctx_size, ctx_rank)
    query_pos = jnp.stack([front_pos, back_pos]).reshape(local_rows)
    key_front, key_back = layout_positions(
        block_len, ctx_size, jnp.arange(ctx_size, dtype=jnp.int32)[:, None]
    )
    key_pos = jnp.stack([key_front, key_back]).reshape(seq_len)
    allowed = (key_pos[None, None, :] <= query_pos[None, :, None]) & (
        key_pos[None, None, :] < lengths[:, None, None]
    )
    valid_rows = (query_pos[None, :] < lengths[:, None]).astype(f32).reshape(total_rows)
    query_heads = queries.reshape(groups, local_rows, head_count, head_dim).transpose(2, 0, 1, 3)
    key_heads = key_blocks.reshape(groups, seq_len, head_count, head_dim).transpose(2, 0, 1, 3)
    value_heads = value_blocks.reshape(groups, seq_len, head_count, head_dim).transpose(2, 0, 1, 3)
    prev_rows = prev_logits.reshape(groups, head_count, local_rows, seq_len)

    def scores_of(head_id):
        raw_scores = (
            jnp.einsum(
                "grd,gkd->grk", query_heads[head_id], key_heads[head_id], preferred_element_type=f32
            )
            * score_scale
        )
        raw_scores = raw_scores + lax.dynamic_index_in_dim(
            prev_rows, head_id, 1, keepdims=False
        ).astype(f32)
        return (raw_scores, jnp.where(allowed, raw_scores, NEG_BIG))

    def attend(head_id):
        raw_scores, masked = scores_of(head_id)
        row_max = jnp.max(masked, axis=-1, keepdims=True)
        exponent = jnp.exp(masked - row_max)
        row_total = jnp.sum(exponent, axis=-1, keepdims=True)
        probability = (exponent / row_total).astype(bf16)
        mixed_part = jnp.einsum(
            "grk,gkd->grd", probability, value_heads[head_id], preferred_element_type=f32
        )
        return (mixed_part, row_max[..., 0] + jnp.log(row_total[..., 0]), raw_scores.astype(bf16))

    mixed_heads, log_totals, raw_heads = lax.map(attend, jnp.arange(head_count))
    raw_logits = jnp.moveaxis(raw_heads, 0, 1).reshape(prev_logits.shape)
    mixed_rows = mixed_heads.transpose(1, 2, 0, 3).reshape(total_rows, model_width).astype(bf16)
    attn_out = jnp.dot(mixed_rows, output_matrix, preferred_element_type=f32) + output_add.astype(
        f32
    )
    first_normed, first_inverse = norm_forward(token_rows.astype(f32) + attn_out)
    first = first_normed * first_gain.astype(f32) + first_shift.astype(f32)
    first_low = first.astype(bf16)
    inner_pre = jnp.dot(first_low, inner_matrix, preferred_element_type=f32) + inner_add.astype(f32)
    active, gelu_back = jax.vjp(gelu_exact, inner_pre)
    active_low = active.astype(bf16)
    outer_pre = jnp.dot(active_low, outer_matrix, preferred_element_type=f32) + outer_add.astype(
        f32
    )
    second_normed, second_inverse = norm_forward(first + outer_pre)
    result = second_normed * second_gain.astype(f32) + second_shift.astype(f32)
    errors = (result - teacher.reshape(total_rows, model_width).astype(f32)) * valid_rows[:, None]
    square_sum, valid_total = lax.psum(
        (jnp.sum(errors * errors), jnp.sum(valid_rows)), ("dp", "ctx")
    )
    loss_value = square_sum / (valid_total * model_width)
    loss_scale = dp_size * groups * seq_len * model_width / 2.0
    grad_result = errors * (loss_scale * 2.0 / (valid_total * model_width))
    grad_second_gain = jnp.sum(grad_result * second_normed, axis=0)
    grad_second_shift = jnp.sum(grad_result, axis=0)
    grad_sum_two = norm_backward(
        grad_result * second_gain.astype(f32), second_normed, second_inverse
    )
    grad_outer = grad_sum_two.astype(bf16)
    grad_outer_matrix = weight_grad(active_low, grad_outer)
    grad_outer_add = column_sum(grad_outer)
    grad_active = back_product(grad_outer, outer_matrix)
    grad_inner = gelu_back(grad_active)[0].astype(bf16)
    grad_inner_matrix = weight_grad(first_low, grad_inner)
    grad_inner_add = column_sum(grad_inner)
    grad_first = grad_sum_two + back_product(grad_inner, inner_matrix)
    grad_first_gain = jnp.sum(grad_first * first_normed, axis=0)
    grad_first_shift = jnp.sum(grad_first, axis=0)
    grad_sum_one = norm_backward(grad_first * first_gain.astype(f32), first_normed, first_inverse)
    grad_attn = grad_sum_one.astype(bf16)
    grad_output_matrix = weight_grad(mixed_rows, grad_attn)
    grad_output_add = column_sum(grad_attn)
    grad_mixed = back_product(grad_attn, output_matrix).astype(bf16)
    grad_mixed_heads = grad_mixed.reshape(groups, local_rows, head_count, head_dim).transpose(
        2, 0, 1, 3
    )

    def attend_back(head_id):
        _, masked = scores_of(head_id)
        probability = jnp.exp(masked - log_totals[head_id][..., None])
        grad_part = grad_mixed_heads[head_id]
        grad_value_part = jnp.einsum(
            "grk,grd->gkd", probability.astype(bf16), grad_part, preferred_element_type=f32
        )
        grad_probs = jnp.einsum(
            "grd,gkd->grk", grad_part, value_heads[head_id], preferred_element_type=f32
        )
        row_dot = jnp.sum(probability * grad_probs, axis=-1, keepdims=True)
        grad_scores = (probability * (grad_probs - row_dot)).astype(bf16)
        grad_query_part = (
            jnp.einsum("grk,gkd->grd", grad_scores, key_heads[head_id], preferred_element_type=f32)
            * score_scale
        )
        grad_key_part = (
            jnp.einsum(
                "grk,grd->gkd", grad_scores, query_heads[head_id], preferred_element_type=f32
            )
            * score_scale
        )
        return (grad_scores, grad_query_part, grad_key_part, grad_value_part)

    grad_score_heads, grad_query_heads, grad_key_heads, grad_value_heads = lax.map(
        attend_back, jnp.arange(head_count)
    )
    grad_logits = jnp.moveaxis(grad_score_heads, 0, 1).reshape(prev_logits.shape)
    grad_queries = (
        grad_query_heads.transpose(1, 2, 0, 3).reshape(total_rows, model_width).astype(bf16)
    )
    key_terms = grad_key_heads.transpose(1, 2, 0, 3).reshape(
        groups, 2, ctx_size, block_len, model_width
    )
    value_terms = grad_value_heads.transpose(1, 2, 0, 3).reshape(
        groups, 2, ctx_size, block_len, model_width
    )
    key_sums, value_sums = (
        lax.psum_scatter(
            key_terms.astype(jnp.bfloat16), "ctx", scatter_dimension=2, tiled=True
        ).astype(jnp.float32),
        lax.psum_scatter(
            value_terms.astype(jnp.bfloat16), "ctx", scatter_dimension=2, tiled=True
        ).astype(jnp.float32),
    )
    grad_keys = key_sums.reshape(total_rows, model_width).astype(bf16)
    grad_values = value_sums.reshape(total_rows, model_width).astype(bf16)
    grad_query_matrix = weight_grad(token_rows, grad_queries)
    grad_key_matrix = weight_grad(token_rows, grad_keys)
    grad_value_matrix = weight_grad(token_rows, grad_values)
    grad_query_add = column_sum(grad_queries)
    grad_value_add = column_sum(grad_values)
    grad_token_rows = (
        grad_sum_one
        + back_product(grad_queries, query_matrix)
        + back_product(grad_keys, key_matrix)
        + back_product(grad_values, value_matrix)
    )
    matrix_grads = (
        grad_query_matrix,
        grad_key_matrix,
        grad_value_matrix,
        grad_output_matrix,
        grad_inner_matrix,
        grad_outer_matrix,
    )
    vector_grads = (
        grad_query_add,
        grad_value_add,
        grad_output_add,
        grad_first_gain,
        grad_first_shift,
        grad_inner_add,
        grad_outer_add,
        grad_second_gain,
        grad_second_shift,
    )
    summed = (
        lax.psum_scatter(
            matrix_grads[0].astype(jnp.bfloat16), "dp", scatter_dimension=0, tiled=True
        ).astype(jnp.float32),
        lax.psum_scatter(
            matrix_grads[1].astype(jnp.bfloat16), "dp", scatter_dimension=0, tiled=True
        ).astype(jnp.float32),
        lax.psum_scatter(
            matrix_grads[2].astype(jnp.bfloat16), "dp", scatter_dimension=0, tiled=True
        ).astype(jnp.float32),
        lax.psum_scatter(
            matrix_grads[3].astype(jnp.bfloat16), "dp", scatter_dimension=0, tiled=True
        ).astype(jnp.float32),
        lax.psum_scatter(
            matrix_grads[4].astype(jnp.bfloat16), "dp", scatter_dimension=0, tiled=True
        ).astype(jnp.float32),
        lax.psum_scatter(
            matrix_grads[5].astype(jnp.bfloat16), "dp", scatter_dimension=0, tiled=True
        ).astype(jnp.float32),
        lax.psum_scatter(
            vector_grads[0].astype(jnp.bfloat16), "dp", scatter_dimension=0, tiled=True
        ).astype(jnp.float32),
        lax.psum_scatter(
            vector_grads[1].astype(jnp.bfloat16), "dp", scatter_dimension=0, tiled=True
        ).astype(jnp.float32),
        lax.psum_scatter(
            vector_grads[2].astype(jnp.bfloat16), "dp", scatter_dimension=0, tiled=True
        ).astype(jnp.float32),
        lax.psum_scatter(
            vector_grads[3].astype(jnp.bfloat16), "dp", scatter_dimension=0, tiled=True
        ).astype(jnp.float32),
        lax.psum_scatter(
            vector_grads[4].astype(jnp.bfloat16), "dp", scatter_dimension=0, tiled=True
        ).astype(jnp.float32),
        lax.psum_scatter(
            vector_grads[5].astype(jnp.bfloat16), "dp", scatter_dimension=0, tiled=True
        ).astype(jnp.float32),
        lax.psum_scatter(
            vector_grads[6].astype(jnp.bfloat16), "dp", scatter_dimension=0, tiled=True
        ).astype(jnp.float32),
        lax.psum_scatter(
            vector_grads[7].astype(jnp.bfloat16), "dp", scatter_dimension=0, tiled=True
        ).astype(jnp.float32),
        lax.psum_scatter(
            vector_grads[8].astype(jnp.bfloat16), "dp", scatter_dimension=0, tiled=True
        ).astype(jnp.float32),
    )
    reduced = (
        lax.psum(summed[0].astype(jnp.bfloat16), "ctx").astype(jnp.float32),
        lax.psum(summed[1].astype(jnp.bfloat16), "ctx").astype(jnp.float32),
        lax.psum(summed[2].astype(jnp.bfloat16), "ctx").astype(jnp.float32),
        lax.psum(summed[3].astype(jnp.bfloat16), "ctx").astype(jnp.float32),
        lax.psum(summed[4].astype(jnp.bfloat16), "ctx").astype(jnp.float32),
        lax.psum(summed[5].astype(jnp.bfloat16), "ctx").astype(jnp.float32),
        lax.psum(summed[6].astype(jnp.bfloat16), "ctx").astype(jnp.float32),
        lax.psum(summed[7].astype(jnp.bfloat16), "ctx").astype(jnp.float32),
        lax.psum(summed[8].astype(jnp.bfloat16), "ctx").astype(jnp.float32),
        lax.psum(summed[9].astype(jnp.bfloat16), "ctx").astype(jnp.float32),
        lax.psum(summed[10].astype(jnp.bfloat16), "ctx").astype(jnp.float32),
        lax.psum(summed[11].astype(jnp.bfloat16), "ctx").astype(jnp.float32),
        lax.psum(summed[12].astype(jnp.bfloat16), "ctx").astype(jnp.float32),
        lax.psum(summed[13].astype(jnp.bfloat16), "ctx").astype(jnp.float32),
        lax.psum(summed[14].astype(jnp.bfloat16), "ctx").astype(jnp.float32),
    )
    return (
        result.astype(bf16).reshape(tokens.shape),
        raw_logits,
        loss_value,
        grad_token_rows.astype(bf16).reshape(tokens.shape),
        grad_logits,
        reduced[0],
        reduced[1],
        reduced[2],
        reduced[3],
        reduced[4],
        reduced[5],
        reduced[6],
        reduced[7],
        reduced[8],
        reduced[9],
        reduced[10],
        reduced[11],
        reduced[12],
        reduced[13],
        reduced[14],
    )


def local_fast(tokens, prev_logits, teacher, lengths, *parameters):
    weights, vectors = parameters[:6], parameters[6:]
    w_outer = weights[5]
    ctx_size = lax.axis_size("ctx")
    core = lax.axis_index("ctx")
    dp_size = lax.axis_size("dp")
    dp_rank = lax.axis_index("dp")
    block_len, width = tokens.shape[3], tokens.shape[4]
    head_count, seq_len = prev_logits.shape[1], prev_logits.shape[-1]
    head_dim = width // head_count
    rows = 2 * block_len
    shard = weights[0].shape[0]
    half = width // 2
    units = weights[4].shape[1] // width
    info = jnp.stack([core, dp_rank % 4, lengths[0], dp_rank // 4]).astype(jnp.int32)
    token_rows = tokens.reshape(rows, width)
    teacher_rows = teacher.reshape(rows, width)
    prev_rows = prev_logits.reshape(head_count, rows, seq_len)
    sizes = (block_len, ctx_size, head_dim)
    pairs = [(i, i) for i in range(head_count * head_dim // LANES)]
    (long_at,) = [i for i, v in enumerate(vectors) if v.shape[0] != shard]
    names = ("bq", "bv", "bo", "gain_one", "shift_one", "long", "b_outer", "gain_two", "shift_two", "count")
    rows_at = {name: i for i, name in enumerate(names)}
    rows_at["scale"] = float(dp_size * seq_len * width)

    chunk_a, chunk_c, chunk_d, chunk_e = pack(info, weights, vectors)
    cut_c, cut_d = split_row(chunk_c.shape[0]), split_row(chunk_d.shape[0])
    rows_at.update(
        rows_c=chunk_c.shape[0], cut_c=cut_c, cut_d=cut_d, deep_d=w_outer.shape[0] - chunk_e.shape[0]
    )
    cross = lambda piece: flip(piece, "ctx", 1)
    parts_a = z_triple(chunk_a)
    parts_e = [chunk_e] + [flip(chunk_e, "dp", step) for step in (1, 2, 3)]
    parts_a, parts_e, token_rows, chunk_c, chunk_d = together(
        parts_a, parts_e, token_rows, chunk_c, chunk_d
    )
    column_a = in_order(dp_rank // 4, parts_a)
    sides_a = side_columns(column_a)
    next_c = flip(chunk_c, "dp", 4)
    other_rows = cross(token_rows)
    pair_c = z_pair(chunk_c, next_c)
    over_c = flip(pair_c, "dp", 8)
    sides_a, other_rows, over_c, chunk_d = together(sides_a, other_rows, over_c, chunk_d)
    corner_a = corner_column(sides_a)
    own_a = [column_a, *sides_a]
    oth_a = [cross(piece) for piece in own_a]
    next_d = flip(chunk_d, "dp", 4)
    corner_a, oth_a, next_d, parts_e = together(corner_a, oth_a, next_d, parts_e)
    oth_a = [*oth_a, *[cross(piece) for piece in corner_a]]
    own_a = [*own_a, *corner_a]
    column_c = z_column(pair_c, over_c)
    sides_c = side_columns(column_c)
    pair_d = z_pair(chunk_d, next_d)
    over_d = flip(pair_d, "dp", 8)
    plane_e = in_order(dp_rank % 4, parts_e)
    next_e = flip(plane_e, "dp", 4)
    oth_e = [cross(plane_e)]
    queries, keys, values, w_attn, table, long_table = project(
        info, token_rows, other_rows, own_a, oth_a, block_len, vectors[long_at].shape[0]
    )
    queries, sides_c, pair_d, over_d, plane_e, next_e, oth_e = together(
        queries, sides_c, pair_d, over_d, plane_e, next_e, oth_e
    )
    column_d = z_column(pair_d, over_d)
    far_up = flip(jnp.concatenate([sides_c[0][:, :cut_c], column_d], axis=1), "dp", 2)
    near_low = flip(jnp.concatenate([sides_c[1][:, cut_c:], column_d], axis=1), "dp", 1)
    over_e = [flip(plane_e, "dp", 8)]
    oth_c = [cross(column_c), cross(sides_c[0])]
    qkv = (queries, keys, values)
    carry = attend(info, qkv, prev_rows, pairs[:4], None, *sizes)
    carry, oth_c, column_d, far_up, near_low, over_e = together(
        carry, oth_c, column_d, far_up, near_low, over_e
    )
    near_d = near_low[:, chunk_c.shape[0] - cut_c :]
    far_d = far_up[:, cut_c:]
    corner_d = [flip(near_d[:, :cut_d], "dp", 2), flip(far_d[:, cut_d:], "dp", 1)]
    over_e.append(flip(next_e, "dp", 8))
    late = [far_up, near_low]
    oth_late = [cross(piece) for piece in late]
    logits, probs, mixed = attend(info, qkv, prev_rows, pairs[4:], carry, *sizes)
    mixed, oth_c, oth_late, corner_d, over_e, column_d, next_e, sides_c = together(
        mixed, oth_c, oth_late, corner_d, over_e, column_d, next_e, sides_c
    )
    own_c = [column_c, *sides_c, far_up, near_low]
    own_d = [column_d, *corner_d, plane_e, next_e, *over_e]
    oth_c += [cross(sides_c[1]), *oth_late]
    oth_d = [cross(piece) for piece in own_d[:3]] + oth_e + [cross(piece) for piece in own_d[4:]]
    result, grad_sum_one, grad_mixed, square, *terms = feed(
        info, mixed, token_rows, teacher_rows, table, long_table,
        [*own_c, *own_d], [*oth_c, *oth_d], rows_at, ctx_size,
    )

    back = lambda some, carry: attend_back(qkv, probs, grad_mixed, some, carry, *sizes)
    kept_d, sent_d, kept_c, sent_c = terms[:2], terms[2:4], terms[4:6], terms[6:8]
    came_d = [cross(sent_d[0])]
    square = square + cross(square)
    sent_d, sent_c, square, came_d, grad_mixed = together(sent_d, sent_c, square, came_d, grad_mixed)
    corner_d = scatter_corner(kept_d[0], came_d[0])
    came_d.append(cross(sent_d[1]))
    came_c = [cross(part) for part in sent_c]
    grads = back(pairs[:2], [])
    grads, corner_d, came_d, came_c, square = together(grads, corner_d, came_d, came_c, square)
    sides_d = send_sides(scatter_sides(kept_d[1], came_d[1], corner_d))
    corner_c = scatter_corner(kept_c[0], came_c[0])
    square = square + flip(square, "dp", 8)
    grad_logits, gq, gk, gv = back(pairs[2:], grads)
    gk, gv = [g.reshape(2, 2, block_len, width) for g in (gk, gv)]
    gq, sides_d, corner_c, square = together(gq, sides_d, corner_c, square)
    sides_c = scatter_sides(kept_c[1], came_c[1], corner_c)
    half_d = scatter_half(kept_d[1], came_d[1], sides_d)
    sides_c, half_d, gq = together(sides_c, half_d, gq)
    sides_c, half_d = send_sides(sides_c), (half_d[0], flip(half_d[1], "dp", 8))
    own_terms, sent_terms, *terms_a = token_back(
        info, token_rows, other_rows, gq, gk, gv, grad_sum_one, w_attn
    )
    own_terms, sent_terms, terms_a, sides_c, half_d = together(
        own_terms, sent_terms, terms_a, sides_c, half_d
    )
    kept_a, sent_a = terms_a[:2], terms_a[2:4]
    came_a = [cross(part) for part in sent_a]
    half_c = scatter_half(kept_c[1], came_c[1], sides_c)
    half_c = (half_c[0], flip(half_c[1], "dp", 8))
    rank_d = scatter_rank(*half_d)
    came_a, rank_d, sent_terms = together(came_a, rank_d, sent_terms)
    corner_a = scatter_corner(kept_a[0], came_a[0])
    total_d = scatter_total(rank_d[0], [rank_d[1]])
    grad_tokens = (own_terms + cross(sent_terms).astype(f32)).astype(bf16)
    corner_a, total_d, grad_tokens = together(corner_a, total_d, grad_tokens)
    sides_a = send_sides(scatter_sides(kept_a[1], came_a[1], corner_a))
    rank_c = scatter_rank(*half_c)
    sides_a, rank_c, square = together(sides_a, rank_c, square)
    triple_a = scatter_triple(kept_a[1], came_a[1], sides_a)
    total_c = scatter_total(rank_c[0], [rank_c[1]])
    square = square + flip(square, "dp", 1)
    square = square + flip(square, "dp", 2)
    triple_a, square, total_c = together(triple_a, square, total_c)
    square = square + flip(square, "dp", 4)
    total_a = scatter_total(*triple_a)
    pair_a, pair_c, pair_d = by_halves(*total_a), by_halves(*total_c), by_halves(*total_d)
    def unit(parts, index):
        return [part[index * shard : (index + 1) * shard] for part in parts]

    grad_w_inner = jnp.concatenate(
        [unit(pair_c[side : side + 1], i)[0] for side in range(2) for i in range(units)], axis=1
    )
    sums_c, sums_a = total_c[0][(units + 1) * shard :].astype(f32), total_a[0][3 * shard :].astype(f32)
    order = (6, 4, 5, None, 2, 0, 1)
    vector_totals = [sums_a[0, :shard], sums_a[1, :shard]]
    vector_totals += [
        sums_c[7, : vectors[long_at].shape[0]] if i is None else sums_c[i, :shard] for i in order
    ]
    return (
        result.reshape(tokens.shape),
        logits.reshape(prev_logits.shape),
        square[0, 0],
        grad_tokens.reshape(tokens.shape),
        grad_logits.reshape(prev_logits.shape),
        *[jnp.concatenate(unit(pair_a, i), axis=1) for i in range(3)],
        jnp.concatenate(unit(pair_c, units), axis=1),
        grad_w_inner,
        jnp.concatenate(pair_d, axis=1),
        *vector_totals,
    )


def local(tokens, prev_logits, teacher, lengths, *parameters):
    width, shard = tokens.shape[-1], parameters[0].shape[0]
    fits = (
        lax.axis_size("dp") == 16
        and lax.axis_size("ctx") == 2
        and tokens.shape[0] == 1
        and shard % 16 == 0
        and width % 256 == 0
    )
    chosen = local_fast if fits else local_plain
    return chosen(tokens, prev_logits, teacher, lengths, *parameters)


def solution(mesh):
    rows = P("dp", None, "ctx", None, None)
    scores = P("dp", None, None, "ctx", None, None)
    matrix, vector = P("dp", None), P("dp")
    return jax.shard_map(
        local,
        mesh=mesh,
        in_specs=(rows, scores, rows, vector) + (matrix,) * 6 + (vector,) * 9,
        out_specs=(rows, scores, P(), rows, scores) + (matrix,) * 6 + (vector,) * 9,
        check_vma=False,
    )
```

```python
import functools

import jax
import jax.numpy as jnp
from jax import lax
from jax.experimental import pallas as pl
from jax.experimental.pallas import tpu as pltpu
from jax.sharding import PartitionSpec as P

EPSILON = 1e-05
NEG_BIG = -1e30
POS_BIG = 3.0e38
LANES = 128
f32 = jnp.float32
bf16 = jnp.bfloat16
ANY = pl.BlockSpec(memory_space=pl.ANY)


def mm(left, right):
    return jnp.dot(left, right, preferred_element_type=f32)


def mm_tn(left, right):
    return lax.dot_general(left, right, (((0,), (0,)), ((), ())), preferred_element_type=f32)


def mm_nt(left, right):
    return lax.dot_general(left, right, (((1,), (1,)), ((), ())), preferred_element_type=f32)


def struct(shape, dtype):
    return jax.ShapeDtypeStruct(shape, dtype)


def params():
    return pltpu.CompilerParams(vmem_limit_bytes=56 << 20)


def cost(flops, bytes_accessed, transcendentals=0):
    return pl.CostEstimate(
        flops=int(flops), bytes_accessed=int(bytes_accessed), transcendentals=int(transcendentals)
    )


def together(*values):
    return lax.optimization_barrier(values)


def after(value, *others):
    return lax.optimization_barrier((value, others))[0]


def whole_block(array):
    rank = len(array.shape)
    return pl.BlockSpec(array.shape, lambda *_: (0,) * rank)


def side_lanes(info, side, width):
    half = info[0] if side == 0 else 1 - info[0]
    return pl.ds(pl.multiple_of(half * width, LANES), width)


def flip(array, axis_name, bit):
    size = lax.axis_size(axis_name)
    return lax.ppermute(array, axis_name, [(i, i ^ bit) for i in range(size)])


def z_bits():
    dp_rank = lax.axis_index("dp")
    return dp_rank // 4 % 2, dp_rank // 8


def z_pair(array, arrived):
    low = z_bits()[0] == 0
    return jnp.stack([jnp.where(low, array, arrived), jnp.where(low, arrived, array)])


def z_column(pair, arrived):
    low = z_bits()[1] == 0
    return jnp.concatenate([jnp.where(low, pair, arrived), jnp.where(low, arrived, pair)])


def z_triple(array):
    return [array] + [flip(array, "dp", 4 * step) for step in (1, 2, 3)]


def in_order(mine, parts):
    return jnp.stack([lax.select_n(mine ^ i, *parts) for i in range(4)])


def side_columns(column):
    return flip(column, "dp", 1), flip(column, "dp", 2)


def corner_column(sides):
    cut = split_row(sides[0].shape[1])
    return flip(sides[0][:, :cut], "dp", 2), flip(sides[1][:, cut:], "dp", 1)


def split_row(rows):
    return rows // 32 * 16


def scatter_corner(kept, arrived):
    cut = split_row(kept.shape[1])
    term = (kept.astype(f32) + arrived.astype(f32)).astype(bf16)
    return flip(term[:, :cut], "dp", 2), flip(term[:, cut:], "dp", 1)


def scatter_sides(kept, arrived, corner):
    upper, lower = [part.astype(f32) for part in corner]
    near = kept[0].astype(f32) + arrived[0].astype(f32)
    far = kept[1].astype(f32) + arrived[1].astype(f32)
    cut = upper.shape[1]
    near = jnp.concatenate([near[:, :cut] + upper, near[:, cut:]], axis=1)
    far = jnp.concatenate([far[:, :cut], far[:, cut:] + lower], axis=1)
    return near.astype(bf16), far.astype(bf16)


def send_sides(sides):
    return flip(sides[0], "dp", 1), flip(sides[1], "dp", 2)


def scatter_half(kept, arrived, sides):
    column = sum(part.astype(f32) for part in (kept[2], arrived[2], *sides))
    column = column.reshape(2, 2, *column.shape[1:])
    high = z_bits()[1]
    pick = lambda half: lax.dynamic_index_in_dim(column, half, 0, keepdims=False)
    return pick(high), pick(1 - high).astype(bf16)


def scatter_rank(kept, arrived):
    column = kept + arrived.astype(f32)
    low = z_bits()[0]
    pick = lambda half: lax.dynamic_index_in_dim(column, half, 0, keepdims=False)
    return pick(low), flip(pick(1 - low).astype(bf16), "dp", 4)


def scatter_triple(kept, arrived, sides):
    mine = lax.axis_index("dp") // 4
    column = sum(part.astype(f32) for part in (kept[2], arrived[2], *sides))
    pick = lambda z: lax.dynamic_index_in_dim(column, z, 0, keepdims=False)
    return pick(mine), [flip(pick(mine ^ step).astype(bf16), "dp", 4 * step) for step in (2, 3, 1)]


def scatter_total(kept, arrived):
    total = kept
    for part in arrived:
        total = total + part.astype(f32)
    total = total.astype(bf16)
    return total, flip(total, "ctx", 1)


def by_halves(total, across):
    core = lax.axis_index("ctx")
    return (
        jnp.where(core == 0, total, across).astype(f32),
        jnp.where(core == 0, across, total).astype(f32),
    )


def pack_kernel(info, *refs):
    vectors, outs = refs[6:-4], refs[-4:]
    half = outs[0].shape[1]
    shard = refs[0].shape[0]
    units = refs[4].shape[1] // (2 * half)
    lanes = side_lanes(info, 0, half)

    def unit(index):
        column = pl.multiple_of((info[0] * units + index) * half, LANES)
        return refs[4][:, pl.ds(column, half)]

    for index in range(3):
        outs[0][index * shard : (index + 1) * shard, :] = refs[index][:, lanes]
    count = units // 2
    for index in range(count):
        rows = slice(index * shard, (index + 1) * shard)
        outs[1][rows, :] = unit(index)
        outs[2][rows, :] = unit(count + index)
    outs[1][count * shard :, :] = refs[3][:, lanes]
    split = refs[5].shape[0] - outs[3].shape[0]
    outs[2][count * shard :, :] = refs[5][:split, lanes]
    outs[3][...] = refs[5][split:, lanes]
    row = lax.broadcasted_iota(jnp.int32, (16, half), 0)
    table = jnp.zeros((16, half), f32)
    for index, ref in enumerate(vectors):
        value = jnp.pad(ref[...].astype(f32), ((0, 0), (0, half - ref.shape[1])))
        table = jnp.where(row == index, value, table)
    table = jnp.where(row == len(vectors), (info[2] // 32).astype(f32), table)
    table = jnp.where(row == len(vectors) + 1, (info[2] % 32).astype(f32), table)
    outs[0][3 * shard :, :] = table.astype(bf16)


def pack(info, weights, vectors):
    shard, width = weights[0].shape
    half, count = width // 2, weights[4].shape[1] // width // 2
    deep = weights[5].shape[0]
    split = deep // 32 * 16
    sizes = (3 * shard + 16, (count + 1) * shard, count * shard + split, deep - split)
    shapes = [struct((size, half), bf16) for size in sizes]
    args = [*weights, *[v[None] for v in vectors]]
    return pl.pallas_call(
        pack_kernel,
        out_shape=shapes,
        grid_spec=pltpu.PrefetchScalarGridSpec(
            num_scalar_prefetch=1,
            grid=(1,),
            in_specs=[whole_block(a) for a in args],
            out_specs=[whole_block(s) for s in shapes],
        ),
        compiler_params=params(),
        cost_estimate=cost(0, 4 * sum(w.size for w in weights)),
        name="pack",
    )(info, *args)


def piece_parts(pieces, cut, plane, start, rows):
    parts = []
    for offset in range(3):
        ref, base = pieces[offset]
        parts.append((ref.at[:, pl.ds(base + start, rows)], plane ^ (0, 1, 2)[offset], 0, rows))
    (upper, base_up), (lower, base_low) = pieces[3:]
    if start < cut:
        count = min(start + rows, cut) - start
        parts.append((upper.at[:, pl.ds(base_up + start, count)], plane ^ 3, 0, count))
    if start + rows > cut:
        skip = max(start, cut)
        count = start + rows - skip
        parts.append((lower.at[:, pl.ds(base_low + skip - cut, count)], plane ^ 3, skip - start, count))
    return parts


def slot_start(slot, ctx_size, block_len):
    half, which = divmod(slot, ctx_size)
    return (which if half == 0 else 2 * ctx_size - 1 - which) * block_len


def head_lanes(which, head_dim):
    lane = lax.broadcasted_iota(jnp.int32, (1, LANES), 1)
    return (lane >= which * head_dim) & (lane < (which + 1) * head_dim)


def attend_kernel(
    block_len, ctx_size, head_dim, info, q_ref, k_ref, v_ref, prev_ref, logit_ref, prob_ref, mix_ref, limit_ref
):
    seq_len = 2 * ctx_size * block_len
    half = ctx_size * block_len
    heads = LANES // head_dim

    @pl.when(pl.program_id(0) == 0)
    def _():
        core, length = info[0], info[2]
        within = lax.broadcasted_iota(jnp.int32, (block_len, block_len), 1)
        row = lax.broadcasted_iota(jnp.int32, (block_len, block_len), 0)
        for part in range(2):
            start = core if part == 0 else 2 * ctx_size - 1 - core
            query_pos = row + start * block_len
            for slot in range(2 * ctx_size):
                key_pos = within + slot_start(slot, ctx_size, block_len)
                allowed = (key_pos <= query_pos) & (key_pos < length)
                limit_ref[
                    part * block_len : (part + 1) * block_len,
                    slot * block_len : (slot + 1) * block_len,
                ] = jnp.where(allowed, POS_BIG, NEG_BIG)

    scale = head_dim ** (-0.5)
    masks = [head_lanes(which, head_dim) for which in range(heads)]
    values = [jnp.where(mask, v_ref[...], 0.0).astype(bf16) for mask in masks]
    scores = []
    for which in range(heads):
        query = jnp.where(masks[which], q_ref[...].astype(f32) * scale, 0.0).astype(bf16)
        scores.append(mm_nt(query, k_ref[...]))
    for part in range(2):
        rows = slice(part * block_len, (part + 1) * block_len)
        keys = half if part == 0 else seq_len
        probabilities = []
        for which in range(heads):
            raw = scores[which][rows, :] + prev_ref[which, rows, :].astype(f32)
            logit_ref[which, rows, :] = raw.astype(bf16)
            masked = jnp.minimum(raw[:, :keys], limit_ref[rows, :keys])
            top = jnp.max(masked, axis=-1, keepdims=True)
            exponent = jnp.exp(masked - top)
            total = jnp.sum(exponent, axis=-1, keepdims=True)
            probability = (exponent * (1.0 / total)).astype(bf16)
            prob_ref[which, rows, :keys] = probability
            probabilities.append(probability)
        mixed = mm(
            jnp.concatenate(probabilities, axis=1),
            jnp.concatenate([value[:keys] for value in values], axis=0),
        )
        mix_ref[rows, :] = mixed.astype(bf16)


def attend_back_kernel(
    block_len, ctx_size, head_dim, q_ref, k_ref, v_ref, prob_ref, gm_ref, gs_ref, gq_ref, gk_ref, gv_ref, gk_sum, gv_sum
):
    seq_len = 2 * ctx_size * block_len
    half = ctx_size * block_len
    heads = LANES // head_dim
    scale = head_dim ** (-0.5)
    masks = [head_lanes(which, head_dim) for which in range(heads)]
    keys_in = [jnp.where(mask, k_ref[...], 0.0).astype(bf16) for mask in masks]
    for part in (1, 0):
        rows = slice(part * block_len, (part + 1) * block_len)
        keys = half if part == 0 else seq_len
        grads, queries, probs, grad_mixes = [], [], [], []
        for which in range(heads):
            grad_mix = jnp.where(masks[which], gm_ref[rows, :], 0.0).astype(bf16)
            prob_low = prob_ref[which, rows, :keys]
            probability = prob_low.astype(f32)
            grad_prob = mm_nt(grad_mix, v_ref[:keys, :])
            term = probability * grad_prob
            row_dot = jnp.sum(term, axis=-1, keepdims=True)
            grad_score = (term - probability * row_dot).astype(bf16)
            gs_ref[which, rows, :keys] = grad_score
            if keys < seq_len:
                gs_ref[which, rows, keys:] = jnp.zeros((block_len, seq_len - keys), bf16)
            grads.append(grad_score)
            queries.append(jnp.where(masks[which], q_ref[rows, :], 0.0).astype(bf16))
            probs.append(prob_low)
            grad_mixes.append(grad_mix)
        grad_value = mm_tn(jnp.concatenate(probs, axis=0), jnp.concatenate(grad_mixes, axis=0))
        grad_key = mm_tn(jnp.concatenate(grads, axis=0), jnp.concatenate(queries, axis=0))
        if part == 1:
            gv_sum[...] = grad_value
            gk_sum[...] = grad_key
        else:
            gv_sum[:keys, :] += grad_value
            gk_sum[:keys, :] += grad_key
        grad_query = mm(
            jnp.concatenate(grads, axis=1), jnp.concatenate([key[:keys] for key in keys_in], axis=0)
        )
        gq_ref[rows, :] = (grad_query * scale).astype(bf16)
    gk_ref[...] = (gk_sum[...] * scale).astype(bf16)
    gv_ref[...] = gv_sum[...].astype(bf16)


def pair_specs(rows, seq_len, heads, places):
    def at(h, which):
        index = places[-1][which]
        for i in range(len(places) - 1):
            index = jnp.where(h == i, places[i][which], index)
        return index

    wide = pl.BlockSpec((heads, rows, seq_len), lambda h, *_: (at(h, 0), 0, 0))
    mixed = pl.BlockSpec((rows, LANES), lambda h, *_: (0, at(h, 0)))
    narrow = pl.BlockSpec((rows, LANES), lambda h, *_: (0, at(h, 1)))
    whole = pl.BlockSpec((seq_len, LANES), lambda h, *_: (0, at(h, 1)))
    return wide, mixed, narrow, whole


def attend(info, qkv, prev, places, carry, block_len, ctx_size, head_dim):
    head_count, rows, seq_len = prev.shape
    heads, count = LANES // head_dim, len(places)
    wide, mixed, narrow, whole = pair_specs(rows, seq_len, heads, places)
    kernel = functools.partial(attend_kernel, block_len, ctx_size, head_dim)
    given = () if carry is None else carry
    mixed_shape = struct((rows, head_count * head_dim), bf16)
    return pl.pallas_call(
        drop_refs(kernel, 5, len(given)),
        out_shape=(struct(prev.shape, bf16), struct(prev.shape, bf16), mixed_shape),
        grid_spec=pltpu.PrefetchScalarGridSpec(
            num_scalar_prefetch=1,
            grid=(count,),
            in_specs=[narrow, whole, whole, wide] + [ANY] * len(given),
            out_specs=[wide, wide, mixed],
            scratch_shapes=[pltpu.VMEM((rows, seq_len), f32)],
        ),
        input_output_aliases={5 + i: i for i in range(len(given))},
        compiler_params=params(),
        cost_estimate=cost(
            8 * rows * seq_len * LANES * heads * count,
            6 * rows * seq_len * heads * count,
            rows * seq_len * heads * count,
        ),
        name="attend",
    )(info, *qkv, prev, *given)


def drop_refs(kernel, start, count):
    def run(*refs):
        kernel(*refs[:start], *refs[start + count :])

    return run if count else kernel


def attend_back(qkv, probs, grad_mixed, places, carry, block_len, ctx_size, head_dim):
    head_count, rows, seq_len = probs.shape
    heads, count = LANES // head_dim, len(places)
    wide, mixed, narrow, whole = pair_specs(rows, seq_len, heads, places)
    kernel = functools.partial(attend_back_kernel, block_len, ctx_size, head_dim)
    given = tuple(carry)
    return pl.pallas_call(
        drop_refs(kernel, 5, len(given)),
        out_shape=[struct(probs.shape, bf16)] + [struct(a.shape, bf16) for a in qkv],
        grid=(count,),
        in_specs=[narrow, whole, whole, wide, mixed] + [ANY] * len(given),
        out_specs=[wide, narrow, whole, whole],
        scratch_shapes=[pltpu.VMEM((seq_len, LANES), f32), pltpu.VMEM((seq_len, LANES), f32)],
        input_output_aliases={5 + i: i for i in range(len(given))},
        compiler_params=params(),
        cost_estimate=cost(
            16 * rows * seq_len * LANES * heads * count, 4 * rows * seq_len * heads * count
        ),
        name="attend_back",
    )(*qkv, probs, grad_mixed, *given)


def by_sides(ref, info, width):
    return jnp.concatenate(
        [ref[:, side_lanes(info, 0, width)], ref[:, side_lanes(info, 1, width)]], axis=1
    )


def project_kernel(info, own_tok, oth_tok, *refs):
    own, oth = [[(ref, 0) for ref in refs[i : i + 5]] for i in (0, 5)]
    cut = split_row(refs[0].shape[1])
    q_ref, k_ref, v_ref, w, table_ref, long_ref, table, sem = refs[10:]
    core, plane = info[0], info[1]
    block_len = k_ref.shape[2]
    rows, width = own_tok.shape
    half, shard = width // 2, width // 16
    cuts = [slice(0, half), slice(half, width)]
    copies = []

    def copy(source, dest):
        copies.append(pltpu.make_async_copy(source, dest, sem.at[len(copies)]))
        copies[-1].start()

    for source, where, _, _ in piece_parts(own, cut, plane, 3 * shard, 16):
        copy(source, table.at[:, where])
    for unit in range(3):
        for side, pieces in enumerate((own, oth)):
            for source, where, first, count in piece_parts(pieces, cut, plane, unit * shard, shard):
                copy(source, w.at[unit, :, where, pl.ds(first, count), cuts[side]])
    for item in copies:
        item.wait()
    long_span = long_ref.shape[1] // 16
    for rank in range(16):
        piece = table[rank // 4, rank % 4].astype(f32)
        table_ref[:, rank * shard : (rank + 1) * shard] = piece[:, :shard]
        long_ref[:, rank * long_span : (rank + 1) * long_span] = piece[:, :long_span]
    weights = [w[unit].reshape(width, width) for unit in range(3)]
    tokens = jnp.concatenate([own_tok[...], oth_tok[...]], axis=0)
    lanes = [side_lanes(info, side, half) for side in range(2)]
    query = mm(own_tok[...], weights[0])
    for side in range(2):
        q_ref[:, lanes[side]] = (query[:, cuts[side]] + table_ref[0:1, lanes[side]]).astype(bf16)
    for out, weight, row in ((k_ref, weights[1], None), (v_ref, weights[2], 1)):
        value = mm(tokens, weight)
        for side in range(2):
            piece = value[:, cuts[side]]
            if row is not None:
                piece = piece + table_ref[row : row + 1, lanes[side]]
            piece = piece.astype(bf16)
            for index in range(4):
                where = core if index < 2 else 1 - core
                out[index % 2, where, :, lanes[side]] = piece[index * block_len : (index + 1) * block_len]


def project(info, own_tok, oth_tok, own, oth, block_len, long_size):
    rows, width = own_tok.shape
    shard = width // 16
    q_shape = struct((rows, width), bf16)
    k_shape = struct((2, 2, block_len, width), bf16)
    shapes = [
        q_shape,
        k_shape,
        k_shape,
        struct((3, 4, 4, shard, width), bf16),
        struct((16, width), f32),
        struct((16, 16 * long_size), f32),
    ]
    q, k, v, w, table, long = pl.pallas_call(
        project_kernel,
        out_shape=shapes,
        grid_spec=pltpu.PrefetchScalarGridSpec(
            num_scalar_prefetch=1,
            grid=(1,),
            in_specs=[whole_block(own_tok)] * 2 + [ANY] * 10,
            out_specs=[whole_block(s) for s in shapes],
            scratch_shapes=[
                pltpu.VMEM((4, 4, 16, width // 2), bf16),
                pltpu.SemaphoreType.DMA((40,)),
            ],
        ),
        compiler_params=params(),
        cost_estimate=cost(10 * rows * width * width, 20 * rows * width + 12 * width * width),
        name="project",
    )(info, own_tok, oth_tok, *own, *oth)
    w = w.reshape(3, width, width)
    return q, k.reshape(2 * rows, width), v.reshape(2 * rows, width), w, table, long


def normalize(total):
    center = total - jnp.mean(total, axis=-1, keepdims=True)
    inverse = lax.rsqrt(jnp.mean(center * center, axis=-1, keepdims=True) + EPSILON)
    return center * inverse, inverse


def normalize_back(grad, normed, inverse):
    mean_grad = jnp.mean(grad, axis=-1, keepdims=True)
    mean_cross = jnp.mean(grad * normed, axis=-1, keepdims=True)
    return inverse * (grad - mean_grad - normed * mean_cross)


def gelu_parts(value):
    size = jnp.abs(value)
    near = 1.0 / (1.0 + (0.3275911 * 0.7071067811865476) * size)
    series = 0.5 * 1.061405429
    for factor in (-1.453152027, 1.421413741, -0.284496736, 0.254829592):
        series = series * near + 0.5 * factor
    bell = jnp.exp2((-0.5 * 1.4426950408889634) * (value * value))
    tail = series * near * bell
    active = jnp.maximum(value, 0.0) - size * tail
    below = jnp.where(value >= 0.0, 1.0 - tail, tail)
    return active, below + value * (bell * 0.3989422804014327)


def put_table(stage, start, sums, count, long_row=None):
    shard = sums.shape[1] // 16
    cols = stage.shape[4]
    low = sums[0:8, :]
    row = lax.broadcasted_iota(jnp.int32, (16, cols), 0)
    for rank in range(16):
        part = low[:, rank * shard : (rank + 1) * shard]
        part = jnp.pad(part, ((0, 8), (0, cols - shard)))
        table = jnp.where(row < count, part, 0.0)
        if long_row is not None:
            at = long_row + rank // 4
            span = sums.shape[1] // 4
            long = sums[at : at + 1, rank % 4 * span : (rank % 4 + 1) * span]
            table = jnp.where(row == count, jnp.pad(long, ((0, 0), (0, cols - span))), table)
        table = table.astype(bf16)
        for side in range(2):
            stage[side, rank // 4, rank % 4, start : start + 16, :] = table


def term_slots(outs, side):
    first, rest = outs[2 * side : 2 * side + 2]
    return [first, rest.at[0], rest.at[1], rest.at[2]]


def chunk_pieces(refs, rows_at, which):
    if which == "c":
        return [(refs[0], 0), (refs[1], 0), (refs[2], 0), (refs[3], 0), (refs[4], 0)]
    low = rows_at["rows_c"] - rows_at["cut_c"]
    return [(refs[5], 0), (refs[4], low), (refs[3], rows_at["cut_c"]), (refs[6], 0), (refs[7], 0)]


def feed_kernel(
    ctx_size, rows_at, info, mix, tok, teacher, table, long_table, *refs
):
    count_in = 12
    own, oth = refs[:count_in], refs[count_in : 2 * count_in]
    (
    out_ref, gs_ref, gm_ref, *terms, wc, wd, act, slope, value_ref, first, norm, inv, low, acc, go, stage_d, stage_c, sum_ref, sem,
    ) = refs[2 * count_in :]
    square_ref, *terms = terms
    terms_d, terms_c = terms[:4], terms[4:]
    core, plane = info[0], info[1]
    b_inner = long_table.at[pl.ds(rows_at["long"], 1)]
    units, rows_all, width = act.shape
    half = width // 2
    shard = width // 16
    block_len = rows_all // 2
    tile = 64
    tiles = [slice(start, start + tile) for start in range(0, rows_all, tile)]
    lanes = [side_lanes(info, side, half) for side in range(2)]
    cuts = [slice(0, half), slice(half, width)]
    count = [0]

    def start(source, dest):
        copy = pltpu.make_async_copy(source, dest, sem.at[count[0]])
        count[0] += 1
        copy.start()
        return copy

    def wait(copies):
        for copy in copies:
            copy.wait()

    def vector(index):
        row = rows_at[index]
        return table[row : row + 1, :]

    def unit_rows(side, unit):
        where = core if side == 0 else 1 - core
        return pl.ds(pl.multiple_of((where * units + unit) * half, LANES), half)

    def unit_parts(pieces, unit):
        split = units // 2
        if split <= unit < units:
            return piece_parts(
                chunk_pieces(pieces, rows_at, "d"), rows_at["cut_d"], plane, (unit - split) * shard, shard
            )
        at = split if unit == units else unit
        return piece_parts(chunk_pieces(pieces, rows_at, "c"), rows_at["cut_c"], plane, at * shard, shard)

    load_c = {}
    for unit in [units] + list(range(units)):
        load_c[unit] = [
            start(source, wc.at[unit, :, where, pl.ds(first_row, rows), cuts[side]])
            for side, pieces in enumerate((own, oth))
            for source, where, first_row, rows in unit_parts(pieces, unit)
        ]
    deep_d = rows_at["deep_d"]
    load_d = [
        start(source, wd.at[:, where, pl.ds(first_row, rows), cuts[side]])
        for side, pieces in enumerate((own, oth))
        for source, where, first_row, rows in piece_parts(
            chunk_pieces(pieces, rows_at, "d"), rows_at["cut_d"], plane, units // 2 * shard, deep_d
        )
    ]
    rest = pl.ds(deep_d, wd.shape[2] - deep_d)
    for side, pieces in enumerate((own, oth)):
        layers = pieces[8:12]
        load_d += [start(ref, wd.at[info[3] ^ i, :, rest, cuts[side]]) for i, ref in enumerate(layers)]

    def outer_unit(unit):
        ranks = half // wd.shape[2]
        blocks = []
        for side in range(2):
            where = core if side == 0 else 1 - core
            for index in range(ranks):
                rank = (where * units + unit) * ranks + index
                blocks.append(wd[rank // 4, rank % 4])
        return jnp.concatenate(blocks, axis=0)

    wait(load_c[units])
    value = mm(mix[...], wc[units].reshape(width, width))
    for side in range(2):
        acc[:, lanes[side]] = value[:, cuts[side]]
    for rows in tiles:
        normed, inverse = normalize(tok[rows, :].astype(f32) + (acc[rows, :] + vector("bo")))
        total = normed * vector("gain_one") + vector("shift_one")
        norm[rows, :] = normed
        inv[rows, :] = jnp.broadcast_to(inverse, (tile, LANES))
        first[rows, :] = total
        low[rows, :] = total.astype(bf16)

    for unit in range(units + 1):
        if unit < units:
            wait(load_c[unit])
        for part in range(2):
            block = slice(part * block_len, (part + 1) * block_len)
            if unit < units:
                value = mm(low[block, :], wc[unit].reshape(width, width))
                for side in range(2):
                    where = core if side == 0 else 1 - core
                    column = pl.ds(pl.multiple_of((where * units + unit) * half, LANES), half)
                    value_ref[unit % 2, block, cuts[side]] = value[:, cuts[side]] + b_inner[:, column]
            if unit > 0:
                for rows in [slice(at, at + 32) for at in range(block.start, block.stop, 32)]:
                    active, steep = gelu_parts(value_ref[(unit - 1) % 2, rows, :])
                    act[unit - 1, rows, :] = active.astype(bf16)
                    slope[unit - 1, rows, :] = steep.astype(bf16)
    value = None
    wait(load_d)
    for unit in range(units):
        term = mm(act[unit], outer_unit(unit))
        value = term if value is None else value + term
    for side in range(2):
        acc[:, lanes[side]] = value[:, cuts[side]]

    valid_total = jnp.sum(
        vector("count") * 32.0 + table[rows_at["count"] + 1 : rows_at["count"] + 2, :], axis=-1, keepdims=True
    )
    factor = rows_at["scale"] * shard / (valid_total * width)
    sums = [jnp.zeros((8, width), f32) for _ in range(4)]
    for rows in tiles:
        part, inside = divmod(rows.start, block_len)
        base = (core if part == 0 else 2 * ctx_size - 1 - core) * block_len + inside
        position = lax.broadcasted_iota(jnp.int32, (tile, 1), 0) + base
        valid = (position < info[2]).astype(f32)
        normed, inverse = normalize(first[rows, :] + (acc[rows, :] + vector("b_outer")))
        result = normed * vector("gain_two") + vector("shift_two")
        out_ref[rows, :] = result.astype(bf16)
        error = (result - teacher[rows, :].astype(f32)) * valid
        grad_result = error * factor
        grad_sum = normalize_back(grad_result * vector("gain_two"), normed, inverse)
        grad_low = grad_sum.astype(bf16)
        acc[rows, :] = grad_sum
        go[rows, :] = grad_low
        terms = (grad_result * normed, grad_result, grad_low.astype(f32), error * error)
        for index, term in enumerate(terms):
            sums[index] = sums[index] + jnp.sum(term.reshape(tile // 8, 8, width), axis=0)
    for index in range(4):
        sum_ref[index : index + 1, :] = jnp.sum(sums[index], axis=0, keepdims=True)
    loss_part = jnp.sum(sum_ref[3:4, :], axis=-1, keepdims=True) * shard / (valid_total * width)
    square_ref[...] = jnp.broadcast_to(loss_part, (8, LANES))

    grad = by_sides(go, info, half)

    def put_c(term, unit):
        term = term.astype(bf16)
        rows = slice(unit * shard, (unit + 1) * shard)
        for side in range(2):
            stage_c[side, :, :, rows, :] = term[:, cuts[side]].reshape(4, 4, shard, half)

    def send(stage, outs):
        return [
            start(stage.at[side, :, plane ^ offset], dest)
            for side in (1, 0)
            for offset, dest in zip((3, 1, 2, 0), term_slots(outs, side))
        ]

    for unit in range(units):
        term = mm_tn(act[unit], grad).astype(bf16)
        deep = stage_d.shape[3]
        for side in range(2):
            where = core if side == 0 else 1 - core
            for index in range(half // deep):
                rank = (where * units + unit) * (half // deep) + index
                rows = slice(side * half + index * deep, side * half + (index + 1) * deep)
                for col in range(2):
                    stage_d[col, rank // 4, rank % 4] = term[rows, cuts[col]]
    sent = send(stage_d, terms_d)
    for unit in range(units):
        grad_active = mm_nt(grad, outer_unit(unit))
        grad_inner = (grad_active * slope[unit].astype(f32)).astype(bf16)
        slope[unit] = grad_inner
        total = jnp.sum(grad_inner.astype(f32), axis=0, keepdims=True)
        for side in range(2):
            column = (core if side == 0 else 1 - core) * units + unit
            at = pl.ds(pl.multiple_of((column % 2) * half, LANES), half)
            sum_ref[pl.ds(8 + column // 2, 1), at] = total[:, cuts[side]]
        put_c(mm_tn(low[...], slope[unit]), unit)
        acc[...] += mm_nt(slope[unit], wc[unit].reshape(width, width))

    sums = [jnp.zeros((8, width), f32) for _ in range(3)]
    for rows in tiles:
        normed, grad_first = norm[rows, :], acc[rows, :]
        grad_sum = normalize_back(grad_first * vector("gain_one"), normed, inv[rows, 0:1])
        grad_low = grad_sum.astype(bf16)
        gs_ref[rows, :] = grad_sum
        go[rows, :] = grad_low
        terms = (grad_first * normed, grad_first, grad_low.astype(f32))
        for index, term in enumerate(terms):
            sums[index] = sums[index] + jnp.sum(term.reshape(tile // 8, 8, width), axis=0)
    for index in range(3):
        sum_ref[4 + index : 5 + index, :] = jnp.sum(sums[index], axis=0, keepdims=True)
    grad = by_sides(go, info, half)
    put_c(mm_tn(mix[...], grad), units)
    put_table(stage_c, (units + 1) * shard, sum_ref, 7, 8)
    sent += send(stage_c, terms_c)
    gm_ref[...] = mm_nt(grad, wc[units].reshape(width, width)).astype(bf16)
    wait(sent)


def feed(info, mix, tok, teacher, table, long_table, own, oth, rows_at, ctx_size):
    rows, width = tok.shape
    half, units = width // 2, long_table.shape[1] // width
    shapes = [
        struct((rows, width), bf16),
        struct((rows, width), f32),
        struct((rows, width), bf16),
        struct((8, LANES), f32),
    ]
    deep = units * width // 16
    terms = []
    for size in (deep, width // 16 * (units + 1) + 16):
        terms += [struct((4, size, half), bf16), struct((3, 4, size, half), bf16)] * 2
    blocks = (mix, tok, teacher, table, long_table)
    flops = 2 * rows * width * (6 * units + 3) * width
    return pl.pallas_call(
        functools.partial(feed_kernel, ctx_size, rows_at),
        out_shape=shapes + terms,
        grid_spec=pltpu.PrefetchScalarGridSpec(
            num_scalar_prefetch=1,
            grid=(1,),
            in_specs=[whole_block(a) for a in blocks] + [ANY] * 24,
            out_specs=[whole_block(s) for s in shapes] + [ANY] * 8,
            scratch_shapes=[
                pltpu.VMEM((units + 1, 4, 4, width // 16, width), bf16),
                pltpu.VMEM((4, 4, deep, width), bf16),
                pltpu.VMEM((units, rows, width), bf16),
                pltpu.VMEM((units, rows, width), bf16),
                pltpu.VMEM((2, rows, width), f32),
                pltpu.VMEM((rows, width), f32),
                pltpu.VMEM((rows, width), f32),
                pltpu.VMEM((rows, LANES), f32),
                pltpu.VMEM((rows, width), bf16),
                pltpu.VMEM((rows, width), f32),
                pltpu.VMEM((rows, width), bf16),
                pltpu.VMEM((2, 4, 4, deep, half), bf16),
                pltpu.VMEM((2, 4, 4, width // 16 * (units + 1) + 16, half), bf16),
                pltpu.VMEM((16, width), f32),
                pltpu.SemaphoreType.DMA((12 * units + 60,)),
            ],
        ),
        compiler_params=params(),
        cost_estimate=cost(flops, 30 * width * width, 2 * rows * width * units),
        name="feed",
    )(info, *blocks, *own, *oth)


def slot_rows(ref, core, lanes):
    return jnp.concatenate(
        [ref[part, where, :, lanes] for where in (core, 1 - core) for part in range(2)], axis=0
    )


def token_back_kernel(info, own_tok, oth_tok, gq, gk, gv, gs_in, w_in, own_ref, send_ref, *refs):
    outs, stage, sum_ref, gs_one, w, sem = refs[:4], refs[4], refs[5], refs[6], refs[7], refs[8]
    late = [
        pltpu.make_async_copy(gs_in, gs_one, sem.at[8]),
        pltpu.make_async_copy(w_in, w, sem.at[9]),
    ]
    for copy in late:
        copy.start()
    core, plane = info[0], info[1]
    width = own_tok.shape[1]
    half, shard = width // 2, width // 16
    tokens = jnp.concatenate([own_tok[...], oth_tok[...]], axis=0)

    def put(term, index):
        term = term.astype(bf16)
        rows = slice(index * shard, (index + 1) * shard)
        for side in range(2):
            cut = slice(side * half, (side + 1) * half)
            stage[side, :, :, rows, :] = term[:, cut].reshape(4, 4, shard, half)

    for index, grad in ((1, gk), (2, gv)):
        left = [slot_rows(grad, core, side_lanes(info, side, half)) for side in range(2)]
        put(mm_tn(tokens, jnp.concatenate(left, axis=1)), index)
    put(mm_tn(own_tok[...], by_sides(gq, info, half)), 0)
    sum_ref[0:1, :] = jnp.sum(gq[...].astype(f32), axis=0, keepdims=True)
    total = jnp.zeros((1, width), f32)
    for part in range(2):
        for where in range(2):
            total = total + jnp.sum(gv[part, where].astype(f32), axis=0, keepdims=True)
    sum_ref[1:2, :] = total
    put_table(stage, 3 * shard, sum_ref, 2)
    copies = []
    for side in (1, 0):
        for offset, dest in zip((3, 1, 2, 0), term_slots(outs, side)):
            copy = pltpu.make_async_copy(
                stage.at[side, :, plane ^ offset], dest, sem.at[len(copies)]
            )
            copy.start()
            copies.append(copy)
    rows = own_tok.shape[0]
    for copy in late:
        copy.wait()
    both = None
    for grad, weight in ((gk, w[1]), (gv, w[2])):
        left = [slot_rows(grad, core, side_lanes(info, side, half)) for side in range(2)]
        part = mm_nt(jnp.concatenate(left, axis=1), weight)
        both = part if both is None else both + part
    query = mm_nt(by_sides(gq, info, half), w[0])
    own_ref[...] = gs_one[...] + query + both[:rows]
    send_ref[...] = both[rows:].astype(bf16)
    for copy in copies:
        copy.wait()


def token_back(info, own_tok, oth_tok, gq, gk, gv, gs_one, w):
    rows, width = own_tok.shape
    deep, half = 3 * width // 16 + 16, width // 2
    args = (own_tok, oth_tok, gq, gk, gv, gs_one, w)
    shapes = [struct((rows, width), f32), struct((rows, width), bf16)]
    return pl.pallas_call(
        token_back_kernel,
        out_shape=shapes + [struct((4, deep, half), bf16), struct((3, 4, deep, half), bf16)] * 2,
        grid_spec=pltpu.PrefetchScalarGridSpec(
            num_scalar_prefetch=1,
            grid=(1,),
            in_specs=[whole_block(a) for a in args[:5]] + [ANY] * 2,
            out_specs=[whole_block(s) for s in shapes] + [ANY] * 4,
            scratch_shapes=[
                pltpu.VMEM((2, 4, 4, deep, half), bf16),
                pltpu.VMEM((8, width), f32),
                pltpu.VMEM(gs_one.shape, f32),
                pltpu.VMEM(w.shape, bf16),
                pltpu.SemaphoreType.DMA((10,)),
            ],
        ),
        compiler_params=params(),
        cost_estimate=cost(20 * rows * width * width, 40 * rows * width),
        name="token_back",
    )(info, *args)


def layout_positions(block_len, ctx_size, slot_index):
    within = jnp.arange(block_len, dtype=jnp.int32)
    front_pos = slot_index * block_len + within
    back_pos = (2 * ctx_size - 1 - slot_index) * block_len + within
    return (front_pos, back_pos)


def norm_forward(activation):
    center = activation - jnp.mean(activation, axis=-1, keepdims=True)
    inverse = lax.rsqrt(jnp.mean(center * center, axis=-1, keepdims=True) + EPSILON)
    return (center * inverse, inverse)


def norm_backward(grad_normed, normed, inverse):
    mean_grad = jnp.mean(grad_normed, axis=-1, keepdims=True)
    mean_cross = jnp.mean(grad_normed * normed, axis=-1, keepdims=True)
    return inverse * (grad_normed - mean_grad - normed * mean_cross)


def weight_grad(left, right):
    return lax.dot_general(
        left, right, (((0,), (0,)), ((), ())), preferred_element_type=jnp.float32
    )


def back_product(left, right):
    return lax.dot_general(
        left, right, (((1,), (1,)), ((), ())), preferred_element_type=jnp.float32
    )


def gelu_exact(inputs):
    return jax.nn.gelu(inputs, approximate=False)


def column_sum(matrix):
    return jnp.sum(matrix.astype(jnp.float32), axis=0)


def local_plain(
    tokens,
    prev_logits,
    teacher,
    lengths,
    w_query,
    w_key,
    w_value,
    w_output,
    w_inner,
    w_outer,
    bias_query,
    bias_value,
    bias_output,
    attn_gain,
    attn_shift,
    inner_bias,
    outer_bias,
    ffn_gain,
    ffn_shift,
):
    f32 = jnp.float32
    bf16 = jnp.bfloat16
    ctx_size = lax.axis_size("ctx")
    ctx_rank = lax.axis_index("ctx")
    dp_size = lax.axis_size("dp")
    groups = tokens.shape[0]
    block_len = tokens.shape[3]
    model_width = tokens.shape[4]
    head_count = prev_logits.shape[1]
    seq_len = prev_logits.shape[-1]
    head_dim = model_width // head_count
    local_rows = 2 * block_len
    total_rows = groups * local_rows
    score_scale = head_dim ** (-0.5)
    (
        query_matrix,
        key_matrix,
        value_matrix,
        output_matrix,
        query_add,
        value_add,
        output_add,
        first_gain,
        first_shift,
    ) = (
        lax.all_gather(w_query, "dp", axis=0, tiled=True),
        lax.all_gather(w_key, "dp", axis=0, tiled=True),
        lax.all_gather(w_value, "dp", axis=0, tiled=True),
        lax.all_gather(w_output, "dp", axis=0, tiled=True),
        lax.all_gather(bias_query, "dp", axis=0, tiled=True),
        lax.all_gather(bias_value, "dp", axis=0, tiled=True),
        lax.all_gather(bias_output, "dp", axis=0, tiled=True),
        lax.all_gather(attn_gain, "dp", axis=0, tiled=True),
        lax.all_gather(attn_shift, "dp", axis=0, tiled=True),
    )
    token_rows = tokens.reshape(total_rows, model_width)
    queries = (
        jnp.dot(token_rows, query_matrix, preferred_element_type=f32) + query_add.astype(f32)
    ).astype(bf16)
    key_rows = jnp.dot(token_rows, key_matrix, preferred_element_type=f32).astype(bf16)
    values = (
        jnp.dot(token_rows, value_matrix, preferred_element_type=f32) + value_add.astype(f32)
    ).astype(bf16)
    key_blocks, value_blocks = (
        lax.all_gather(
            key_rows.reshape(groups, 2, 1, block_len, model_width), "ctx", axis=2, tiled=True
        ),
        lax.all_gather(
            values.reshape(groups, 2, 1, block_len, model_width), "ctx", axis=2, tiled=True
        ),
    )
    inner_matrix, outer_matrix, inner_add, outer_add, second_gain, second_shift = (
        lax.all_gather(w_inner, "dp", axis=0, tiled=True),
        lax.all_gather(w_outer, "dp", axis=0, tiled=True),
        lax.all_gather(inner_bias, "dp", axis=0, tiled=True),
        lax.all_gather(outer_bias, "dp", axis=0, tiled=True),
        lax.all_gather(ffn_gain, "dp", axis=0, tiled=True),
        lax.all_gather(ffn_shift, "dp", axis=0, tiled=True),
    )
    front_pos, back_pos = layout_positions(block_len, ctx_size, ctx_rank)
    query_pos = jnp.stack([front_pos, back_pos]).reshape(local_rows)
    key_front, key_back = layout_positions(
        block_len, ctx_size, jnp.arange(ctx_size, dtype=jnp.int32)[:, None]
    )
    key_pos = jnp.stack([key_front, key_back]).reshape(seq_len)
    allowed = (key_pos[None, None, :] <= query_pos[None, :, None]) & (
        key_pos[None, None, :] < lengths[:, None, None]
    )
    valid_rows = (query_pos[None, :] < lengths[:, None]).astype(f32).reshape(total_rows)
    query_heads = queries.reshape(groups, local_rows, head_count, head_dim).transpose(2, 0, 1, 3)
    key_heads = key_blocks.reshape(groups, seq_len, head_count, head_dim).transpose(2, 0, 1, 3)
    value_heads = value_blocks.reshape(groups, seq_len, head_count, head_dim).transpose(2, 0, 1, 3)
    prev_rows = prev_logits.reshape(groups, head_count, local_rows, seq_len)

    def scores_of(head_id):
        raw_scores = (
            jnp.einsum(
                "grd,gkd->grk", query_heads[head_id], key_heads[head_id], preferred_element_type=f32
            )
            * score_scale
        )
        raw_scores = raw_scores + lax.dynamic_index_in_dim(
            prev_rows, head_id, 1, keepdims=False
        ).astype(f32)
        return (raw_scores, jnp.where(allowed, raw_scores, NEG_BIG))

    def attend(head_id):
        raw_scores, masked = scores_of(head_id)
        row_max = jnp.max(masked, axis=-1, keepdims=True)
        exponent = jnp.exp(masked - row_max)
        row_total = jnp.sum(exponent, axis=-1, keepdims=True)
        probability = (exponent / row_total).astype(bf16)
        mixed_part = jnp.einsum(
            "grk,gkd->grd", probability, value_heads[head_id], preferred_element_type=f32
        )
        return (mixed_part, row_max[..., 0] + jnp.log(row_total[..., 0]), raw_scores.astype(bf16))

    mixed_heads, log_totals, raw_heads = lax.map(attend, jnp.arange(head_count))
    raw_logits = jnp.moveaxis(raw_heads, 0, 1).reshape(prev_logits.shape)
    mixed_rows = mixed_heads.transpose(1, 2, 0, 3).reshape(total_rows, model_width).astype(bf16)
    attn_out = jnp.dot(mixed_rows, output_matrix, preferred_element_type=f32) + output_add.astype(
        f32
    )
    first_normed, first_inverse = norm_forward(token_rows.astype(f32) + attn_out)
    first = first_normed * first_gain.astype(f32) + first_shift.astype(f32)
    first_low = first.astype(bf16)
    inner_pre = jnp.dot(first_low, inner_matrix, preferred_element_type=f32) + inner_add.astype(f32)
    active, gelu_back = jax.vjp(gelu_exact, inner_pre)
    active_low = active.astype(bf16)
    outer_pre = jnp.dot(active_low, outer_matrix, preferred_element_type=f32) + outer_add.astype(
        f32
    )
    second_normed, second_inverse = norm_forward(first + outer_pre)
    result = second_normed * second_gain.astype(f32) + second_shift.astype(f32)
    errors = (result - teacher.reshape(total_rows, model_width).astype(f32)) * valid_rows[:, None]
    square_sum, valid_total = lax.psum(
        (jnp.sum(errors * errors), jnp.sum(valid_rows)), ("dp", "ctx")
    )
    loss_value = square_sum / (valid_total * model_width)
    loss_scale = dp_size * groups * seq_len * model_width / 2.0
    grad_result = errors * (loss_scale * 2.0 / (valid_total * model_width))
    grad_second_gain = jnp.sum(grad_result * second_normed, axis=0)
    grad_second_shift = jnp.sum(grad_result, axis=0)
    grad_sum_two = norm_backward(
        grad_result * second_gain.astype(f32), second_normed, second_inverse
    )
    grad_outer = grad_sum_two.astype(bf16)
    grad_outer_matrix = weight_grad(active_low, grad_outer)
    grad_outer_add = column_sum(grad_outer)
    grad_active = back_product(grad_outer, outer_matrix)
    grad_inner = gelu_back(grad_active)[0].astype(bf16)
    grad_inner_matrix = weight_grad(first_low, grad_inner)
    grad_inner_add = column_sum(grad_inner)
    grad_first = grad_sum_two + back_product(grad_inner, inner_matrix)
    grad_first_gain = jnp.sum(grad_first * first_normed, axis=0)
    grad_first_shift = jnp.sum(grad_first, axis=0)
    grad_sum_one = norm_backward(grad_first * first_gain.astype(f32), first_normed, first_inverse)
    grad_attn = grad_sum_one.astype(bf16)
    grad_output_matrix = weight_grad(mixed_rows, grad_attn)
    grad_output_add = column_sum(grad_attn)
    grad_mixed = back_product(grad_attn, output_matrix).astype(bf16)
    grad_mixed_heads = grad_mixed.reshape(groups, local_rows, head_count, head_dim).transpose(
        2, 0, 1, 3
    )

    def attend_back(head_id):
        _, masked = scores_of(head_id)
        probability = jnp.exp(masked - log_totals[head_id][..., None])
        grad_part = grad_mixed_heads[head_id]
        grad_value_part = jnp.einsum(
            "grk,grd->gkd", probability.astype(bf16), grad_part, preferred_element_type=f32
        )
        grad_probs = jnp.einsum(
            "grd,gkd->grk", grad_part, value_heads[head_id], preferred_element_type=f32
        )
        row_dot = jnp.sum(probability * grad_probs, axis=-1, keepdims=True)
        grad_scores = (probability * (grad_probs - row_dot)).astype(bf16)
        grad_query_part = (
            jnp.einsum("grk,gkd->grd", grad_scores, key_heads[head_id], preferred_element_type=f32)
            * score_scale
        )
        grad_key_part = (
            jnp.einsum(
                "grk,grd->gkd", grad_scores, query_heads[head_id], preferred_element_type=f32
            )
            * score_scale
        )
        return (grad_scores, grad_query_part, grad_key_part, grad_value_part)

    grad_score_heads, grad_query_heads, grad_key_heads, grad_value_heads = lax.map(
        attend_back, jnp.arange(head_count)
    )
    grad_logits = jnp.moveaxis(grad_score_heads, 0, 1).reshape(prev_logits.shape)
    grad_queries = (
        grad_query_heads.transpose(1, 2, 0, 3).reshape(total_rows, model_width).astype(bf16)
    )
    key_terms = grad_key_heads.transpose(1, 2, 0, 3).reshape(
        groups, 2, ctx_size, block_len, model_width
    )
    value_terms = grad_value_heads.transpose(1, 2, 0, 3).reshape(
        groups, 2, ctx_size, block_len, model_width
    )
    key_sums, value_sums = (
        lax.psum_scatter(
            key_terms.astype(jnp.bfloat16), "ctx", scatter_dimension=2, tiled=True
        ).astype(jnp.float32),
        lax.psum_scatter(
            value_terms.astype(jnp.bfloat16), "ctx", scatter_dimension=2, tiled=True
        ).astype(jnp.float32),
    )
    grad_keys = key_sums.reshape(total_rows, model_width).astype(bf16)
    grad_values = value_sums.reshape(total_rows, model_width).astype(bf16)
    grad_query_matrix = weight_grad(token_rows, grad_queries)
    grad_key_matrix = weight_grad(token_rows, grad_keys)
    grad_value_matrix = weight_grad(token_rows, grad_values)
    grad_query_add = column_sum(grad_queries)
    grad_value_add = column_sum(grad_values)
    grad_token_rows = (
        grad_sum_one
        + back_product(grad_queries, query_matrix)
        + back_product(grad_keys, key_matrix)
        + back_product(grad_values, value_matrix)
    )
    matrix_grads = (
        grad_query_matrix,
        grad_key_matrix,
        grad_value_matrix,
        grad_output_matrix,
        grad_inner_matrix,
        grad_outer_matrix,
    )
    vector_grads = (
        grad_query_add,
        grad_value_add,
        grad_output_add,
        grad_first_gain,
        grad_first_shift,
        grad_inner_add,
        grad_outer_add,
        grad_second_gain,
        grad_second_shift,
    )
    summed = (
        lax.psum_scatter(
            matrix_grads[0].astype(jnp.bfloat16), "dp", scatter_dimension=0, tiled=True
        ).astype(jnp.float32),
        lax.psum_scatter(
            matrix_grads[1].astype(jnp.bfloat16), "dp", scatter_dimension=0, tiled=True
        ).astype(jnp.float32),
        lax.psum_scatter(
            matrix_grads[2].astype(jnp.bfloat16), "dp", scatter_dimension=0, tiled=True
        ).astype(jnp.float32),
        lax.psum_scatter(
            matrix_grads[3].astype(jnp.bfloat16), "dp", scatter_dimension=0, tiled=True
        ).astype(jnp.float32),
        lax.psum_scatter(
            matrix_grads[4].astype(jnp.bfloat16), "dp", scatter_dimension=0, tiled=True
        ).astype(jnp.float32),
        lax.psum_scatter(
            matrix_grads[5].astype(jnp.bfloat16), "dp", scatter_dimension=0, tiled=True
        ).astype(jnp.float32),
        lax.psum_scatter(
            vector_grads[0].astype(jnp.bfloat16), "dp", scatter_dimension=0, tiled=True
        ).astype(jnp.float32),
        lax.psum_scatter(
            vector_grads[1].astype(jnp.bfloat16), "dp", scatter_dimension=0, tiled=True
        ).astype(jnp.float32),
        lax.psum_scatter(
            vector_grads[2].astype(jnp.bfloat16), "dp", scatter_dimension=0, tiled=True
        ).astype(jnp.float32),
        lax.psum_scatter(
            vector_grads[3].astype(jnp.bfloat16), "dp", scatter_dimension=0, tiled=True
        ).astype(jnp.float32),
        lax.psum_scatter(
            vector_grads[4].astype(jnp.bfloat16), "dp", scatter_dimension=0, tiled=True
        ).astype(jnp.float32),
        lax.psum_scatter(
            vector_grads[5].astype(jnp.bfloat16), "dp", scatter_dimension=0, tiled=True
        ).astype(jnp.float32),
        lax.psum_scatter(
            vector_grads[6].astype(jnp.bfloat16), "dp", scatter_dimension=0, tiled=True
        ).astype(jnp.float32),
        lax.psum_scatter(
            vector_grads[7].astype(jnp.bfloat16), "dp", scatter_dimension=0, tiled=True
        ).astype(jnp.float32),
        lax.psum_scatter(
            vector_grads[8].astype(jnp.bfloat16), "dp", scatter_dimension=0, tiled=True
        ).astype(jnp.float32),
    )
    reduced = (
        lax.psum(summed[0].astype(jnp.bfloat16), "ctx").astype(jnp.float32),
        lax.psum(summed[1].astype(jnp.bfloat16), "ctx").astype(jnp.float32),
        lax.psum(summed[2].astype(jnp.bfloat16), "ctx").astype(jnp.float32),
        lax.psum(summed[3].astype(jnp.bfloat16), "ctx").astype(jnp.float32),
        lax.psum(summed[4].astype(jnp.bfloat16), "ctx").astype(jnp.float32),
        lax.psum(summed[5].astype(jnp.bfloat16), "ctx").astype(jnp.float32),
        lax.psum(summed[6].astype(jnp.bfloat16), "ctx").astype(jnp.float32),
        lax.psum(summed[7].astype(jnp.bfloat16), "ctx").astype(jnp.float32),
        lax.psum(summed[8].astype(jnp.bfloat16), "ctx").astype(jnp.float32),
        lax.psum(summed[9].astype(jnp.bfloat16), "ctx").astype(jnp.float32),
        lax.psum(summed[10].astype(jnp.bfloat16), "ctx").astype(jnp.float32),
        lax.psum(summed[11].astype(jnp.bfloat16), "ctx").astype(jnp.float32),
        lax.psum(summed[12].astype(jnp.bfloat16), "ctx").astype(jnp.float32),
        lax.psum(summed[13].astype(jnp.bfloat16), "ctx").astype(jnp.float32),
        lax.psum(summed[14].astype(jnp.bfloat16), "ctx").astype(jnp.float32),
    )
    return (
        result.astype(bf16).reshape(tokens.shape),
        raw_logits,
        loss_value,
        grad_token_rows.astype(bf16).reshape(tokens.shape),
        grad_logits,
        reduced[0],
        reduced[1],
        reduced[2],
        reduced[3],
        reduced[4],
        reduced[5],
        reduced[6],
        reduced[7],
        reduced[8],
        reduced[9],
        reduced[10],
        reduced[11],
        reduced[12],
        reduced[13],
        reduced[14],
    )


def local_fast(tokens, prev_logits, teacher, lengths, *parameters):
    weights, vectors = parameters[:6], parameters[6:]
    w_outer = weights[5]
    ctx_size = lax.axis_size("ctx")
    core = lax.axis_index("ctx")
    dp_size = lax.axis_size("dp")
    dp_rank = lax.axis_index("dp")
    block_len, width = tokens.shape[3], tokens.shape[4]
    head_count, seq_len = prev_logits.shape[1], prev_logits.shape[-1]
    head_dim = width // head_count
    rows = 2 * block_len
    shard = weights[0].shape[0]
    half = width // 2
    units = weights[4].shape[1] // width
    info = jnp.stack([core, dp_rank % 4, lengths[0], dp_rank // 4]).astype(jnp.int32)
    token_rows = tokens.reshape(rows, width)
    teacher_rows = teacher.reshape(rows, width)
    prev_rows = prev_logits.reshape(head_count, rows, seq_len)
    sizes = (block_len, ctx_size, head_dim)
    pairs = [(i, i) for i in range(head_count * head_dim // LANES)]
    (long_at,) = [i for i, v in enumerate(vectors) if v.shape[0] != shard]
    names = ("bq", "bv", "bo", "gain_one", "shift_one", "long", "b_outer", "gain_two", "shift_two", "count")
    rows_at = {name: i for i, name in enumerate(names)}
    rows_at["scale"] = float(dp_size * seq_len * width)

    chunk_a, chunk_c, chunk_d, chunk_e = pack(info, weights, vectors)
    cut_c, cut_d = split_row(chunk_c.shape[0]), split_row(chunk_d.shape[0])
    rows_at.update(
        rows_c=chunk_c.shape[0], cut_c=cut_c, cut_d=cut_d, deep_d=w_outer.shape[0] - chunk_e.shape[0]
    )
    cross = lambda piece: flip(piece, "ctx", 1)
    parts_a = z_triple(chunk_a)
    parts_e = [chunk_e] + [flip(chunk_e, "dp", step) for step in (1, 2, 3)]
    parts_a, parts_e, token_rows, chunk_c, chunk_d = together(
        parts_a, parts_e, token_rows, chunk_c, chunk_d
    )
    column_a = in_order(dp_rank // 4, parts_a)
    sides_a = side_columns(column_a)
    next_c = flip(chunk_c, "dp", 4)
    other_rows = cross(token_rows)
    pair_c = z_pair(chunk_c, next_c)
    over_c = flip(pair_c, "dp", 8)
    sides_a, other_rows, over_c, chunk_d = together(sides_a, other_rows, over_c, chunk_d)
    corner_a = corner_column(sides_a)
    own_a = [column_a, *sides_a]
    oth_a = [cross(piece) for piece in own_a]
    next_d = flip(chunk_d, "dp", 4)
    corner_a, oth_a, next_d, parts_e = together(corner_a, oth_a, next_d, parts_e)
    oth_a = [*oth_a, *[cross(piece) for piece in corner_a]]
    own_a = [*own_a, *corner_a]
    column_c = z_column(pair_c, over_c)
    sides_c = side_columns(column_c)
    pair_d = z_pair(chunk_d, next_d)
    over_d = flip(pair_d, "dp", 8)
    plane_e = in_order(dp_rank % 4, parts_e)
    next_e = flip(plane_e, "dp", 4)
    oth_e = [cross(plane_e)]
    queries, keys, values, w_attn, table, long_table = project(
        info, token_rows, other_rows, own_a, oth_a, block_len, vectors[long_at].shape[0]
    )
    queries, sides_c, pair_d, over_d, plane_e, next_e, oth_e = together(
        queries, sides_c, pair_d, over_d, plane_e, next_e, oth_e
    )
    column_d = z_column(pair_d, over_d)
    far_up = flip(jnp.concatenate([sides_c[0][:, :cut_c], column_d], axis=1), "dp", 2)
    near_low = flip(jnp.concatenate([sides_c[1][:, cut_c:], column_d], axis=1), "dp", 1)
    over_e = [flip(plane_e, "dp", 8)]
    oth_c = [cross(column_c), cross(sides_c[0])]
    qkv = (queries, keys, values)
    carry = attend(info, qkv, prev_rows, pairs[:4], None, *sizes)
    carry, oth_c, column_d, far_up, near_low, over_e = together(
        carry, oth_c, column_d, far_up, near_low, over_e
    )
    near_d = near_low[:, chunk_c.shape[0] - cut_c :]
    far_d = far_up[:, cut_c:]
    corner_d = [flip(near_d[:, :cut_d], "dp", 2), flip(far_d[:, cut_d:], "dp", 1)]
    over_e.append(flip(next_e, "dp", 8))
    late = [far_up, near_low]
    oth_late = [cross(piece) for piece in late]
    logits, probs, mixed = attend(info, qkv, prev_rows, pairs[4:], carry, *sizes)
    mixed, oth_c, oth_late, corner_d, over_e, column_d, next_e, sides_c = together(
        mixed, oth_c, oth_late, corner_d, over_e, column_d, next_e, sides_c
    )
    own_c = [column_c, *sides_c, far_up, near_low]
    own_d = [column_d, *corner_d, plane_e, next_e, *over_e]
    oth_c += [cross(sides_c[1]), *oth_late]
    oth_d = [cross(piece) for piece in own_d[:3]] + oth_e + [cross(piece) for piece in own_d[4:]]
    result, grad_sum_one, grad_mixed, square, *terms = feed(
        info, mixed, token_rows, teacher_rows, table, long_table,
        [*own_c, *own_d], [*oth_c, *oth_d], rows_at, ctx_size,
    )

    back = lambda some, carry: attend_back(qkv, probs, grad_mixed, some, carry, *sizes)
    kept_d, sent_d, kept_c, sent_c = terms[:2], terms[2:4], terms[4:6], terms[6:8]
    came_d = [cross(sent_d[0])]
    square = square + cross(square)
    sent_d, sent_c, square, came_d, grad_mixed = together(sent_d, sent_c, square, came_d, grad_mixed)
    corner_d = scatter_corner(kept_d[0], came_d[0])
    came_d.append(cross(sent_d[1]))
    came_c = [cross(part) for part in sent_c]
    grads = back(pairs[:2], [])
    grads, corner_d, came_d, came_c, square = together(grads, corner_d, came_d, came_c, square)
    sides_d = send_sides(scatter_sides(kept_d[1], came_d[1], corner_d))
    corner_c = scatter_corner(kept_c[0], came_c[0])
    square = square + flip(square, "dp", 8)
    grad_logits, gq, gk, gv = back(pairs[2:], grads)
    gk, gv = [g.reshape(2, 2, block_len, width) for g in (gk, gv)]
    gq, sides_d, corner_c, square = together(gq, sides_d, corner_c, square)
    sides_c = scatter_sides(kept_c[1], came_c[1], corner_c)
    half_d = scatter_half(kept_d[1], came_d[1], sides_d)
    sides_c, half_d, gq = together(sides_c, half_d, gq)
    sides_c, half_d = send_sides(sides_c), (half_d[0], flip(half_d[1], "dp", 8))
    own_terms, sent_terms, *terms_a = token_back(
        info, token_rows, other_rows, gq, gk, gv, grad_sum_one, w_attn
    )
    own_terms, sent_terms, terms_a, sides_c, half_d = together(
        own_terms, sent_terms, terms_a, sides_c, half_d
    )
    kept_a, sent_a = terms_a[:2], terms_a[2:4]
    came_a = [cross(part) for part in sent_a]
    half_c = scatter_half(kept_c[1], came_c[1], sides_c)
    half_c = (half_c[0], flip(half_c[1], "dp", 8))
    rank_d = scatter_rank(*half_d)
    came_a, rank_d, sent_terms = together(came_a, rank_d, sent_terms)
    corner_a = scatter_corner(kept_a[0], came_a[0])
    total_d = scatter_total(rank_d[0], [rank_d[1]])
    grad_tokens = (own_terms + cross(sent_terms).astype(f32)).astype(bf16)
    corner_a, total_d, grad_tokens = together(corner_a, total_d, grad_tokens)
    sides_a = send_sides(scatter_sides(kept_a[1], came_a[1], corner_a))
    rank_c = scatter_rank(*half_c)
    sides_a, rank_c, square = together(sides_a, rank_c, square)
    triple_a = scatter_triple(kept_a[1], came_a[1], sides_a)
    total_c = scatter_total(rank_c[0], [rank_c[1]])
    square = square + flip(square, "dp", 1)
    square = square + flip(square, "dp", 2)
    triple_a, square, total_c = together(triple_a, square, total_c)
    square = square + flip(square, "dp", 4)
    total_a = scatter_total(*triple_a)
    pair_a, pair_c, pair_d = by_halves(*total_a), by_halves(*total_c), by_halves(*total_d)
    (joined_a,) = together(jnp.concatenate(pair_a, axis=1))

    def unit(parts, index):
        return [part[index * shard : (index + 1) * shard] for part in parts]

    grad_w_inner = jnp.concatenate(
        [unit(pair_c[side : side + 1], i)[0] for side in range(2) for i in range(units)], axis=1
    )
    sums_c, sums_a = total_c[0][(units + 1) * shard :].astype(f32), total_a[0][3 * shard :].astype(f32)
    order = (6, 4, 5, None, 2, 0, 1)
    vector_totals = [sums_a[0, :shard], sums_a[1, :shard]]
    vector_totals += [
        sums_c[7, : vectors[long_at].shape[0]] if i is None else sums_c[i, :shard] for i in order
    ]
    return (
        result.reshape(tokens.shape),
        logits.reshape(prev_logits.shape),
        square[0, 0],
        grad_tokens.reshape(tokens.shape),
        grad_logits.reshape(prev_logits.shape),
        *[joined_a[i * shard : (i + 1) * shard] for i in range(3)],
        jnp.concatenate(unit(pair_c, units), axis=1),
        grad_w_inner,
        jnp.concatenate(pair_d, axis=1),
        *vector_totals,
    )


def local(tokens, prev_logits, teacher, lengths, *parameters):
    width, shard = tokens.shape[-1], parameters[0].shape[0]
    fits = (
        lax.axis_size("dp") == 16
        and lax.axis_size("ctx") == 2
        and tokens.shape[0] == 1
        and shard % 16 == 0
        and width % 256 == 0
    )
    chosen = local_fast if fits else local_plain
    return chosen(tokens, prev_logits, teacher, lengths, *parameters)


def solution(mesh):
    rows = P("dp", None, "ctx", None, None)
    scores = P("dp", None, None, "ctx", None, None)
    matrix, vector = P("dp", None), P("dp")
    return jax.shard_map(
        local,
        mesh=mesh,
        in_specs=(rows, scores, rows, vector) + (matrix,) * 6 + (vector,) * 9,
        out_specs=(rows, scores, P(), rows, scores) + (matrix,) * 6 + (vector,) * 9,
        check_vma=False,
    )
```
